512 devices in a mesh: spot: 128 (over y_lo, z, x, core), var: 4 (over y_hi).
Axes of the slice: x: 4, y: 8 (y_hi: 4, y_lo: 2; y = y_hi * 2 + y_lo), z: 8, core: 2. Of those that a mesh axis runs over, the one named last changes fastest.
Arguments:
- option_value: float32 [256, 64, 1024], P('spot', None, 'var'), may hold values from -6 to 6
- spot_nodes: int32 [256], replicated, may hold values from 0 to 1023, as said below
- var_nodes: int32 [1024], replicated, may hold values from 0 to 4095, as said below
- rate_nodes: int32 [64], replicated, may hold values from 0 to 255, as said below
Outputs:
- advanced: float32 [256, 64, 1024], P('spot', None, 'var')
The draws below stay inside these ranges and needn't reach their ends.
Inputs may be any that keep to these rules, and one draw needn't show every extreme that they name: `spot_nodes`: strictly increasing, consecutive entries differ by 1 to 7, the first is 0 and the last 1023. `var_nodes`: strictly increasing, consecutive entries differ by 1 to 7, the first is 0 and the last 4095. `rate_nodes`: strictly increasing, consecutive entries differ by 1 to 7, the first is 0 and the last 255.
All inputs are finite; a program needn't handle non-finite values.
Results may differ from the reference program's by a relative error of at most 0.00045.
Values sent between devices are 32-bit elements; how exact they have to be, the bound alone decides.
A program may use at most 64 MiB of HBM per device.

```python
import jax
import jax.numpy as jnp
from jax import lax

NR = 64
NS = 256
NV = 1024


def node_draw(key, length):
    jitter = jax.random.randint(key, (length,), 0, 4)
    position = lax.broadcasted_iota(jnp.int32, (length,), 0)
    jitter = jnp.where(position == 0, 0, jnp.where(position == length - 1, 3, jitter))
    return (4 * position + jitter).astype(jnp.int32)


def draw_spot_nodes(key, part):
    return node_draw(jax.random.fold_in(key, 11), NS)


def draw_var_nodes(key, part):
    return node_draw(jax.random.fold_in(key, 23), NV)


def draw_rate_nodes(key, part):
    return node_draw(jax.random.fold_in(key, 37), NR)


def draw_option_value(key, part):
    own_key = jax.random.fold_in(key, 51)
    return jnp.clip(jax.random.normal(own_key, (NS, NR, NV), jnp.float32), -6.0, 6.0)


def setup_inputs(seed: int = 0) -> dict:
    seeds = jax.random.split(jax.random.key(seed), 5)
    option_value = draw_option_value(jax.random.fold_in(seeds[4], 71), 0)
    spot_nodes = draw_spot_nodes(jax.random.fold_in(seeds[4], 71), 0)
    var_nodes = draw_var_nodes(jax.random.fold_in(seeds[4], 71), 0)
    rate_nodes = draw_rate_nodes(jax.random.fold_in(seeds[4], 71), 0)
    return {"option_value": option_value, "spot_nodes": spot_nodes, "var_nodes": var_nodes, "rate_nodes": rate_nodes}


time_step = 0.01
solve_scale = 0.5 * time_step
half_step = 0.5 * time_step
spot_low = 0.5
spot_high = 2.5
var_low = 0.02
var_high = 1.0
rate_low = -0.1
rate_high = 0.2
dividend_yield = 0.02
reversion_var = 2.0
long_var = 0.04
vol_var = 0.6
reversion_rate = 0.1
long_rate = 0.05
vol_rate = 0.1
coupling_sv = -0.7 * vol_var
coupling_sr = 0.2 * vol_rate
coupling_vr = 0.1 * vol_var * vol_rate

def coordinates(node_list, low_end, high_end):
    length = node_list.shape[0]
    extended = jnp.concatenate([jnp.full((1,), -1, jnp.int32), node_list.astype(jnp.int32), jnp.full((1,), 4 * length, jnp.int32)])
    return low_end + (high_end - low_end) * extended.astype(jnp.float32) / (4 * length - 1)

def stencil_weights(coords):
    behind = coords[1:-1] - coords[:-2]
    ahead = coords[2:] - coords[1:-1]
    spread = behind + ahead
    first_diff = (-ahead / (behind * spread), (ahead - behind) / (behind * ahead), behind / (ahead * spread))
    second_diff = (2.0 / (behind * spread), -2.0 / (behind * ahead), 2.0 / (ahead * spread))
    return (first_diff, second_diff)

def geometry(coords, position, dim_count, offset, length):
    first_diff, second_diff = stencil_weights(coords)
    vectors = (coords[1:-1],) + first_diff + second_diff
    target = [1] * dim_count
    target[position] = length
    pieces = [lax.dynamic_slice_in_dim(vector, offset, length).reshape(target) for vector in vectors]
    return (pieces[0], tuple(pieces[1:4]), tuple(pieces[4:7]))

def spot_terms(spot_x, var_x, rate_x):
    return (0.5 * spot_x * spot_x * var_x, (rate_x - dividend_yield) * spot_x)

def var_terms(var_x):
    return (0.5 * vol_var * vol_var * var_x, reversion_var * (long_var - var_x))

def rate_terms(rate_x):
    return (0.5 * vol_rate * vol_rate, reversion_rate * (long_rate - rate_x))

def line_coefficients(diffusion, advection, reaction, first_diff, second_diff):
    behind = diffusion * second_diff[0] + advection * first_diff[0]
    centre = diffusion * second_diff[1] + advection * first_diff[1] - reaction
    ahead = diffusion * second_diff[2] + advection * first_diff[2]
    return (behind, centre, ahead)

def explicit_terms(padded, spot_geo, var_geo, rate_geo, mixing_only):
    spot_x, spot_first, spot_second = spot_geo
    var_x, var_first, var_second = var_geo
    rate_x, rate_first, rate_second = rate_geo
    spot_rows = padded.shape[0] - 2
    planes = padded.shape[1] - 2
    var_cols = padded.shape[2] - 2
    middle = padded[1:-1, 1:-1, 1:-1]
    cross_sv = 0.0
    cross_sr = 0.0
    cross_vr = 0.0
    for outer_step in range(3):
        for inner_step in range(3):
            cross_sv = cross_sv + spot_first[outer_step] * var_first[inner_step] * padded[outer_step:outer_step + spot_rows, 1:-1, inner_step:inner_step + var_cols]
            cross_sr = cross_sr + spot_first[outer_step] * rate_first[inner_step] * padded[outer_step:outer_step + spot_rows, inner_step:inner_step + planes, 1:-1]
            cross_vr = cross_vr + var_first[outer_step] * rate_first[inner_step] * padded[1:-1, inner_step:inner_step + planes, outer_step:outer_step + var_cols]
    root_var = jnp.sqrt(var_x)
    mixing = coupling_sv * spot_x * var_x * cross_sv + coupling_sr * spot_x * root_var * cross_sr + coupling_vr * root_var * cross_vr
    if mixing_only:
        return mixing
    reaction = rate_x / 3.0
    diffusion, advection = spot_terms(spot_x, var_x, rate_x)
    behind, centre, ahead = line_coefficients(diffusion, advection, reaction, spot_first, spot_second)
    along_spot = behind * padded[:-2, 1:-1, 1:-1] + centre * middle + ahead * padded[2:, 1:-1, 1:-1]
    diffusion, advection = var_terms(var_x)
    behind, centre, ahead = line_coefficients(diffusion, advection, reaction, var_first, var_second)
    along_var = behind * padded[1:-1, 1:-1, :-2] + centre * middle + ahead * padded[1:-1, 1:-1, 2:]
    diffusion, advection = rate_terms(rate_x)
    behind, centre, ahead = line_coefficients(diffusion, advection, reaction, rate_first, rate_second)
    along_rate = behind * padded[1:-1, :-2, 1:-1] + centre * middle + ahead * padded[1:-1, 2:, 1:-1]
    return mixing + along_spot + along_var + along_rate

def reduce_solve(lower_band, main_band, upper_band, right_side, dimension):
    length = right_side.shape[dimension]
    if length == 1:
        return right_side / main_band
    if length % 2 == 1:
        blank_row = jnp.zeros_like(lax.slice_in_dim(right_side, 0, 1, axis=dimension))
        grown_solution = reduce_solve(jnp.concatenate([lower_band, blank_row], axis=dimension), jnp.concatenate([main_band, blank_row + 1.0], axis=dimension), jnp.concatenate([upper_band, blank_row], axis=dimension), jnp.concatenate([right_side, blank_row], axis=dimension), dimension)
        return lax.slice_in_dim(grown_solution, 0, length, axis=dimension)

    def even_rows(source):
        return lax.slice_in_dim(source, 0, length, 2, dimension)

    def odd_rows(source):
        return lax.slice_in_dim(source, 1, length, 2, dimension)

    def onward(source, filler):
        remainder = lax.slice_in_dim(source, 1, source.shape[dimension], axis=dimension)
        return jnp.concatenate([remainder, jnp.zeros_like(lax.slice_in_dim(source, 0, 1, axis=dimension)) + filler], axis=dimension)

    def backward(source):
        remainder = lax.slice_in_dim(source, 0, source.shape[dimension] - 1, axis=dimension)
        return jnp.concatenate([jnp.zeros_like(lax.slice_in_dim(source, 0, 1, axis=dimension)), remainder], axis=dimension)
    lower_even, main_even, upper_even, right_even = [even_rows(source) for source in (lower_band, main_band, upper_band, right_side)]
    lower_odd, main_odd, upper_odd, right_odd = [odd_rows(source) for source in (lower_band, main_band, upper_band, right_side)]
    lower_next = onward(lower_even, 0.0)
    main_next = onward(main_even, 1.0)
    upper_next = onward(upper_even, 0.0)
    right_next = onward(right_even, 0.0)
    ratio_back = -lower_odd / main_even
    ratio_ahead = -upper_odd / main_next
    solved_odd = reduce_solve(ratio_back * lower_even, main_odd + ratio_back * upper_even + ratio_ahead * lower_next, ratio_ahead * upper_next, right_odd + ratio_back * right_even + ratio_ahead * right_next, dimension)
    solved_even = (right_even - lower_even * backward(solved_odd) - upper_even * solved_odd) / main_even
    joined = jnp.stack([solved_even, solved_odd], axis=dimension + 1)
    return joined.reshape(right_side.shape)

def implicit(system, right_side, dimension):
    behind, centre, ahead = system
    lower_band = jnp.broadcast_to(-solve_scale * behind, right_side.shape)
    main_band = jnp.broadcast_to(1.0 - solve_scale * centre, right_side.shape)
    upper_band = jnp.broadcast_to(-solve_scale * ahead, right_side.shape)
    return reduce_solve(lower_band, main_band, upper_band, right_side, dimension)

def reference(option_value, spot_nodes, var_nodes, rate_nodes):
    spot_coords = coordinates(spot_nodes, spot_low, spot_high)
    var_coords = coordinates(var_nodes, var_low, var_high)
    rate_coords = coordinates(rate_nodes, rate_low, rate_high)
    spot_geo = geometry(spot_coords, 0, 3, 0, spot_nodes.shape[0])
    var_geo = geometry(var_coords, 2, 3, 0, var_nodes.shape[0])
    rate_geo = geometry(rate_coords, 1, 3, 0, rate_nodes.shape[0])
    reaction = rate_geo[0] / 3.0
    diffusion, advection = spot_terms(spot_geo[0], var_geo[0], rate_geo[0])
    spot_system = line_coefficients(diffusion, advection, reaction, spot_geo[1], spot_geo[2])
    diffusion, advection = var_terms(var_geo[0])
    var_system = line_coefficients(diffusion, advection, reaction, var_geo[1], var_geo[2])
    diffusion, advection = rate_terms(rate_geo[0])
    rate_system = line_coefficients(diffusion, advection, reaction, rate_geo[1], rate_geo[2])
    z_zero = time_step * explicit_terms(jnp.pad(option_value, 1), spot_geo, var_geo, rate_geo, False)
    z_one = implicit(spot_system, z_zero, 0)
    z_two = implicit(var_system, z_one, 2)
    z_three = implicit(rate_system, z_two, 1)
    w_zero = z_zero + half_step * explicit_terms(jnp.pad(z_three, 1), spot_geo, var_geo, rate_geo, True)
    w_one = implicit(spot_system, w_zero, 0)
    w_two = implicit(var_system, w_one, 2)
    w_three = implicit(rate_system, w_two, 1)
    return option_value + w_three
```

```python
import jax
import jax.numpy as jnp
from jax import lax
from jax.sharding import PartitionSpec as P

time_step = 0.01
solve_scale = 0.5 * time_step
half_step = 0.5 * time_step
spot_low = 0.5
spot_high = 2.5
var_low = 0.02
var_high = 1.0
rate_low = -0.1
rate_high = 0.2
dividend_yield = 0.02
reversion_var = 2.0
long_var = 0.04
vol_var = 0.6
reversion_rate = 0.1
long_rate = 0.05
vol_rate = 0.1
coupling_sv = -0.7 * vol_var
coupling_sr = 0.2 * vol_rate
coupling_vr = 0.1 * vol_var * vol_rate


def padded_2(array, sides, width):
    for axis, dim in sides:
        devices, length = (lax.axis_size(axis), array.shape[dim])
        up = [(i, (i + 1) % devices) for i in range(devices - 1)]
        down = [(j, i) for i, j in up]
        last = lax.slice_in_dim(array, length - width, length, axis=dim)
        initial = lax.slice_in_dim(array, 0, width, axis=dim)
        before = lax.ppermute(last, axis, up)
        after = lax.ppermute(initial, axis, down)
        array = jnp.concatenate([before, array, after], axis=dim)
    return array


def coordinates(node_list, low_end, high_end):
    length = node_list.shape[0]
    extended = jnp.concatenate(
        [jnp.full((1,), -1, jnp.int32), node_list, jnp.full((1,), 4 * length, jnp.int32)]
    )
    return low_end + (high_end - low_end) * extended.astype(jnp.float32) / (4 * length - 1)


def stencil_weights(coords):
    behind = coords[1:-1] - coords[:-2]
    ahead = coords[2:] - coords[1:-1]
    spread = behind + ahead
    first_diff = (
        -ahead / (behind * spread),
        (ahead - behind) / (behind * ahead),
        behind / (ahead * spread),
    )
    second_diff = (2.0 / (behind * spread), -2.0 / (behind * ahead), 2.0 / (ahead * spread))
    return (first_diff, second_diff)


def geometry(coords, position, dim_count, offset, length):
    first_diff, second_diff = stencil_weights(coords)
    vectors = (coords[1:-1],) + first_diff + second_diff
    target = [1] * dim_count
    target[position] = length
    pieces = [
        lax.dynamic_slice_in_dim(vector, offset, length).reshape(target) for vector in vectors
    ]
    return (pieces[0], tuple(pieces[1:4]), tuple(pieces[4:7]))


def spot_terms(spot_x, var_x, rate_x):
    return (0.5 * spot_x * spot_x * var_x, (rate_x - dividend_yield) * spot_x)


def var_terms(var_x):
    return (0.5 * vol_var * vol_var * var_x, reversion_var * (long_var - var_x))


def rate_terms(rate_x):
    return (0.5 * vol_rate * vol_rate, reversion_rate * (long_rate - rate_x))


def line_coefficients(diffusion, advection, reaction, first_diff, second_diff):
    behind = diffusion * second_diff[0] + advection * first_diff[0]
    centre = diffusion * second_diff[1] + advection * first_diff[1] - reaction
    ahead = diffusion * second_diff[2] + advection * first_diff[2]
    return (behind, centre, ahead)


def explicit_terms(padded, spot_geo, var_geo, rate_geo, mixing_only):
    spot_x, spot_first, spot_second = spot_geo
    var_x, var_first, var_second = var_geo
    rate_x, rate_first, rate_second = rate_geo
    spot_rows = padded.shape[0] - 2
    planes = padded.shape[1] - 2
    var_cols = padded.shape[2] - 2
    middle = padded[1:-1, 1:-1, 1:-1]
    cross_sv = 0.0
    cross_sr = 0.0
    cross_vr = 0.0
    for outer_step in range(3):
        for inner_step in range(3):
            cross_sv = (
                cross_sv
                + spot_first[outer_step]
                * var_first[inner_step]
                * padded[
                    outer_step : outer_step + spot_rows, 1:-1, inner_step : inner_step + var_cols
                ]
            )
            cross_sr = (
                cross_sr
                + spot_first[outer_step]
                * rate_first[inner_step]
                * padded[
                    outer_step : outer_step + spot_rows, inner_step : inner_step + planes, 1:-1
                ]
            )
            cross_vr = (
                cross_vr
                + var_first[outer_step]
                * rate_first[inner_step]
                * padded[1:-1, inner_step : inner_step + planes, outer_step : outer_step + var_cols]
            )
    root_var = jnp.sqrt(var_x)
    mixing = (
        coupling_sv * spot_x * var_x * cross_sv
        + coupling_sr * spot_x * root_var * cross_sr
        + coupling_vr * root_var * cross_vr
    )
    if mixing_only:
        return mixing
    reaction = rate_x / 3.0
    diffusion, advection = spot_terms(spot_x, var_x, rate_x)
    behind, centre, ahead = line_coefficients(
        diffusion, advection, reaction, spot_first, spot_second
    )
    along_spot = behind * padded[:-2, 1:-1, 1:-1] + centre * middle + ahead * padded[2:, 1:-1, 1:-1]
    diffusion, advection = var_terms(var_x)
    behind, centre, ahead = line_coefficients(diffusion, advection, reaction, var_first, var_second)
    along_var = behind * padded[1:-1, 1:-1, :-2] + centre * middle + ahead * padded[1:-1, 1:-1, 2:]
    diffusion, advection = rate_terms(rate_x)
    behind, centre, ahead = line_coefficients(
        diffusion, advection, reaction, rate_first, rate_second
    )
    along_rate = behind * padded[1:-1, :-2, 1:-1] + centre * middle + ahead * padded[1:-1, 2:, 1:-1]
    return mixing + along_spot + along_var + along_rate


def reduce_solve(lower_band, main_band, upper_band, right_side, dimension):
    length = right_side.shape[dimension]
    if length == 1:
        return right_side / main_band

    def even_rows(source):
        return lax.slice_in_dim(source, 0, length, 2, dimension)

    def odd_rows(source):
        return lax.slice_in_dim(source, 1, length, 2, dimension)

    def onward(source, filler):
        remainder = lax.slice_in_dim(source, 1, source.shape[dimension], axis=dimension)
        return jnp.concatenate(
            [remainder, jnp.zeros_like(lax.slice_in_dim(source, 0, 1, axis=dimension)) + filler],
            axis=dimension,
        )

    lower_even, main_even, upper_even, right_even = [
        even_rows(source) for source in (lower_band, main_band, upper_band, right_side)
    ]
    lower_odd, main_odd, upper_odd, right_odd = [
        odd_rows(source) for source in (lower_band, main_band, upper_band, right_side)
    ]
    lower_next = onward(lower_even, 0.0)
    main_next = onward(main_even, 1.0)
    upper_next = onward(upper_even, 0.0)
    right_next = onward(right_even, 0.0)
    ratio_back = -lower_odd / main_even
    ratio_ahead = -upper_odd / main_next
    solved_odd = reduce_solve(
        ratio_back * lower_even,
        main_odd + ratio_back * upper_even + ratio_ahead * lower_next,
        ratio_ahead * upper_next,
        right_odd + ratio_back * right_even + ratio_ahead * right_next,
        dimension,
    )
    remainder = lax.slice_in_dim(solved_odd, 0, solved_odd.shape[dimension] - 1, axis=dimension)
    solved_even = (
        right_even
        - lower_even
        * jnp.concatenate(
            [jnp.zeros_like(lax.slice_in_dim(solved_odd, 0, 1, axis=dimension)), remainder],
            axis=dimension,
        )
        - upper_even * solved_odd
    ) / main_even
    joined = jnp.stack([solved_even, solved_odd], axis=dimension + 1)
    return joined.reshape(right_side.shape)


def implicit(system, right_side, dimension):
    behind, centre, ahead = system
    lower_band = jnp.broadcast_to(-solve_scale * behind, right_side.shape)
    main_band = jnp.broadcast_to(1.0 - solve_scale * centre, right_side.shape)
    upper_band = jnp.broadcast_to(-solve_scale * ahead, right_side.shape)
    return reduce_solve(lower_band, main_band, upper_band, right_side, dimension)


def shards(option_value, spot_nodes, var_nodes, rate_nodes):
    spot_rows, planes, var_cols = option_value.shape
    line_count = planes * var_cols
    spot_place = lax.axis_index("spot")
    var_place = lax.axis_index("var")
    spot_coords = coordinates(spot_nodes, spot_low, spot_high)
    var_coords = coordinates(var_nodes, var_low, var_high)
    rate_coords = coordinates(rate_nodes, rate_low, rate_high)
    spot_geo = geometry(spot_coords, 0, 3, spot_place * spot_rows, spot_rows)
    var_geo = geometry(var_coords, 2, 3, var_place * var_cols, var_cols)
    rate_geo = geometry(rate_coords, 1, 3, 0, planes)
    spot_whole = geometry(spot_coords, 0, 2, 0, spot_nodes.shape[0])
    var_whole = geometry(var_coords, 1, 2, 0, var_nodes.shape[0])
    rate_plain = rate_geo[0].reshape(planes)
    var_plain = var_geo[0].reshape(var_cols)

    def edge_terms(values, mixing_only):
        padded = padded_2(values, (("spot", 0), ("var", 2)), 1)
        padded = jnp.pad(padded, ((0, 0), (1, 1), (0, 0)))
        return explicit_terms(padded, spot_geo, var_geo, rate_geo, mixing_only)

    def spot_solve(values):
        gathered = lax.all_to_all(
            values.reshape(spot_rows, line_count), "spot", split_axis=1, concat_axis=0, tiled=True
        )
        per_device = gathered.shape[1]
        first_line = spot_place * per_device
        rate_flat = jnp.broadcast_to(rate_plain.reshape(planes, 1), (planes, var_cols)).reshape(
            line_count
        )
        var_flat = jnp.broadcast_to(var_plain.reshape(1, var_cols), (planes, var_cols)).reshape(
            line_count
        )
        rate_line = lax.dynamic_slice_in_dim(rate_flat, first_line, per_device).reshape(
            1, per_device
        )
        var_line = lax.dynamic_slice_in_dim(var_flat, first_line, per_device).reshape(1, per_device)
        diffusion, advection = spot_terms(spot_whole[0], var_line, rate_line)
        system = line_coefficients(
            diffusion, advection, rate_line / 3.0, spot_whole[1], spot_whole[2]
        )
        solved = implicit(system, gathered, 0)
        return lax.all_to_all(solved, "spot", split_axis=0, concat_axis=1, tiled=True).reshape(
            spot_rows, planes, var_cols
        )

    var_count = var_nodes.shape[0]
    blocks = var_count // var_cols
    var_vec = var_coords[1:-1]
    var_first, var_second = stencil_weights(var_coords)
    var_diffusion, var_advection = var_terms(var_vec)
    var_behind = var_diffusion * var_second[0] + var_advection * var_first[0]
    var_middle = var_diffusion * var_second[1] + var_advection * var_first[1]
    var_ahead = var_diffusion * var_second[2] + var_advection * var_first[2]
    reaction_plain = rate_plain / 3.0
    var_lower = (-solve_scale * var_behind).reshape(blocks, var_cols)
    var_upper = (-solve_scale * var_ahead).reshape(blocks, var_cols)
    var_main = (
        1.0 - solve_scale * (var_middle.reshape(var_count, 1) - reaction_plain.reshape(1, planes))
    ).reshape(blocks, var_cols, planes)

    lower_cols = jnp.broadcast_to(
        var_lower.T.reshape(var_cols, blocks, 1, 1), (var_cols, blocks, 2, planes)
    )
    upper_cols = jnp.broadcast_to(
        var_upper.T.reshape(var_cols, blocks, 1, 1), (var_cols, blocks, 2, planes)
    )
    main_cols = jnp.broadcast_to(
        var_main.transpose(1, 0, 2).reshape(var_cols, blocks, 1, planes),
        (var_cols, blocks, 2, planes),
    )
    position = lax.broadcasted_iota(jnp.int32, (var_cols, blocks, 2, planes), 0)
    kind = lax.broadcasted_iota(jnp.int32, (var_cols, blocks, 2, planes), 2)
    coupling = jnp.where(
        (kind == 0) & (position == 0),
        var_lower[:, 0].reshape(1, blocks, 1, 1),
        jnp.where(
            (kind == 1) & (position == var_cols - 1),
            var_upper[:, var_cols - 1].reshape(1, blocks, 1, 1),
            0.0,
        ),
    )
    columns = reduce_solve(lower_cols, main_cols, upper_cols, coupling, 0)
    g_first, g_last = columns[0, :, 0, :], columns[var_cols - 1, :, 0, :]
    h_first, h_last = columns[0, :, 1, :], columns[var_cols - 1, :, 1, :]
    g_own = lax.dynamic_index_in_dim(columns[:, :, 0, :], var_place, 1, keepdims=False)
    h_own = lax.dynamic_index_in_dim(columns[:, :, 1, :], var_place, 1, keepdims=False)
    lower_own = lax.dynamic_index_in_dim(var_lower, var_place, 0, keepdims=False)
    upper_own = lax.dynamic_index_in_dim(var_upper, var_place, 0, keepdims=False)
    main_own = lax.dynamic_index_in_dim(var_main, var_place, 0, keepdims=False)

    def interface_solve(y_first, y_last):
        size = 2 * (blocks - 1)
        matrix = [[None] * size for _ in range(size)]
        rhs = [None] * size
        for b in range(blocks - 1):
            matrix[2 * b][2 * b] = 1.0
            if b >= 1:
                matrix[2 * b][2 * b - 2] = g_last[b]
            matrix[2 * b][2 * b + 1] = h_last[b]
            rhs[2 * b] = y_last[b]
            matrix[2 * b + 1][2 * b + 1] = 1.0
            matrix[2 * b + 1][2 * b] = g_first[b + 1]
            if b + 2 <= blocks - 1:
                matrix[2 * b + 1][2 * b + 3] = h_first[b + 1]
            rhs[2 * b + 1] = y_first[b + 1]
        for k in range(size):
            for i in range(k + 1, size):
                if matrix[i][k] is None:
                    continue
                factor = matrix[i][k] / matrix[k][k]
                for c in range(k + 1, size):
                    if matrix[k][c] is None:
                        continue
                    update = factor * matrix[k][c]
                    matrix[i][c] = -update if matrix[i][c] is None else matrix[i][c] - update
                rhs[i] = rhs[i] - factor * rhs[k]
                matrix[i][k] = None
        solved = [None] * size
        for k in reversed(range(size)):
            total = rhs[k]
            for c in range(k + 1, size):
                if matrix[k][c] is not None:
                    total = total - matrix[k][c] * solved[c]
            solved[k] = total / matrix[k][k]
        zero = jnp.zeros_like(y_first[0])
        left = jnp.stack([zero] + [solved[2 * b] for b in range(blocks - 1)])
        right = jnp.stack([solved[2 * b + 1] for b in range(blocks - 1)] + [zero])
        return (
            lax.dynamic_index_in_dim(left, var_place, 0, keepdims=False),
            lax.dynamic_index_in_dim(right, var_place, 0, keepdims=False),
        )

    def var_solve(values):
        lines = values.transpose(2, 0, 1)
        shape = lines.shape
        local = reduce_solve(
            jnp.broadcast_to(lower_own.reshape(var_cols, 1, 1), shape),
            jnp.broadcast_to(main_own.reshape(var_cols, 1, planes), shape),
            jnp.broadcast_to(upper_own.reshape(var_cols, 1, 1), shape),
            lines,
            0,
        )
        ends = lax.all_gather(jnp.stack([local[0], local[var_cols - 1]]), "var")
        left, right = interface_solve(ends[:, 0], ends[:, 1])
        solved = (
            local
            - left.reshape(1, spot_rows, planes) * g_own.reshape(var_cols, 1, planes)
            - right.reshape(1, spot_rows, planes) * h_own.reshape(var_cols, 1, planes)
        )
        return solved.transpose(1, 2, 0)

    def rate_solve(values):
        diffusion, advection = rate_terms(rate_geo[0])
        system = line_coefficients(
            diffusion, advection, rate_geo[0] / 3.0, rate_geo[1], rate_geo[2]
        )
        return implicit(system, values, 1)

    z_zero = time_step * edge_terms(option_value, False)
    z_one = spot_solve(z_zero)
    z_two = var_solve(z_one)
    z_three = rate_solve(z_two)
    w_zero = z_zero + half_step * edge_terms(z_three, True)
    w_one = spot_solve(w_zero)
    w_two = var_solve(w_one)
    w_three = rate_solve(w_two)
    return option_value + w_three


def solution(mesh):
    in_specs = (P("spot", None, "var"), P(), P(), P())
    out_specs = P("spot", None, "var")
    return jax.shard_map(shards, mesh=mesh, in_specs=in_specs, out_specs=out_specs, check_vma=False)
```

```python
import jax
import jax.numpy as jnp
from jax import lax
from jax.sharding import PartitionSpec as P

time_step = 0.01
solve_scale = 0.5 * time_step
half_step = 0.5 * time_step
spot_low = 0.5
spot_high = 2.5
var_low = 0.02
var_high = 1.0
rate_low = -0.1
rate_high = 0.2
dividend_yield = 0.02
reversion_var = 2.0
long_var = 0.04
vol_var = 0.6
reversion_rate = 0.1
long_rate = 0.05
vol_rate = 0.1
coupling_sv = -0.7 * vol_var
coupling_sr = 0.2 * vol_rate
coupling_vr = 0.1 * vol_var * vol_rate


def padded_2(array, sides, width):
    for axis, dim in sides:
        devices, length = (lax.axis_size(axis), array.shape[dim])
        up = [(i, (i + 1) % devices) for i in range(devices - 1)]
        down = [(j, i) for i, j in up]
        last = lax.slice_in_dim(array, length - width, length, axis=dim)
        initial = lax.slice_in_dim(array, 0, width, axis=dim)
        before = lax.ppermute(last, axis, up)
        after = lax.ppermute(initial, axis, down)
        array = jnp.concatenate([before, array, after], axis=dim)
    return array


def coordinates(node_list, low_end, high_end):
    length = node_list.shape[0]
    extended = jnp.concatenate(
        [jnp.full((1,), -1, jnp.int32), node_list, jnp.full((1,), 4 * length, jnp.int32)]
    )
    return low_end + (high_end - low_end) * extended.astype(jnp.float32) / (4 * length - 1)


def stencil_weights(coords):
    behind = coords[1:-1] - coords[:-2]
    ahead = coords[2:] - coords[1:-1]
    spread = behind + ahead
    first_diff = (
        -ahead / (behind * spread),
        (ahead - behind) / (behind * ahead),
        behind / (ahead * spread),
    )
    second_diff = (2.0 / (behind * spread), -2.0 / (behind * ahead), 2.0 / (ahead * spread))
    return (first_diff, second_diff)


def geometry(coords, position, dim_count, offset, length):
    first_diff, second_diff = stencil_weights(coords)
    vectors = (coords[1:-1],) + first_diff + second_diff
    target = [1] * dim_count
    target[position] = length
    pieces = [
        lax.dynamic_slice_in_dim(vector, offset, length).reshape(target) for vector in vectors
    ]
    return (pieces[0], tuple(pieces[1:4]), tuple(pieces[4:7]))


def spot_terms(spot_x, var_x, rate_x):
    return (0.5 * spot_x * spot_x * var_x, (rate_x - dividend_yield) * spot_x)


def var_terms(var_x):
    return (0.5 * vol_var * vol_var * var_x, reversion_var * (long_var - var_x))


def rate_terms(rate_x):
    return (0.5 * vol_rate * vol_rate, reversion_rate * (long_rate - rate_x))


def line_coefficients(diffusion, advection, reaction, first_diff, second_diff):
    behind = diffusion * second_diff[0] + advection * first_diff[0]
    centre = diffusion * second_diff[1] + advection * first_diff[1] - reaction
    ahead = diffusion * second_diff[2] + advection * first_diff[2]
    return (behind, centre, ahead)


def explicit_terms(padded, spot_geo, var_geo, rate_geo, mixing_only):
    spot_x, spot_first, spot_second = spot_geo
    var_x, var_first, var_second = var_geo
    rate_x, rate_first, rate_second = rate_geo
    spot_rows = padded.shape[0] - 2
    planes = padded.shape[1] - 2
    var_cols = padded.shape[2] - 2
    middle = padded[1:-1, 1:-1, 1:-1]
    cross_sv = 0.0
    cross_sr = 0.0
    cross_vr = 0.0
    for outer_step in range(3):
        for inner_step in range(3):
            cross_sv = (
                cross_sv
                + spot_first[outer_step]
                * var_first[inner_step]
                * padded[
                    outer_step : outer_step + spot_rows, 1:-1, inner_step : inner_step + var_cols
                ]
            )
            cross_sr = (
                cross_sr
                + spot_first[outer_step]
                * rate_first[inner_step]
                * padded[
                    outer_step : outer_step + spot_rows, inner_step : inner_step + planes, 1:-1
                ]
            )
            cross_vr = (
                cross_vr
                + var_first[outer_step]
                * rate_first[inner_step]
                * padded[1:-1, inner_step : inner_step + planes, outer_step : outer_step + var_cols]
            )
    root_var = jnp.sqrt(var_x)
    mixing = (
        coupling_sv * spot_x * var_x * cross_sv
        + coupling_sr * spot_x * root_var * cross_sr
        + coupling_vr * root_var * cross_vr
    )
    if mixing_only:
        return mixing
    reaction = rate_x / 3.0
    diffusion, advection = spot_terms(spot_x, var_x, rate_x)
    behind, centre, ahead = line_coefficients(
        diffusion, advection, reaction, spot_first, spot_second
    )
    along_spot = behind * padded[:-2, 1:-1, 1:-1] + centre * middle + ahead * padded[2:, 1:-1, 1:-1]
    diffusion, advection = var_terms(var_x)
    behind, centre, ahead = line_coefficients(diffusion, advection, reaction, var_first, var_second)
    along_var = behind * padded[1:-1, 1:-1, :-2] + centre * middle + ahead * padded[1:-1, 1:-1, 2:]
    diffusion, advection = rate_terms(rate_x)
    behind, centre, ahead = line_coefficients(
        diffusion, advection, reaction, rate_first, rate_second
    )
    along_rate = behind * padded[1:-1, :-2, 1:-1] + centre * middle + ahead * padded[1:-1, 2:, 1:-1]
    return mixing + along_spot + along_var + along_rate


def reduce_solve(lower_band, main_band, upper_band, right_side, dimension):
    length = right_side.shape[dimension]
    if length == 1:
        return right_side / main_band

    def even_rows(source):
        return lax.slice_in_dim(source, 0, length, 2, dimension)

    def odd_rows(source):
        return lax.slice_in_dim(source, 1, length, 2, dimension)

    def onward(source, filler):
        remainder = lax.slice_in_dim(source, 1, source.shape[dimension], axis=dimension)
        return jnp.concatenate(
            [remainder, jnp.zeros_like(lax.slice_in_dim(source, 0, 1, axis=dimension)) + filler],
            axis=dimension,
        )

    lower_even, main_even, upper_even, right_even = [
        even_rows(source) for source in (lower_band, main_band, upper_band, right_side)
    ]
    lower_odd, main_odd, upper_odd, right_odd = [
        odd_rows(source) for source in (lower_band, main_band, upper_band, right_side)
    ]
    lower_next = onward(lower_even, 0.0)
    main_next = onward(main_even, 1.0)
    upper_next = onward(upper_even, 0.0)
    right_next = onward(right_even, 0.0)
    ratio_back = -lower_odd / main_even
    ratio_ahead = -upper_odd / main_next
    solved_odd = reduce_solve(
        ratio_back * lower_even,
        main_odd + ratio_back * upper_even + ratio_ahead * lower_next,
        ratio_ahead * upper_next,
        right_odd + ratio_back * right_even + ratio_ahead * right_next,
        dimension,
    )
    remainder = lax.slice_in_dim(solved_odd, 0, solved_odd.shape[dimension] - 1, axis=dimension)
    solved_even = (
        right_even
        - lower_even
        * jnp.concatenate(
            [jnp.zeros_like(lax.slice_in_dim(solved_odd, 0, 1, axis=dimension)), remainder],
            axis=dimension,
        )
        - upper_even * solved_odd
    ) / main_even
    joined = jnp.stack([solved_even, solved_odd], axis=dimension + 1)
    return joined.reshape(right_side.shape)


def implicit(system, right_side, dimension):
    behind, centre, ahead = system
    lower_band = jnp.broadcast_to(-solve_scale * behind, right_side.shape)
    main_band = jnp.broadcast_to(1.0 - solve_scale * centre, right_side.shape)
    upper_band = jnp.broadcast_to(-solve_scale * ahead, right_side.shape)
    return reduce_solve(lower_band, main_band, upper_band, right_side, dimension)


def shards(option_value, spot_nodes, var_nodes, rate_nodes):
    spot_rows, planes, var_cols = option_value.shape
    line_count = planes * var_cols
    spot_place = lax.axis_index("spot")
    var_place = lax.axis_index("var")
    spot_coords = coordinates(spot_nodes, spot_low, spot_high)
    var_coords = coordinates(var_nodes, var_low, var_high)
    rate_coords = coordinates(rate_nodes, rate_low, rate_high)
    spot_geo = geometry(spot_coords, 0, 3, spot_place * spot_rows, spot_rows)
    var_geo = geometry(var_coords, 2, 3, var_place * var_cols, var_cols)
    rate_geo = geometry(rate_coords, 1, 3, 0, planes)
    spot_whole = geometry(spot_coords, 0, 2, 0, spot_nodes.shape[0])
    var_whole = geometry(var_coords, 1, 2, 0, var_nodes.shape[0])
    rate_plain = rate_geo[0].reshape(planes)
    var_plain = var_geo[0].reshape(var_cols)

    def edge_terms(values, mixing_only):
        padded = padded_2(values, (("spot", 0), ("var", 2)), 1)
        padded = jnp.pad(padded, ((0, 0), (1, 1), (0, 0)))
        return explicit_terms(padded, spot_geo, var_geo, rate_geo, mixing_only)

    def spot_solve(values):
        gathered = lax.all_to_all(
            values.reshape(spot_rows, line_count), "spot", split_axis=1, concat_axis=0, tiled=True
        )
        per_device = gathered.shape[1]
        first_line = spot_place * per_device
        rate_flat = jnp.broadcast_to(rate_plain.reshape(planes, 1), (planes, var_cols)).reshape(
            line_count
        )
        var_flat = jnp.broadcast_to(var_plain.reshape(1, var_cols), (planes, var_cols)).reshape(
            line_count
        )
        rate_line = lax.dynamic_slice_in_dim(rate_flat, first_line, per_device).reshape(
            1, per_device
        )
        var_line = lax.dynamic_slice_in_dim(var_flat, first_line, per_device).reshape(1, per_device)
        diffusion, advection = spot_terms(spot_whole[0], var_line, rate_line)
        system = line_coefficients(
            diffusion, advection, rate_line / 3.0, spot_whole[1], spot_whole[2]
        )
        solved = implicit(system, gathered, 0)
        return lax.all_to_all(solved, "spot", split_axis=0, concat_axis=1, tiled=True).reshape(
            spot_rows, planes, var_cols
        )

    var_count = var_nodes.shape[0]
    blocks = var_count // var_cols
    var_vec = var_coords[1:-1]
    var_first, var_second = stencil_weights(var_coords)
    var_diffusion, var_advection = var_terms(var_vec)
    var_behind = var_diffusion * var_second[0] + var_advection * var_first[0]
    var_middle = var_diffusion * var_second[1] + var_advection * var_first[1]
    var_ahead = var_diffusion * var_second[2] + var_advection * var_first[2]
    reaction_plain = rate_plain / 3.0
    var_lower = (-solve_scale * var_behind).reshape(blocks, var_cols)
    var_upper = (-solve_scale * var_ahead).reshape(blocks, var_cols)
    var_main = (
        1.0 - solve_scale * (var_middle.reshape(var_count, 1) - reaction_plain.reshape(1, planes))
    ).reshape(blocks, var_cols, planes)

    column_shape = (var_cols, blocks, 2, planes)
    lower_cols = jnp.broadcast_to(var_lower.T.reshape(var_cols, blocks, 1, 1), column_shape)
    upper_cols = jnp.broadcast_to(var_upper.T.reshape(var_cols, blocks, 1, 1), column_shape)
    main_cols = jnp.broadcast_to(
        var_main.transpose(1, 0, 2).reshape(var_cols, blocks, 1, planes), column_shape
    )
    position = lax.broadcasted_iota(jnp.int32, column_shape, 0)
    kind = lax.broadcasted_iota(jnp.int32, column_shape, 2)
    coupling = jnp.where(
        (kind == 0) & (position == 0),
        var_lower[:, 0].reshape(1, blocks, 1, 1),
        jnp.where(
            (kind == 1) & (position == var_cols - 1),
            var_upper[:, var_cols - 1].reshape(1, blocks, 1, 1),
            0.0,
        ),
    )
    flat = (var_cols, blocks * 2 * planes)
    columns = reduce_solve(
        lower_cols.reshape(flat),
        main_cols.reshape(flat),
        upper_cols.reshape(flat),
        coupling.reshape(flat),
        0,
    ).reshape(column_shape)
    g_first, g_last = columns[0, :, 0, :], columns[var_cols - 1, :, 0, :]
    h_first, h_last = columns[0, :, 1, :], columns[var_cols - 1, :, 1, :]
    g_own = lax.dynamic_index_in_dim(columns[:, :, 0, :], var_place, 1, keepdims=False)
    h_own = lax.dynamic_index_in_dim(columns[:, :, 1, :], var_place, 1, keepdims=False)
    lower_own = lax.dynamic_index_in_dim(var_lower, var_place, 0, keepdims=False)
    upper_own = lax.dynamic_index_in_dim(var_upper, var_place, 0, keepdims=False)
    main_own = lax.dynamic_index_in_dim(var_main, var_place, 0, keepdims=False)

    def interface_solve(y_first, y_last):
        size = 2 * (blocks - 1)
        matrix = [[None] * size for _ in range(size)]
        rhs = [None] * size
        for b in range(blocks - 1):
            matrix[2 * b][2 * b] = 1.0
            if b >= 1:
                matrix[2 * b][2 * b - 2] = g_last[b]
            matrix[2 * b][2 * b + 1] = h_last[b]
            rhs[2 * b] = y_last[b]
            matrix[2 * b + 1][2 * b + 1] = 1.0
            matrix[2 * b + 1][2 * b] = g_first[b + 1]
            if b + 2 <= blocks - 1:
                matrix[2 * b + 1][2 * b + 3] = h_first[b + 1]
            rhs[2 * b + 1] = y_first[b + 1]
        for k in range(size):
            for i in range(k + 1, size):
                if matrix[i][k] is None:
                    continue
                factor = matrix[i][k] / matrix[k][k]
                for c in range(k + 1, size):
                    if matrix[k][c] is None:
                        continue
                    update = factor * matrix[k][c]
                    matrix[i][c] = -update if matrix[i][c] is None else matrix[i][c] - update
                rhs[i] = rhs[i] - factor * rhs[k]
                matrix[i][k] = None
        solved = [None] * size
        for k in reversed(range(size)):
            total = rhs[k]
            for c in range(k + 1, size):
                if matrix[k][c] is not None:
                    total = total - matrix[k][c] * solved[c]
            solved[k] = total / matrix[k][k]
        zero = jnp.zeros_like(y_first[0])
        left = jnp.stack([zero] + [solved[2 * b] for b in range(blocks - 1)])
        right = jnp.stack([solved[2 * b + 1] for b in range(blocks - 1)] + [zero])
        return (
            lax.dynamic_index_in_dim(left, var_place, 0, keepdims=False),
            lax.dynamic_index_in_dim(right, var_place, 0, keepdims=False),
        )

    def gather_var(ends):
        parts = [ends]
        for shift in range(1, blocks):
            pairs = [(i, (i + shift) % blocks) for i in range(blocks)]
            parts.append(lax.ppermute(ends, "var", pairs))
        stacked = jnp.stack(parts)
        order = (var_place - jnp.arange(blocks)) % blocks
        return jnp.take(stacked, order, axis=0)

    def var_solve(values):
        line_count = spot_rows * planes
        lines = values.transpose(2, 0, 1).reshape(var_cols, line_count)
        shape = lines.shape
        local = reduce_solve(
            jnp.broadcast_to(lower_own.reshape(var_cols, 1), shape),
            jnp.broadcast_to(main_own.reshape(var_cols, 1, planes), (var_cols, spot_rows, planes)).reshape(shape),
            jnp.broadcast_to(upper_own.reshape(var_cols, 1), shape),
            lines,
            0,
        ).reshape(var_cols, spot_rows, planes)
        ends = gather_var(jnp.stack([local[0], local[var_cols - 1]]))
        left, right = interface_solve(ends[:, 0], ends[:, 1])
        solved = (
            local
            - left.reshape(1, spot_rows, planes) * g_own.reshape(var_cols, 1, planes)
            - right.reshape(1, spot_rows, planes) * h_own.reshape(var_cols, 1, planes)
        )
        return solved.transpose(1, 2, 0)

    def rate_solve(values):
        diffusion, advection = rate_terms(rate_geo[0])
        system = line_coefficients(
            diffusion, advection, rate_geo[0] / 3.0, rate_geo[1], rate_geo[2]
        )
        return implicit(system, values, 1)

    z_zero = time_step * edge_terms(option_value, False)
    z_one = spot_solve(z_zero)
    z_two = var_solve(z_one)
    z_three = rate_solve(z_two)
    w_zero = z_zero + half_step * edge_terms(z_three, True)
    w_one = spot_solve(w_zero)
    w_two = var_solve(w_one)
    w_three = rate_solve(w_two)
    return option_value + w_three


def solution(mesh):
    in_specs = (P("spot", None, "var"), P(), P(), P())
    out_specs = P("spot", None, "var")
    return jax.shard_map(shards, mesh=mesh, in_specs=in_specs, out_specs=out_specs, check_vma=False)
```

```python
import jax
import jax.numpy as jnp
from jax import lax
from jax.experimental import pallas as pl
from jax.experimental.pallas import tpu as pltpu
from jax.sharding import PartitionSpec as P

time_step = 0.01
solve_scale = 0.5 * time_step
half_step = 0.5 * time_step
spot_low = 0.5
spot_high = 2.5
var_low = 0.02
var_high = 1.0
rate_low = -0.1
rate_high = 0.2
dividend_yield = 0.02
reversion_var = 2.0
long_var = 0.04
vol_var = 0.6
reversion_rate = 0.1
long_rate = 0.05
vol_rate = 0.1
coupling_sv = -0.7 * vol_var
coupling_sr = 0.2 * vol_rate
coupling_vr = 0.1 * vol_var * vol_rate


def padded_2(array, sides, width):
    for axis, dim in sides:
        devices, length = (lax.axis_size(axis), array.shape[dim])
        up = [(i, (i + 1) % devices) for i in range(devices - 1)]
        down = [(j, i) for i, j in up]
        last = lax.slice_in_dim(array, length - width, length, axis=dim)
        initial = lax.slice_in_dim(array, 0, width, axis=dim)
        before = lax.ppermute(last, axis, up)
        after = lax.ppermute(initial, axis, down)
        array = jnp.concatenate([before, array, after], axis=dim)
    return array


def coordinates(node_list, low_end, high_end):
    length = node_list.shape[0]
    extended = jnp.concatenate(
        [jnp.full((1,), -1, jnp.int32), node_list, jnp.full((1,), 4 * length, jnp.int32)]
    )
    return low_end + (high_end - low_end) * extended.astype(jnp.float32) / (4 * length - 1)


def stencil_weights(coords):
    behind = coords[1:-1] - coords[:-2]
    ahead = coords[2:] - coords[1:-1]
    spread = behind + ahead
    first_diff = (
        -ahead / (behind * spread),
        (ahead - behind) / (behind * ahead),
        behind / (ahead * spread),
    )
    second_diff = (2.0 / (behind * spread), -2.0 / (behind * ahead), 2.0 / (ahead * spread))
    return (first_diff, second_diff)


def geometry(coords, position, dim_count, offset, length):
    first_diff, second_diff = stencil_weights(coords)
    vectors = (coords[1:-1],) + first_diff + second_diff
    target = [1] * dim_count
    target[position] = length
    pieces = [
        lax.dynamic_slice_in_dim(vector, offset, length).reshape(target) for vector in vectors
    ]
    return (pieces[0], tuple(pieces[1:4]), tuple(pieces[4:7]))


def spot_terms(spot_x, var_x, rate_x):
    return (0.5 * spot_x * spot_x * var_x, (rate_x - dividend_yield) * spot_x)


def var_terms(var_x):
    return (0.5 * vol_var * vol_var * var_x, reversion_var * (long_var - var_x))


def rate_terms(rate_x):
    return (0.5 * vol_rate * vol_rate, reversion_rate * (long_rate - rate_x))


def line_coefficients(diffusion, advection, reaction, first_diff, second_diff):
    behind = diffusion * second_diff[0] + advection * first_diff[0]
    centre = diffusion * second_diff[1] + advection * first_diff[1] - reaction
    ahead = diffusion * second_diff[2] + advection * first_diff[2]
    return (behind, centre, ahead)


def explicit_terms(padded, spot_geo, var_geo, rate_geo, mixing_only):
    spot_x, spot_first, spot_second = spot_geo
    var_x, var_first, var_second = var_geo
    rate_x, rate_first, rate_second = rate_geo
    spot_rows = padded.shape[0] - 2
    planes = padded.shape[1] - 2
    var_cols = padded.shape[2] - 2
    middle = padded[1:-1, 1:-1, 1:-1]
    cross_sv = 0.0
    cross_sr = 0.0
    cross_vr = 0.0
    for outer_step in range(3):
        for inner_step in range(3):
            cross_sv = (
                cross_sv
                + spot_first[outer_step]
                * var_first[inner_step]
                * padded[
                    outer_step : outer_step + spot_rows, 1:-1, inner_step : inner_step + var_cols
                ]
            )
            cross_sr = (
                cross_sr
                + spot_first[outer_step]
                * rate_first[inner_step]
                * padded[
                    outer_step : outer_step + spot_rows, inner_step : inner_step + planes, 1:-1
                ]
            )
            cross_vr = (
                cross_vr
                + var_first[outer_step]
                * rate_first[inner_step]
                * padded[1:-1, inner_step : inner_step + planes, outer_step : outer_step + var_cols]
            )
    root_var = jnp.sqrt(var_x)
    mixing = (
        coupling_sv * spot_x * var_x * cross_sv
        + coupling_sr * spot_x * root_var * cross_sr
        + coupling_vr * root_var * cross_vr
    )
    if mixing_only:
        return mixing
    reaction = rate_x / 3.0
    diffusion, advection = spot_terms(spot_x, var_x, rate_x)
    behind, centre, ahead = line_coefficients(
        diffusion, advection, reaction, spot_first, spot_second
    )
    along_spot = behind * padded[:-2, 1:-1, 1:-1] + centre * middle + ahead * padded[2:, 1:-1, 1:-1]
    diffusion, advection = var_terms(var_x)
    behind, centre, ahead = line_coefficients(diffusion, advection, reaction, var_first, var_second)
    along_var = behind * padded[1:-1, 1:-1, :-2] + centre * middle + ahead * padded[1:-1, 1:-1, 2:]
    diffusion, advection = rate_terms(rate_x)
    behind, centre, ahead = line_coefficients(
        diffusion, advection, reaction, rate_first, rate_second
    )
    along_rate = behind * padded[1:-1, :-2, 1:-1] + centre * middle + ahead * padded[1:-1, 2:, 1:-1]
    return mixing + along_spot + along_var + along_rate


def reduce_solve(lower_band, main_band, upper_band, right_side, dimension):
    length = right_side.shape[dimension]
    if length == 1:
        return right_side / main_band

    def even_rows(source):
        return lax.slice_in_dim(source, 0, length, 2, dimension)

    def odd_rows(source):
        return lax.slice_in_dim(source, 1, length, 2, dimension)

    def onward(source, filler):
        remainder = lax.slice_in_dim(source, 1, source.shape[dimension], axis=dimension)
        return jnp.concatenate(
            [remainder, jnp.zeros_like(lax.slice_in_dim(source, 0, 1, axis=dimension)) + filler],
            axis=dimension,
        )

    lower_even, main_even, upper_even, right_even = [
        even_rows(source) for source in (lower_band, main_band, upper_band, right_side)
    ]
    lower_odd, main_odd, upper_odd, right_odd = [
        odd_rows(source) for source in (lower_band, main_band, upper_band, right_side)
    ]
    lower_next = onward(lower_even, 0.0)
    main_next = onward(main_even, 1.0)
    upper_next = onward(upper_even, 0.0)
    right_next = onward(right_even, 0.0)
    ratio_back = -lower_odd / main_even
    ratio_ahead = -upper_odd / main_next
    solved_odd = reduce_solve(
        ratio_back * lower_even,
        main_odd + ratio_back * upper_even + ratio_ahead * lower_next,
        ratio_ahead * upper_next,
        right_odd + ratio_back * right_even + ratio_ahead * right_next,
        dimension,
    )
    remainder = lax.slice_in_dim(solved_odd, 0, solved_odd.shape[dimension] - 1, axis=dimension)
    solved_even = (
        right_even
        - lower_even
        * jnp.concatenate(
            [jnp.zeros_like(lax.slice_in_dim(solved_odd, 0, 1, axis=dimension)), remainder],
            axis=dimension,
        )
        - upper_even * solved_odd
    ) / main_even
    joined = jnp.stack([solved_even, solved_odd], axis=dimension + 1)
    return joined.reshape(right_side.shape)


def cyclic_kernel(lower_ref, main_ref, upper_ref, rhs_ref, out_ref, a_s, b_s, c_s, d_s):
    count, width = rhs_ref.shape
    pad = count // 2
    for ref, fill in ((a_s, 0.0), (b_s, 1.0), (c_s, 0.0), (d_s, 0.0)):
        ref[0:pad, :] = jnp.full((pad, width), fill, jnp.float32)
        ref[pad + count : 2 * pad + count, :] = jnp.full((pad, width), fill, jnp.float32)
    row = lax.broadcasted_iota(jnp.int32, (count, width), 0)
    a_s[pad : pad + count, :] = jnp.where(row == 0, 0.0, lower_ref[...])
    b_s[pad : pad + count, :] = main_ref[...]
    c_s[pad : pad + count, :] = jnp.where(row == count - 1, 0.0, upper_ref[...])
    d_s[pad : pad + count, :] = rhs_ref[...]
    stride = 1
    while stride < count:
        centre = slice(pad, pad + count)
        before = slice(pad - stride, pad - stride + count)
        after = slice(pad + stride, pad + stride + count)
        a, b, c, d = a_s[centre, :], b_s[centre, :], c_s[centre, :], d_s[centre, :]
        ratio_back = -a / b_s[before, :]
        ratio_ahead = -c / b_s[after, :]
        new_b = b + ratio_back * c_s[before, :] + ratio_ahead * a_s[after, :]
        new_d = d + ratio_back * d_s[before, :] + ratio_ahead * d_s[after, :]
        new_a = ratio_back * a_s[before, :]
        new_c = ratio_ahead * c_s[after, :]
        a_s[centre, :] = new_a
        b_s[centre, :] = new_b
        c_s[centre, :] = new_c
        d_s[centre, :] = new_d
        stride *= 2
    out_ref[...] = d_s[pad : pad + count, :] / b_s[pad : pad + count, :]


def line_solve(lower_band, main_band, upper_band, right_side):
    count, width = right_side.shape
    scratch = pltpu.VMEM((2 * (count // 2) + count, width), jnp.float32)
    return pl.pallas_call(
        cyclic_kernel,
        out_shape=jax.ShapeDtypeStruct((count, width), jnp.float32),
        scratch_shapes=[scratch] * 4,
    )(lower_band, main_band, upper_band, right_side)


def implicit(system, right_side, dimension):
    behind, centre, ahead = system
    lower_band = jnp.broadcast_to(-solve_scale * behind, right_side.shape)
    main_band = jnp.broadcast_to(1.0 - solve_scale * centre, right_side.shape)
    upper_band = jnp.broadcast_to(-solve_scale * ahead, right_side.shape)
    return reduce_solve(lower_band, main_band, upper_band, right_side, dimension)


def shards(option_value, spot_nodes, var_nodes, rate_nodes):
    spot_rows, planes, var_cols = option_value.shape
    line_count = planes * var_cols
    spot_place = lax.axis_index("spot")
    var_place = lax.axis_index("var")
    spot_coords = coordinates(spot_nodes, spot_low, spot_high)
    var_coords = coordinates(var_nodes, var_low, var_high)
    rate_coords = coordinates(rate_nodes, rate_low, rate_high)
    spot_geo = geometry(spot_coords, 0, 3, spot_place * spot_rows, spot_rows)
    var_geo = geometry(var_coords, 2, 3, var_place * var_cols, var_cols)
    rate_geo = geometry(rate_coords, 1, 3, 0, planes)
    spot_whole = geometry(spot_coords, 0, 2, 0, spot_nodes.shape[0])
    var_whole = geometry(var_coords, 1, 2, 0, var_nodes.shape[0])
    rate_plain = rate_geo[0].reshape(planes)
    var_plain = var_geo[0].reshape(var_cols)

    def edge_terms(values, mixing_only):
        padded = padded_2(values, (("spot", 0), ("var", 2)), 1)
        padded = jnp.pad(padded, ((0, 0), (1, 1), (0, 0)))
        return explicit_terms(padded, spot_geo, var_geo, rate_geo, mixing_only)

    def spot_solve(values):
        gathered = lax.all_to_all(
            values.reshape(spot_rows, line_count), "spot", split_axis=1, concat_axis=0, tiled=True
        )
        per_device = gathered.shape[1]
        first_line = spot_place * per_device
        rate_flat = jnp.broadcast_to(rate_plain.reshape(planes, 1), (planes, var_cols)).reshape(
            line_count
        )
        var_flat = jnp.broadcast_to(var_plain.reshape(1, var_cols), (planes, var_cols)).reshape(
            line_count
        )
        rate_line = lax.dynamic_slice_in_dim(rate_flat, first_line, per_device).reshape(
            1, per_device
        )
        var_line = lax.dynamic_slice_in_dim(var_flat, first_line, per_device).reshape(1, per_device)
        diffusion, advection = spot_terms(spot_whole[0], var_line, rate_line)
        system = line_coefficients(
            diffusion, advection, rate_line / 3.0, spot_whole[1], spot_whole[2]
        )
        solved = implicit(system, gathered, 0)
        return lax.all_to_all(solved, "spot", split_axis=0, concat_axis=1, tiled=True).reshape(
            spot_rows, planes, var_cols
        )

    var_count = var_nodes.shape[0]
    blocks = var_count // var_cols
    var_vec = var_coords[1:-1]
    var_first, var_second = stencil_weights(var_coords)
    var_diffusion, var_advection = var_terms(var_vec)
    var_behind = var_diffusion * var_second[0] + var_advection * var_first[0]
    var_middle = var_diffusion * var_second[1] + var_advection * var_first[1]
    var_ahead = var_diffusion * var_second[2] + var_advection * var_first[2]
    reaction_plain = rate_plain / 3.0
    var_lower = (-solve_scale * var_behind).reshape(blocks, var_cols)
    var_upper = (-solve_scale * var_ahead).reshape(blocks, var_cols)
    var_main = (
        1.0 - solve_scale * (var_middle.reshape(var_count, 1) - reaction_plain.reshape(1, planes))
    ).reshape(blocks, var_cols, planes)

    column_shape = (var_cols, blocks, 2, planes)
    lower_cols = jnp.broadcast_to(var_lower.T.reshape(var_cols, blocks, 1, 1), column_shape)
    upper_cols = jnp.broadcast_to(var_upper.T.reshape(var_cols, blocks, 1, 1), column_shape)
    main_cols = jnp.broadcast_to(
        var_main.transpose(1, 0, 2).reshape(var_cols, blocks, 1, planes), column_shape
    )
    position = lax.broadcasted_iota(jnp.int32, column_shape, 0)
    kind = lax.broadcasted_iota(jnp.int32, column_shape, 2)
    coupling = jnp.where(
        (kind == 0) & (position == 0),
        var_lower[:, 0].reshape(1, blocks, 1, 1),
        jnp.where(
            (kind == 1) & (position == var_cols - 1),
            var_upper[:, var_cols - 1].reshape(1, blocks, 1, 1),
            0.0,
        ),
    )
    flat = (var_cols, blocks * 2 * planes)
    columns = line_solve(
        lower_cols.reshape(flat),
        main_cols.reshape(flat),
        upper_cols.reshape(flat),
        coupling.reshape(flat),
    ).reshape(column_shape)
    g_first, g_last = columns[0, :, 0, :], columns[var_cols - 1, :, 0, :]
    h_first, h_last = columns[0, :, 1, :], columns[var_cols - 1, :, 1, :]
    g_own = lax.dynamic_index_in_dim(columns[:, :, 0, :], var_place, 1, keepdims=False)
    h_own = lax.dynamic_index_in_dim(columns[:, :, 1, :], var_place, 1, keepdims=False)
    lower_own = lax.dynamic_index_in_dim(var_lower, var_place, 0, keepdims=False)
    upper_own = lax.dynamic_index_in_dim(var_upper, var_place, 0, keepdims=False)
    main_own = lax.dynamic_index_in_dim(var_main, var_place, 0, keepdims=False)

    def interface_solve(y_first, y_last):
        size = 2 * (blocks - 1)
        matrix = [[None] * size for _ in range(size)]
        rhs = [None] * size
        for b in range(blocks - 1):
            matrix[2 * b][2 * b] = 1.0
            if b >= 1:
                matrix[2 * b][2 * b - 2] = g_last[b]
            matrix[2 * b][2 * b + 1] = h_last[b]
            rhs[2 * b] = y_last[b]
            matrix[2 * b + 1][2 * b + 1] = 1.0
            matrix[2 * b + 1][2 * b] = g_first[b + 1]
            if b + 2 <= blocks - 1:
                matrix[2 * b + 1][2 * b + 3] = h_first[b + 1]
            rhs[2 * b + 1] = y_first[b + 1]
        for k in range(size):
            for i in range(k + 1, size):
                if matrix[i][k] is None:
                    continue
                factor = matrix[i][k] / matrix[k][k]
                for c in range(k + 1, size):
                    if matrix[k][c] is None:
                        continue
                    update = factor * matrix[k][c]
                    matrix[i][c] = -update if matrix[i][c] is None else matrix[i][c] - update
                rhs[i] = rhs[i] - factor * rhs[k]
                matrix[i][k] = None
        solved = [None] * size
        for k in reversed(range(size)):
            total = rhs[k]
            for c in range(k + 1, size):
                if matrix[k][c] is not None:
                    total = total - matrix[k][c] * solved[c]
            solved[k] = total / matrix[k][k]
        zero = jnp.zeros_like(y_first[0])
        left = jnp.stack([zero] + [solved[2 * b] for b in range(blocks - 1)])
        right = jnp.stack([solved[2 * b + 1] for b in range(blocks - 1)] + [zero])
        return (
            lax.dynamic_index_in_dim(left, var_place, 0, keepdims=False),
            lax.dynamic_index_in_dim(right, var_place, 0, keepdims=False),
        )

    def gather_var(ends):
        parts = [ends]
        for shift in range(1, blocks):
            pairs = [(i, (i + shift) % blocks) for i in range(blocks)]
            parts.append(lax.ppermute(ends, "var", pairs))
        stacked = jnp.stack(parts)
        order = (var_place - jnp.arange(blocks)) % blocks
        return jnp.take(stacked, order, axis=0)

    def var_solve(values):
        line_count = spot_rows * planes
        lines = values.transpose(2, 0, 1).reshape(var_cols, line_count)
        shape = lines.shape
        local = line_solve(
            jnp.broadcast_to(lower_own.reshape(var_cols, 1), shape),
            jnp.broadcast_to(main_own.reshape(var_cols, 1, planes), (var_cols, spot_rows, planes)).reshape(shape),
            jnp.broadcast_to(upper_own.reshape(var_cols, 1), shape),
            lines,
        ).reshape(var_cols, spot_rows, planes)
        ends = gather_var(jnp.stack([local[0], local[var_cols - 1]]))
        left, right = interface_solve(ends[:, 0], ends[:, 1])
        solved = (
            local
            - left.reshape(1, spot_rows, planes) * g_own.reshape(var_cols, 1, planes)
            - right.reshape(1, spot_rows, planes) * h_own.reshape(var_cols, 1, planes)
        )
        return solved.transpose(1, 2, 0)

    def rate_solve(values):
        diffusion, advection = rate_terms(rate_geo[0])
        system = line_coefficients(
            diffusion, advection, rate_geo[0] / 3.0, rate_geo[1], rate_geo[2]
        )
        return implicit(system, values, 1)

    z_zero = time_step * edge_terms(option_value, False)
    z_one = spot_solve(z_zero)
    z_two = var_solve(z_one)
    z_three = rate_solve(z_two)
    w_zero = z_zero + half_step * edge_terms(z_three, True)
    w_one = spot_solve(w_zero)
    w_two = var_solve(w_one)
    w_three = rate_solve(w_two)
    return option_value + w_three


def solution(mesh):
    in_specs = (P("spot", None, "var"), P(), P(), P())
    out_specs = P("spot", None, "var")
    return jax.shard_map(shards, mesh=mesh, in_specs=in_specs, out_specs=out_specs, check_vma=False)
```

```python
import functools

import jax
import jax.numpy as jnp
from jax import lax
from jax.experimental import pallas as pl
from jax.experimental.pallas import tpu as pltpu
from jax.sharding import PartitionSpec as P

time_step = 0.01
solve_scale = 0.5 * time_step
half_step = 0.5 * time_step
spot_low = 0.5
spot_high = 2.5
var_low = 0.02
var_high = 1.0
rate_low = -0.1
rate_high = 0.2
dividend_yield = 0.02
reversion_var = 2.0
long_var = 0.04
vol_var = 0.6
reversion_rate = 0.1
long_rate = 0.05
vol_rate = 0.1
coupling_sv = -0.7 * vol_var
coupling_sr = 0.2 * vol_rate
coupling_vr = 0.1 * vol_var * vol_rate


def padded_2(array, sides, width):
    for axis, dim in sides:
        devices, length = (lax.axis_size(axis), array.shape[dim])
        up = [(i, (i + 1) % devices) for i in range(devices - 1)]
        down = [(j, i) for i, j in up]
        last = lax.slice_in_dim(array, length - width, length, axis=dim)
        initial = lax.slice_in_dim(array, 0, width, axis=dim)
        before = lax.ppermute(last, axis, up)
        after = lax.ppermute(initial, axis, down)
        array = jnp.concatenate([before, array, after], axis=dim)
    return array


def coordinates(node_list, low_end, high_end):
    length = node_list.shape[0]
    extended = jnp.concatenate(
        [jnp.full((1,), -1, jnp.int32), node_list, jnp.full((1,), 4 * length, jnp.int32)]
    )
    return low_end + (high_end - low_end) * extended.astype(jnp.float32) / (4 * length - 1)


def stencil_weights(coords):
    behind = coords[1:-1] - coords[:-2]
    ahead = coords[2:] - coords[1:-1]
    spread = behind + ahead
    first_diff = (
        -ahead / (behind * spread),
        (ahead - behind) / (behind * ahead),
        behind / (ahead * spread),
    )
    second_diff = (2.0 / (behind * spread), -2.0 / (behind * ahead), 2.0 / (ahead * spread))
    return (first_diff, second_diff)


def geometry(coords, position, dim_count, offset, length):
    first_diff, second_diff = stencil_weights(coords)
    vectors = (coords[1:-1],) + first_diff + second_diff
    target = [1] * dim_count
    target[position] = length
    pieces = [
        lax.dynamic_slice_in_dim(vector, offset, length).reshape(target) for vector in vectors
    ]
    return (pieces[0], tuple(pieces[1:4]), tuple(pieces[4:7]))


def spot_terms(spot_x, var_x, rate_x):
    return (0.5 * spot_x * spot_x * var_x, (rate_x - dividend_yield) * spot_x)


def var_terms(var_x):
    return (0.5 * vol_var * vol_var * var_x, reversion_var * (long_var - var_x))


def rate_terms(rate_x):
    return (0.5 * vol_rate * vol_rate, reversion_rate * (long_rate - rate_x))


def line_coefficients(diffusion, advection, reaction, first_diff, second_diff):
    behind = diffusion * second_diff[0] + advection * first_diff[0]
    centre = diffusion * second_diff[1] + advection * first_diff[1] - reaction
    ahead = diffusion * second_diff[2] + advection * first_diff[2]
    return (behind, centre, ahead)


def explicit_terms(padded, spot_geo, var_geo, rate_geo, mixing_only):
    spot_x, spot_first, spot_second = spot_geo
    var_x, var_first, var_second = var_geo
    rate_x, rate_first, rate_second = rate_geo
    spot_rows = padded.shape[0] - 2
    planes = padded.shape[1] - 2
    var_cols = padded.shape[2] - 2
    middle = padded[1:-1, 1:-1, 1:-1]
    cross_sv = 0.0
    cross_sr = 0.0
    cross_vr = 0.0
    for outer_step in range(3):
        for inner_step in range(3):
            cross_sv = (
                cross_sv
                + spot_first[outer_step]
                * var_first[inner_step]
                * padded[
                    outer_step : outer_step + spot_rows, 1:-1, inner_step : inner_step + var_cols
                ]
            )
            cross_sr = (
                cross_sr
                + spot_first[outer_step]
                * rate_first[inner_step]
                * padded[
                    outer_step : outer_step + spot_rows, inner_step : inner_step + planes, 1:-1
                ]
            )
            cross_vr = (
                cross_vr
                + var_first[outer_step]
                * rate_first[inner_step]
                * padded[1:-1, inner_step : inner_step + planes, outer_step : outer_step + var_cols]
            )
    root_var = jnp.sqrt(var_x)
    mixing = (
        coupling_sv * spot_x * var_x * cross_sv
        + coupling_sr * spot_x * root_var * cross_sr
        + coupling_vr * root_var * cross_vr
    )
    if mixing_only:
        return mixing
    reaction = rate_x / 3.0
    diffusion, advection = spot_terms(spot_x, var_x, rate_x)
    behind, centre, ahead = line_coefficients(
        diffusion, advection, reaction, spot_first, spot_second
    )
    along_spot = behind * padded[:-2, 1:-1, 1:-1] + centre * middle + ahead * padded[2:, 1:-1, 1:-1]
    diffusion, advection = var_terms(var_x)
    behind, centre, ahead = line_coefficients(diffusion, advection, reaction, var_first, var_second)
    along_var = behind * padded[1:-1, 1:-1, :-2] + centre * middle + ahead * padded[1:-1, 1:-1, 2:]
    diffusion, advection = rate_terms(rate_x)
    behind, centre, ahead = line_coefficients(
        diffusion, advection, reaction, rate_first, rate_second
    )
    along_rate = behind * padded[1:-1, :-2, 1:-1] + centre * middle + ahead * padded[1:-1, 2:, 1:-1]
    return mixing + along_spot + along_var + along_rate


def reduce_solve(lower_band, main_band, upper_band, right_side, dimension):
    length = right_side.shape[dimension]
    if length == 1:
        return right_side / main_band

    def even_rows(source):
        return lax.slice_in_dim(source, 0, length, 2, dimension)

    def odd_rows(source):
        return lax.slice_in_dim(source, 1, length, 2, dimension)

    def onward(source, filler):
        remainder = lax.slice_in_dim(source, 1, source.shape[dimension], axis=dimension)
        return jnp.concatenate(
            [remainder, jnp.zeros_like(lax.slice_in_dim(source, 0, 1, axis=dimension)) + filler],
            axis=dimension,
        )

    lower_even, main_even, upper_even, right_even = [
        even_rows(source) for source in (lower_band, main_band, upper_band, right_side)
    ]
    lower_odd, main_odd, upper_odd, right_odd = [
        odd_rows(source) for source in (lower_band, main_band, upper_band, right_side)
    ]
    lower_next = onward(lower_even, 0.0)
    main_next = onward(main_even, 1.0)
    upper_next = onward(upper_even, 0.0)
    right_next = onward(right_even, 0.0)
    ratio_back = -lower_odd / main_even
    ratio_ahead = -upper_odd / main_next
    solved_odd = reduce_solve(
        ratio_back * lower_even,
        main_odd + ratio_back * upper_even + ratio_ahead * lower_next,
        ratio_ahead * upper_next,
        right_odd + ratio_back * right_even + ratio_ahead * right_next,
        dimension,
    )
    remainder = lax.slice_in_dim(solved_odd, 0, solved_odd.shape[dimension] - 1, axis=dimension)
    solved_even = (
        right_even
        - lower_even
        * jnp.concatenate(
            [jnp.zeros_like(lax.slice_in_dim(solved_odd, 0, 1, axis=dimension)), remainder],
            axis=dimension,
        )
        - upper_even * solved_odd
    ) / main_even
    joined = jnp.stack([solved_even, solved_odd], axis=dimension + 1)
    return joined.reshape(right_side.shape)


def cyclic_kernel(lower_ref, main_ref, upper_ref, rhs_ref, out_ref, a_s, b_s, c_s, d_s):
    count, width = rhs_ref.shape
    pad = count // 2
    for ref, fill in ((a_s, 0.0), (b_s, 1.0), (c_s, 0.0), (d_s, 0.0)):
        ref[0:pad, :] = jnp.full((pad, width), fill, jnp.float32)
        ref[pad + count : 2 * pad + count, :] = jnp.full((pad, width), fill, jnp.float32)
    row = lax.broadcasted_iota(jnp.int32, (count, width), 0)
    a_s[pad : pad + count, :] = jnp.where(row == 0, 0.0, lower_ref[...])
    b_s[pad : pad + count, :] = main_ref[...]
    c_s[pad : pad + count, :] = jnp.where(row == count - 1, 0.0, upper_ref[...])
    d_s[pad : pad + count, :] = rhs_ref[...]
    stride = 1
    while stride < count:
        centre = slice(pad, pad + count)
        before = slice(pad - stride, pad - stride + count)
        after = slice(pad + stride, pad + stride + count)
        a, b, c, d = a_s[centre, :], b_s[centre, :], c_s[centre, :], d_s[centre, :]
        ratio_back = -a / b_s[before, :]
        ratio_ahead = -c / b_s[after, :]
        new_b = b + ratio_back * c_s[before, :] + ratio_ahead * a_s[after, :]
        new_d = d + ratio_back * d_s[before, :] + ratio_ahead * d_s[after, :]
        new_a = ratio_back * a_s[before, :]
        new_c = ratio_ahead * c_s[after, :]
        a_s[centre, :] = new_a
        b_s[centre, :] = new_b
        c_s[centre, :] = new_c
        d_s[centre, :] = new_d
        stride *= 2
    out_ref[...] = d_s[pad : pad + count, :] / b_s[pad : pad + count, :]


def line_solve(lower_band, main_band, upper_band, right_side):
    count, width = right_side.shape
    scratch = pltpu.VMEM((2 * (count // 2) + count, width), jnp.float32)
    return pl.pallas_call(
        cyclic_kernel,
        out_shape=jax.ShapeDtypeStruct((count, width), jnp.float32),
        scratch_shapes=[scratch] * 4,
    )(lower_band, main_band, upper_band, right_side)


def gather_kernel(blocks, ends_ref, out_ref, landed, send_sem, recv_sem):
    me = lax.axis_index("var")
    spot = lax.axis_index("spot")
    barrier = pltpu.get_barrier_semaphore()
    for shift in range(1, blocks):
        peer = lax.rem(me + shift, blocks)
        pl.semaphore_signal(barrier, inc=1, device_id=(spot, peer), device_id_type=pl.DeviceIdType.MESH)
    pl.semaphore_wait(barrier, blocks - 1)
    copies = []
    for shift in range(1, blocks):
        peer = lax.rem(me + shift, blocks)
        copy = pltpu.make_async_remote_copy(
            src_ref=ends_ref,
            dst_ref=landed.at[shift - 1],
            send_sem=send_sem.at[shift - 1],
            recv_sem=recv_sem.at[shift - 1],
            device_id=(spot, peer),
            device_id_type=pl.DeviceIdType.MESH,
        )
        copy.start()
        copies.append(copy)
    out_ref[0] = ends_ref[...]
    for copy in copies:
        copy.wait()
    for shift in range(1, blocks):
        out_ref[shift] = landed[shift - 1]


def gather_var(ends, blocks):
    return pl.pallas_call(
        functools.partial(gather_kernel, blocks),
        out_shape=jax.ShapeDtypeStruct((blocks,) + ends.shape, jnp.float32),
        scratch_shapes=[
            pltpu.VMEM((blocks - 1,) + ends.shape, jnp.float32),
            pltpu.SemaphoreType.DMA((blocks - 1,)),
            pltpu.SemaphoreType.DMA((blocks - 1,)),
        ],
        compiler_params=pltpu.CompilerParams(collective_id=0, has_side_effects=True),
    )(ends)


def implicit(system, right_side, dimension):
    behind, centre, ahead = system
    lower_band = jnp.broadcast_to(-solve_scale * behind, right_side.shape)
    main_band = jnp.broadcast_to(1.0 - solve_scale * centre, right_side.shape)
    upper_band = jnp.broadcast_to(-solve_scale * ahead, right_side.shape)
    return reduce_solve(lower_band, main_band, upper_band, right_side, dimension)


def shards(option_value, spot_nodes, var_nodes, rate_nodes):
    spot_rows, planes, var_cols = option_value.shape
    line_count = planes * var_cols
    spot_place = lax.axis_index("spot")
    var_place = lax.axis_index("var")
    spot_coords = coordinates(spot_nodes, spot_low, spot_high)
    var_coords = coordinates(var_nodes, var_low, var_high)
    rate_coords = coordinates(rate_nodes, rate_low, rate_high)
    spot_geo = geometry(spot_coords, 0, 3, spot_place * spot_rows, spot_rows)
    var_geo = geometry(var_coords, 2, 3, var_place * var_cols, var_cols)
    rate_geo = geometry(rate_coords, 1, 3, 0, planes)
    spot_whole = geometry(spot_coords, 0, 2, 0, spot_nodes.shape[0])
    var_whole = geometry(var_coords, 1, 2, 0, var_nodes.shape[0])
    rate_plain = rate_geo[0].reshape(planes)
    var_plain = var_geo[0].reshape(var_cols)

    def edge_terms(values, mixing_only):
        padded = padded_2(values, (("spot", 0), ("var", 2)), 1)
        padded = jnp.pad(padded, ((0, 0), (1, 1), (0, 0)))
        return explicit_terms(padded, spot_geo, var_geo, rate_geo, mixing_only)

    def spot_solve(values):
        gathered = lax.all_to_all(
            values.reshape(spot_rows, line_count), "spot", split_axis=1, concat_axis=0, tiled=True
        )
        per_device = gathered.shape[1]
        first_line = spot_place * per_device
        rate_flat = jnp.broadcast_to(rate_plain.reshape(planes, 1), (planes, var_cols)).reshape(
            line_count
        )
        var_flat = jnp.broadcast_to(var_plain.reshape(1, var_cols), (planes, var_cols)).reshape(
            line_count
        )
        rate_line = lax.dynamic_slice_in_dim(rate_flat, first_line, per_device).reshape(
            1, per_device
        )
        var_line = lax.dynamic_slice_in_dim(var_flat, first_line, per_device).reshape(1, per_device)
        diffusion, advection = spot_terms(spot_whole[0], var_line, rate_line)
        system = line_coefficients(
            diffusion, advection, rate_line / 3.0, spot_whole[1], spot_whole[2]
        )
        solved = implicit(system, gathered, 0)
        return lax.all_to_all(solved, "spot", split_axis=0, concat_axis=1, tiled=True).reshape(
            spot_rows, planes, var_cols
        )

    var_count = var_nodes.shape[0]
    blocks = var_count // var_cols
    var_vec = var_coords[1:-1]
    var_first, var_second = stencil_weights(var_coords)
    var_diffusion, var_advection = var_terms(var_vec)
    var_behind = var_diffusion * var_second[0] + var_advection * var_first[0]
    var_middle = var_diffusion * var_second[1] + var_advection * var_first[1]
    var_ahead = var_diffusion * var_second[2] + var_advection * var_first[2]
    reaction_plain = rate_plain / 3.0
    var_lower = (-solve_scale * var_behind).reshape(blocks, var_cols)
    var_upper = (-solve_scale * var_ahead).reshape(blocks, var_cols)
    var_main = (
        1.0 - solve_scale * (var_middle.reshape(var_count, 1) - reaction_plain.reshape(1, planes))
    ).reshape(blocks, var_cols, planes)

    column_shape = (var_cols, blocks, 2, planes)
    lower_cols = jnp.broadcast_to(var_lower.T.reshape(var_cols, blocks, 1, 1), column_shape)
    upper_cols = jnp.broadcast_to(var_upper.T.reshape(var_cols, blocks, 1, 1), column_shape)
    main_cols = jnp.broadcast_to(
        var_main.transpose(1, 0, 2).reshape(var_cols, blocks, 1, planes), column_shape
    )
    position = lax.broadcasted_iota(jnp.int32, column_shape, 0)
    kind = lax.broadcasted_iota(jnp.int32, column_shape, 2)
    coupling = jnp.where(
        (kind == 0) & (position == 0),
        var_lower[:, 0].reshape(1, blocks, 1, 1),
        jnp.where(
            (kind == 1) & (position == var_cols - 1),
            var_upper[:, var_cols - 1].reshape(1, blocks, 1, 1),
            0.0,
        ),
    )
    flat = (var_cols, blocks * 2 * planes)
    columns = line_solve(
        lower_cols.reshape(flat),
        main_cols.reshape(flat),
        upper_cols.reshape(flat),
        coupling.reshape(flat),
    ).reshape(column_shape)
    g_first, g_last = columns[0, :, 0, :], columns[var_cols - 1, :, 0, :]
    h_first, h_last = columns[0, :, 1, :], columns[var_cols - 1, :, 1, :]
    g_own = lax.dynamic_index_in_dim(columns[:, :, 0, :], var_place, 1, keepdims=False)
    h_own = lax.dynamic_index_in_dim(columns[:, :, 1, :], var_place, 1, keepdims=False)
    lower_own = lax.dynamic_index_in_dim(var_lower, var_place, 0, keepdims=False)
    upper_own = lax.dynamic_index_in_dim(var_upper, var_place, 0, keepdims=False)
    main_own = lax.dynamic_index_in_dim(var_main, var_place, 0, keepdims=False)

    def interface_solve(y_first, y_last):
        size = 2 * (blocks - 1)
        matrix = [[None] * size for _ in range(size)]
        rhs = [None] * size
        for b in range(blocks - 1):
            matrix[2 * b][2 * b] = 1.0
            if b >= 1:
                matrix[2 * b][2 * b - 2] = g_last[b]
            matrix[2 * b][2 * b + 1] = h_last[b]
            rhs[2 * b] = y_last[b]
            matrix[2 * b + 1][2 * b + 1] = 1.0
            matrix[2 * b + 1][2 * b] = g_first[b + 1]
            if b + 2 <= blocks - 1:
                matrix[2 * b + 1][2 * b + 3] = h_first[b + 1]
            rhs[2 * b + 1] = y_first[b + 1]
        for k in range(size):
            for i in range(k + 1, size):
                if matrix[i][k] is None:
                    continue
                factor = matrix[i][k] / matrix[k][k]
                for c in range(k + 1, size):
                    if matrix[k][c] is None:
                        continue
                    update = factor * matrix[k][c]
                    matrix[i][c] = -update if matrix[i][c] is None else matrix[i][c] - update
                rhs[i] = rhs[i] - factor * rhs[k]
                matrix[i][k] = None
        solved = [None] * size
        for k in reversed(range(size)):
            total = rhs[k]
            for c in range(k + 1, size):
                if matrix[k][c] is not None:
                    total = total - matrix[k][c] * solved[c]
            solved[k] = total / matrix[k][k]
        zero = jnp.zeros_like(y_first[0])
        left = jnp.stack([zero] + [solved[2 * b] for b in range(blocks - 1)])
        right = jnp.stack([solved[2 * b + 1] for b in range(blocks - 1)] + [zero])
        return (
            lax.dynamic_index_in_dim(left, var_place, 0, keepdims=False),
            lax.dynamic_index_in_dim(right, var_place, 0, keepdims=False),
        )

    def gather_ends(ends):
        stacked = gather_var(ends, blocks)
        order = (var_place - jnp.arange(blocks)) % blocks
        return jnp.take(stacked, order, axis=0)

    def var_solve(values):
        line_count = spot_rows * planes
        lines = values.transpose(2, 0, 1).reshape(var_cols, line_count)
        shape = lines.shape
        local = line_solve(
            jnp.broadcast_to(lower_own.reshape(var_cols, 1), shape),
            jnp.broadcast_to(main_own.reshape(var_cols, 1, planes), (var_cols, spot_rows, planes)).reshape(shape),
            jnp.broadcast_to(upper_own.reshape(var_cols, 1), shape),
            lines,
        ).reshape(var_cols, spot_rows, planes)
        ends = gather_ends(jnp.stack([local[0], local[var_cols - 1]]))
        left, right = interface_solve(ends[:, 0], ends[:, 1])
        solved = (
            local
            - left.reshape(1, spot_rows, planes) * g_own.reshape(var_cols, 1, planes)
            - right.reshape(1, spot_rows, planes) * h_own.reshape(var_cols, 1, planes)
        )
        return solved.transpose(1, 2, 0)

    def rate_solve(values):
        diffusion, advection = rate_terms(rate_geo[0])
        system = line_coefficients(
            diffusion, advection, rate_geo[0] / 3.0, rate_geo[1], rate_geo[2]
        )
        return implicit(system, values, 1)

    z_zero = time_step * edge_terms(option_value, False)
    z_one = spot_solve(z_zero)
    z_two = var_solve(z_one)
    z_three = rate_solve(z_two)
    w_zero = z_zero + half_step * edge_terms(z_three, True)
    w_one = spot_solve(w_zero)
    w_two = var_solve(w_one)
    w_three = rate_solve(w_two)
    return option_value + w_three


def solution(mesh):
    in_specs = (P("spot", None, "var"), P(), P(), P())
    out_specs = P("spot", None, "var")
    return jax.shard_map(shards, mesh=mesh, in_specs=in_specs, out_specs=out_specs, check_vma=False)
```

```python
import functools

import jax
import jax.numpy as jnp
from jax import lax
from jax.experimental import pallas as pl
from jax.experimental.pallas import tpu as pltpu
from jax.sharding import PartitionSpec as P

time_step = 0.01
solve_scale = 0.5 * time_step
half_step = 0.5 * time_step
spot_low = 0.5
spot_high = 2.5
var_low = 0.02
var_high = 1.0
rate_low = -0.1
rate_high = 0.2
dividend_yield = 0.02
reversion_var = 2.0
long_var = 0.04
vol_var = 0.6
reversion_rate = 0.1
long_rate = 0.05
vol_rate = 0.1
coupling_sv = -0.7 * vol_var
coupling_sr = 0.2 * vol_rate
coupling_vr = 0.1 * vol_var * vol_rate


def padded_2(array, sides, width):
    for axis, dim in sides:
        devices, length = (lax.axis_size(axis), array.shape[dim])
        up = [(i, (i + 1) % devices) for i in range(devices - 1)]
        down = [(j, i) for i, j in up]
        last = lax.slice_in_dim(array, length - width, length, axis=dim)
        initial = lax.slice_in_dim(array, 0, width, axis=dim)
        before = lax.ppermute(last, axis, up)
        after = lax.ppermute(initial, axis, down)
        array = jnp.concatenate([before, array, after], axis=dim)
    return array


def coordinates(node_list, low_end, high_end):
    length = node_list.shape[0]
    extended = jnp.concatenate(
        [jnp.full((1,), -1, jnp.int32), node_list, jnp.full((1,), 4 * length, jnp.int32)]
    )
    return low_end + (high_end - low_end) * extended.astype(jnp.float32) / (4 * length - 1)


def stencil_weights(coords):
    behind = coords[1:-1] - coords[:-2]
    ahead = coords[2:] - coords[1:-1]
    spread = behind + ahead
    first_diff = (
        -ahead / (behind * spread),
        (ahead - behind) / (behind * ahead),
        behind / (ahead * spread),
    )
    second_diff = (2.0 / (behind * spread), -2.0 / (behind * ahead), 2.0 / (ahead * spread))
    return (first_diff, second_diff)


def geometry(coords, position, dim_count, offset, length):
    first_diff, second_diff = stencil_weights(coords)
    vectors = (coords[1:-1],) + first_diff + second_diff
    target = [1] * dim_count
    target[position] = length
    pieces = [
        lax.dynamic_slice_in_dim(vector, offset, length).reshape(target) for vector in vectors
    ]
    return (pieces[0], tuple(pieces[1:4]), tuple(pieces[4:7]))


def spot_terms(spot_x, var_x, rate_x):
    return (0.5 * spot_x * spot_x * var_x, (rate_x - dividend_yield) * spot_x)


def var_terms(var_x):
    return (0.5 * vol_var * vol_var * var_x, reversion_var * (long_var - var_x))


def rate_terms(rate_x):
    return (0.5 * vol_rate * vol_rate, reversion_rate * (long_rate - rate_x))


def line_coefficients(diffusion, advection, reaction, first_diff, second_diff):
    behind = diffusion * second_diff[0] + advection * first_diff[0]
    centre = diffusion * second_diff[1] + advection * first_diff[1] - reaction
    ahead = diffusion * second_diff[2] + advection * first_diff[2]
    return (behind, centre, ahead)


def explicit_terms(padded, spot_geo, var_geo, rate_geo, mixing_only):
    spot_x, spot_first, spot_second = spot_geo
    var_x, var_first, var_second = var_geo
    rate_x, rate_first, rate_second = rate_geo
    spot_rows = padded.shape[0] - 2
    planes = padded.shape[1] - 2
    var_cols = padded.shape[2] - 2
    middle = padded[1:-1, 1:-1, 1:-1]
    cross_sv = 0.0
    cross_sr = 0.0
    cross_vr = 0.0
    for outer_step in range(3):
        for inner_step in range(3):
            cross_sv = (
                cross_sv
                + spot_first[outer_step]
                * var_first[inner_step]
                * padded[
                    outer_step : outer_step + spot_rows, 1:-1, inner_step : inner_step + var_cols
                ]
            )
            cross_sr = (
                cross_sr
                + spot_first[outer_step]
                * rate_first[inner_step]
                * padded[
                    outer_step : outer_step + spot_rows, inner_step : inner_step + planes, 1:-1
                ]
            )
            cross_vr = (
                cross_vr
                + var_first[outer_step]
                * rate_first[inner_step]
                * padded[1:-1, inner_step : inner_step + planes, outer_step : outer_step + var_cols]
            )
    root_var = jnp.sqrt(var_x)
    mixing = (
        coupling_sv * spot_x * var_x * cross_sv
        + coupling_sr * spot_x * root_var * cross_sr
        + coupling_vr * root_var * cross_vr
    )
    if mixing_only:
        return mixing
    reaction = rate_x / 3.0
    diffusion, advection = spot_terms(spot_x, var_x, rate_x)
    behind, centre, ahead = line_coefficients(
        diffusion, advection, reaction, spot_first, spot_second
    )
    along_spot = behind * padded[:-2, 1:-1, 1:-1] + centre * middle + ahead * padded[2:, 1:-1, 1:-1]
    diffusion, advection = var_terms(var_x)
    behind, centre, ahead = line_coefficients(diffusion, advection, reaction, var_first, var_second)
    along_var = behind * padded[1:-1, 1:-1, :-2] + centre * middle + ahead * padded[1:-1, 1:-1, 2:]
    diffusion, advection = rate_terms(rate_x)
    behind, centre, ahead = line_coefficients(
        diffusion, advection, reaction, rate_first, rate_second
    )
    along_rate = behind * padded[1:-1, :-2, 1:-1] + centre * middle + ahead * padded[1:-1, 2:, 1:-1]
    return mixing + along_spot + along_var + along_rate


def reduce_solve(lower_band, main_band, upper_band, right_side, dimension):
    length = right_side.shape[dimension]
    if length == 1:
        return right_side / main_band

    def even_rows(source):
        return lax.slice_in_dim(source, 0, length, 2, dimension)

    def odd_rows(source):
        return lax.slice_in_dim(source, 1, length, 2, dimension)

    def onward(source, filler):
        remainder = lax.slice_in_dim(source, 1, source.shape[dimension], axis=dimension)
        return jnp.concatenate(
            [remainder, jnp.zeros_like(lax.slice_in_dim(source, 0, 1, axis=dimension)) + filler],
            axis=dimension,
        )

    lower_even, main_even, upper_even, right_even = [
        even_rows(source) for source in (lower_band, main_band, upper_band, right_side)
    ]
    lower_odd, main_odd, upper_odd, right_odd = [
        odd_rows(source) for source in (lower_band, main_band, upper_band, right_side)
    ]
    lower_next = onward(lower_even, 0.0)
    main_next = onward(main_even, 1.0)
    upper_next = onward(upper_even, 0.0)
    right_next = onward(right_even, 0.0)
    ratio_back = -lower_odd / main_even
    ratio_ahead = -upper_odd / main_next
    solved_odd = reduce_solve(
        ratio_back * lower_even,
        main_odd + ratio_back * upper_even + ratio_ahead * lower_next,
        ratio_ahead * upper_next,
        right_odd + ratio_back * right_even + ratio_ahead * right_next,
        dimension,
    )
    remainder = lax.slice_in_dim(solved_odd, 0, solved_odd.shape[dimension] - 1, axis=dimension)
    solved_even = (
        right_even
        - lower_even
        * jnp.concatenate(
            [jnp.zeros_like(lax.slice_in_dim(solved_odd, 0, 1, axis=dimension)), remainder],
            axis=dimension,
        )
        - upper_even * solved_odd
    ) / main_even
    joined = jnp.stack([solved_even, solved_odd], axis=dimension + 1)
    return joined.reshape(right_side.shape)


def cyclic_kernel(lower_ref, main_ref, upper_ref, rhs_ref, out_ref, a_s, b_s, c_s, d_s):
    count, width = rhs_ref.shape
    pad = count // 2
    for ref, fill in ((a_s, 0.0), (b_s, 1.0), (c_s, 0.0), (d_s, 0.0)):
        ref[0:pad, :] = jnp.full((pad, width), fill, jnp.float32)
        ref[pad + count : 2 * pad + count, :] = jnp.full((pad, width), fill, jnp.float32)
    row = lax.broadcasted_iota(jnp.int32, (count, width), 0)
    a_s[pad : pad + count, :] = jnp.where(row == 0, 0.0, lower_ref[...])
    b_s[pad : pad + count, :] = main_ref[...]
    c_s[pad : pad + count, :] = jnp.where(row == count - 1, 0.0, upper_ref[...])
    d_s[pad : pad + count, :] = rhs_ref[...]
    stride = 1
    while stride < count:
        centre = slice(pad, pad + count)
        before = slice(pad - stride, pad - stride + count)
        after = slice(pad + stride, pad + stride + count)
        a, b, c, d = a_s[centre, :], b_s[centre, :], c_s[centre, :], d_s[centre, :]
        ratio_back = -a / b_s[before, :]
        ratio_ahead = -c / b_s[after, :]
        new_b = b + ratio_back * c_s[before, :] + ratio_ahead * a_s[after, :]
        new_d = d + ratio_back * d_s[before, :] + ratio_ahead * d_s[after, :]
        new_a = ratio_back * a_s[before, :]
        new_c = ratio_ahead * c_s[after, :]
        a_s[centre, :] = new_a
        b_s[centre, :] = new_b
        c_s[centre, :] = new_c
        d_s[centre, :] = new_d
        stride *= 2
    out_ref[...] = d_s[pad : pad + count, :] / b_s[pad : pad + count, :]


def line_solve(lower_band, main_band, upper_band, right_side):
    count, width = right_side.shape
    scratch = pltpu.VMEM((2 * (count // 2) + count, width), jnp.float32)
    return pl.pallas_call(
        cyclic_kernel,
        out_shape=jax.ShapeDtypeStruct((count, width), jnp.float32),
        scratch_shapes=[scratch] * 4,
    )(lower_band, main_band, upper_band, right_side)


def gather_kernel(blocks, ends_ref, out_ref, landed, send_sem, recv_sem):
    me = lax.axis_index("var")
    spot = lax.axis_index("spot")
    barrier = pltpu.get_barrier_semaphore()
    for shift in range(1, blocks):
        peer = lax.rem(me + shift, blocks)
        pl.semaphore_signal(barrier, inc=1, device_id=(spot, peer), device_id_type=pl.DeviceIdType.MESH)
    pl.semaphore_wait(barrier, blocks - 1)
    copies = []
    for shift in range(1, blocks):
        peer = lax.rem(me + shift, blocks)
        copy = pltpu.make_async_remote_copy(
            src_ref=ends_ref,
            dst_ref=landed.at[shift - 1],
            send_sem=send_sem.at[shift - 1],
            recv_sem=recv_sem.at[shift - 1],
            device_id=(spot, peer),
            device_id_type=pl.DeviceIdType.MESH,
        )
        copy.start()
        copies.append(copy)
    out_ref[0] = ends_ref[...]
    for copy in copies:
        copy.wait()
    for shift in range(1, blocks):
        out_ref[shift] = landed[shift - 1]


def gather_var(ends, blocks):
    return pl.pallas_call(
        functools.partial(gather_kernel, blocks),
        out_shape=jax.ShapeDtypeStruct((blocks,) + ends.shape, jnp.float32),
        scratch_shapes=[
            pltpu.VMEM((blocks - 1,) + ends.shape, jnp.float32),
            pltpu.SemaphoreType.DMA((blocks - 1,)),
            pltpu.SemaphoreType.DMA((blocks - 1,)),
        ],
        compiler_params=pltpu.CompilerParams(collective_id=0, has_side_effects=True),
    )(ends)


def exchange_kernel(count, chunks_ref, out_ref, landed, send_sem, recv_sem):
    me = lax.axis_index("spot")
    var = lax.axis_index("var")

    def send(step, carry):
        peer = lax.rem(me + step, count)
        pltpu.make_async_remote_copy(
            src_ref=chunks_ref.at[peer],
            dst_ref=landed.at[me],
            send_sem=send_sem,
            recv_sem=recv_sem,
            device_id=(peer, var),
            device_id_type=pl.DeviceIdType.MESH,
        ).start()
        return carry

    lax.fori_loop(1, count, send, 0)
    landed[me] = chunks_ref[me]
    every = pltpu.make_async_remote_copy(
        src_ref=chunks_ref.at[pl.ds(0, count - 1)],
        dst_ref=landed.at[pl.ds(0, count - 1)],
        send_sem=send_sem,
        recv_sem=recv_sem,
        device_id=(me, var),
        device_id_type=pl.DeviceIdType.MESH,
    )
    every.wait_send()
    every.wait_recv()
    out_ref[...] = landed[...]


def exchange_spot(chunks):
    count = chunks.shape[0]
    return pl.pallas_call(
        functools.partial(exchange_kernel, count),
        out_shape=jax.ShapeDtypeStruct(chunks.shape, jnp.float32),
        scratch_shapes=[
            pltpu.VMEM(chunks.shape, jnp.float32),
            pltpu.SemaphoreType.DMA(()),
            pltpu.SemaphoreType.DMA(()),
        ],
        compiler_params=pltpu.CompilerParams(has_side_effects=True),
    )(chunks)


def implicit(system, right_side, dimension):
    behind, centre, ahead = system
    lower_band = jnp.broadcast_to(-solve_scale * behind, right_side.shape)
    main_band = jnp.broadcast_to(1.0 - solve_scale * centre, right_side.shape)
    upper_band = jnp.broadcast_to(-solve_scale * ahead, right_side.shape)
    return reduce_solve(lower_band, main_band, upper_band, right_side, dimension)


def shards(option_value, spot_nodes, var_nodes, rate_nodes):
    spot_rows, planes, var_cols = option_value.shape
    line_count = planes * var_cols
    spot_place = lax.axis_index("spot")
    var_place = lax.axis_index("var")
    spot_coords = coordinates(spot_nodes, spot_low, spot_high)
    var_coords = coordinates(var_nodes, var_low, var_high)
    rate_coords = coordinates(rate_nodes, rate_low, rate_high)
    spot_geo = geometry(spot_coords, 0, 3, spot_place * spot_rows, spot_rows)
    var_geo = geometry(var_coords, 2, 3, var_place * var_cols, var_cols)
    rate_geo = geometry(rate_coords, 1, 3, 0, planes)
    spot_whole = geometry(spot_coords, 0, 2, 0, spot_nodes.shape[0])
    var_whole = geometry(var_coords, 1, 2, 0, var_nodes.shape[0])
    rate_plain = rate_geo[0].reshape(planes)
    var_plain = var_geo[0].reshape(var_cols)

    def edge_terms(values, mixing_only):
        padded = padded_2(values, (("spot", 0), ("var", 2)), 1)
        padded = jnp.pad(padded, ((0, 0), (1, 1), (0, 0)))
        return explicit_terms(padded, spot_geo, var_geo, rate_geo, mixing_only)

    def spot_solve(values):
        devices = lax.axis_size("spot")
        per_device = line_count // devices
        chunks = values.reshape(spot_rows, devices, per_device).transpose(1, 0, 2)
        gathered = exchange_spot(chunks).reshape(devices * spot_rows, per_device)
        first_line = spot_place * per_device
        rate_flat = jnp.broadcast_to(rate_plain.reshape(planes, 1), (planes, var_cols)).reshape(
            line_count
        )
        var_flat = jnp.broadcast_to(var_plain.reshape(1, var_cols), (planes, var_cols)).reshape(
            line_count
        )
        rate_line = lax.dynamic_slice_in_dim(rate_flat, first_line, per_device).reshape(
            1, per_device
        )
        var_line = lax.dynamic_slice_in_dim(var_flat, first_line, per_device).reshape(1, per_device)
        diffusion, advection = spot_terms(spot_whole[0], var_line, rate_line)
        system = line_coefficients(
            diffusion, advection, rate_line / 3.0, spot_whole[1], spot_whole[2]
        )
        solved = implicit(system, gathered, 0)
        returned = exchange_spot(solved.reshape(devices, spot_rows, per_device))
        return returned.transpose(1, 0, 2).reshape(spot_rows, planes, var_cols)

    var_count = var_nodes.shape[0]
    blocks = var_count // var_cols
    var_vec = var_coords[1:-1]
    var_first, var_second = stencil_weights(var_coords)
    var_diffusion, var_advection = var_terms(var_vec)
    var_behind = var_diffusion * var_second[0] + var_advection * var_first[0]
    var_middle = var_diffusion * var_second[1] + var_advection * var_first[1]
    var_ahead = var_diffusion * var_second[2] + var_advection * var_first[2]
    reaction_plain = rate_plain / 3.0
    var_lower = (-solve_scale * var_behind).reshape(blocks, var_cols)
    var_upper = (-solve_scale * var_ahead).reshape(blocks, var_cols)
    var_main = (
        1.0 - solve_scale * (var_middle.reshape(var_count, 1) - reaction_plain.reshape(1, planes))
    ).reshape(blocks, var_cols, planes)

    column_shape = (var_cols, blocks, 2, planes)
    lower_cols = jnp.broadcast_to(var_lower.T.reshape(var_cols, blocks, 1, 1), column_shape)
    upper_cols = jnp.broadcast_to(var_upper.T.reshape(var_cols, blocks, 1, 1), column_shape)
    main_cols = jnp.broadcast_to(
        var_main.transpose(1, 0, 2).reshape(var_cols, blocks, 1, planes), column_shape
    )
    position = lax.broadcasted_iota(jnp.int32, column_shape, 0)
    kind = lax.broadcasted_iota(jnp.int32, column_shape, 2)
    coupling = jnp.where(
        (kind == 0) & (position == 0),
        var_lower[:, 0].reshape(1, blocks, 1, 1),
        jnp.where(
            (kind == 1) & (position == var_cols - 1),
            var_upper[:, var_cols - 1].reshape(1, blocks, 1, 1),
            0.0,
        ),
    )
    flat = (var_cols, blocks * 2 * planes)
    columns = line_solve(
        lower_cols.reshape(flat),
        main_cols.reshape(flat),
        upper_cols.reshape(flat),
        coupling.reshape(flat),
    ).reshape(column_shape)
    g_first, g_last = columns[0, :, 0, :], columns[var_cols - 1, :, 0, :]
    h_first, h_last = columns[0, :, 1, :], columns[var_cols - 1, :, 1, :]
    g_own = lax.dynamic_index_in_dim(columns[:, :, 0, :], var_place, 1, keepdims=False)
    h_own = lax.dynamic_index_in_dim(columns[:, :, 1, :], var_place, 1, keepdims=False)
    lower_own = lax.dynamic_index_in_dim(var_lower, var_place, 0, keepdims=False)
    upper_own = lax.dynamic_index_in_dim(var_upper, var_place, 0, keepdims=False)
    main_own = lax.dynamic_index_in_dim(var_main, var_place, 0, keepdims=False)

    def interface_solve(y_first, y_last):
        size = 2 * (blocks - 1)
        matrix = [[None] * size for _ in range(size)]
        rhs = [None] * size
        for b in range(blocks - 1):
            matrix[2 * b][2 * b] = 1.0
            if b >= 1:
                matrix[2 * b][2 * b - 2] = g_last[b]
            matrix[2 * b][2 * b + 1] = h_last[b]
            rhs[2 * b] = y_last[b]
            matrix[2 * b + 1][2 * b + 1] = 1.0
            matrix[2 * b + 1][2 * b] = g_first[b + 1]
            if b + 2 <= blocks - 1:
                matrix[2 * b + 1][2 * b + 3] = h_first[b + 1]
            rhs[2 * b + 1] = y_first[b + 1]
        for k in range(size):
            for i in range(k + 1, size):
                if matrix[i][k] is None:
                    continue
                factor = matrix[i][k] / matrix[k][k]
                for c in range(k + 1, size):
                    if matrix[k][c] is None:
                        continue
                    update = factor * matrix[k][c]
                    matrix[i][c] = -update if matrix[i][c] is None else matrix[i][c] - update
                rhs[i] = rhs[i] - factor * rhs[k]
                matrix[i][k] = None
        solved = [None] * size
        for k in reversed(range(size)):
            total = rhs[k]
            for c in range(k + 1, size):
                if matrix[k][c] is not None:
                    total = total - matrix[k][c] * solved[c]
            solved[k] = total / matrix[k][k]
        zero = jnp.zeros_like(y_first[0])
        left = jnp.stack([zero] + [solved[2 * b] for b in range(blocks - 1)])
        right = jnp.stack([solved[2 * b + 1] for b in range(blocks - 1)] + [zero])
        return (
            lax.dynamic_index_in_dim(left, var_place, 0, keepdims=False),
            lax.dynamic_index_in_dim(right, var_place, 0, keepdims=False),
        )

    def gather_ends(ends):
        stacked = gather_var(ends, blocks)
        order = (var_place - jnp.arange(blocks)) % blocks
        return jnp.take(stacked, order, axis=0)

    def var_solve(values):
        line_count = spot_rows * planes
        lines = values.transpose(2, 0, 1).reshape(var_cols, line_count)
        shape = lines.shape
        local = line_solve(
            jnp.broadcast_to(lower_own.reshape(var_cols, 1), shape),
            jnp.broadcast_to(main_own.reshape(var_cols, 1, planes), (var_cols, spot_rows, planes)).reshape(shape),
            jnp.broadcast_to(upper_own.reshape(var_cols, 1), shape),
            lines,
        ).reshape(var_cols, spot_rows, planes)
        ends = gather_ends(jnp.stack([local[0], local[var_cols - 1]]))
        left, right = interface_solve(ends[:, 0], ends[:, 1])
        solved = (
            local
            - left.reshape(1, spot_rows, planes) * g_own.reshape(var_cols, 1, planes)
            - right.reshape(1, spot_rows, planes) * h_own.reshape(var_cols, 1, planes)
        )
        return solved.transpose(1, 2, 0)

    def rate_solve(values):
        diffusion, advection = rate_terms(rate_geo[0])
        system = line_coefficients(
            diffusion, advection, rate_geo[0] / 3.0, rate_geo[1], rate_geo[2]
        )
        return implicit(system, values, 1)

    z_zero = time_step * edge_terms(option_value, False)
    z_one = spot_solve(z_zero)
    z_two = var_solve(z_one)
    z_three = rate_solve(z_two)
    w_zero = z_zero + half_step * edge_terms(z_three, True)
    w_one = spot_solve(w_zero)
    w_two = var_solve(w_one)
    w_three = rate_solve(w_two)
    return option_value + w_three


def solution(mesh):
    in_specs = (P("spot", None, "var"), P(), P(), P())
    out_specs = P("spot", None, "var")
    return jax.shard_map(shards, mesh=mesh, in_specs=in_specs, out_specs=out_specs, check_vma=False)
```

```python
import functools

import jax
import jax.numpy as jnp
from jax import lax
from jax.experimental import pallas as pl
from jax.experimental.pallas import tpu as pltpu
from jax.sharding import PartitionSpec as P

time_step = 0.01
solve_scale = 0.5 * time_step
half_step = 0.5 * time_step
spot_low = 0.5
spot_high = 2.5
var_low = 0.02
var_high = 1.0
rate_low = -0.1
rate_high = 0.2
dividend_yield = 0.02
reversion_var = 2.0
long_var = 0.04
vol_var = 0.6
reversion_rate = 0.1
long_rate = 0.05
vol_rate = 0.1
coupling_sv = -0.7 * vol_var
coupling_sr = 0.2 * vol_rate
coupling_vr = 0.1 * vol_var * vol_rate


def padded_2(array, sides, width):
    for axis, dim in sides:
        devices, length = (lax.axis_size(axis), array.shape[dim])
        up = [(i, (i + 1) % devices) for i in range(devices - 1)]
        down = [(j, i) for i, j in up]
        last = lax.slice_in_dim(array, length - width, length, axis=dim)
        initial = lax.slice_in_dim(array, 0, width, axis=dim)
        before = lax.ppermute(last, axis, up)
        after = lax.ppermute(initial, axis, down)
        array = jnp.concatenate([before, array, after], axis=dim)
    return array


def coordinates(node_list, low_end, high_end):
    length = node_list.shape[0]
    extended = jnp.concatenate(
        [jnp.full((1,), -1, jnp.int32), node_list, jnp.full((1,), 4 * length, jnp.int32)]
    )
    return low_end + (high_end - low_end) * extended.astype(jnp.float32) / (4 * length - 1)


def stencil_weights(coords):
    behind = coords[1:-1] - coords[:-2]
    ahead = coords[2:] - coords[1:-1]
    spread = behind + ahead
    first_diff = (
        -ahead / (behind * spread),
        (ahead - behind) / (behind * ahead),
        behind / (ahead * spread),
    )
    second_diff = (2.0 / (behind * spread), -2.0 / (behind * ahead), 2.0 / (ahead * spread))
    return (first_diff, second_diff)


def geometry(coords, position, dim_count, offset, length):
    first_diff, second_diff = stencil_weights(coords)
    vectors = (coords[1:-1],) + first_diff + second_diff
    target = [1] * dim_count
    target[position] = length
    pieces = [
        lax.dynamic_slice_in_dim(vector, offset, length).reshape(target) for vector in vectors
    ]
    return (pieces[0], tuple(pieces[1:4]), tuple(pieces[4:7]))


def spot_terms(spot_x, var_x, rate_x):
    return (0.5 * spot_x * spot_x * var_x, (rate_x - dividend_yield) * spot_x)


def var_terms(var_x):
    return (0.5 * vol_var * vol_var * var_x, reversion_var * (long_var - var_x))


def rate_terms(rate_x):
    return (0.5 * vol_rate * vol_rate, reversion_rate * (long_rate - rate_x))


def line_coefficients(diffusion, advection, reaction, first_diff, second_diff):
    behind = diffusion * second_diff[0] + advection * first_diff[0]
    centre = diffusion * second_diff[1] + advection * first_diff[1] - reaction
    ahead = diffusion * second_diff[2] + advection * first_diff[2]
    return (behind, centre, ahead)


def explicit_terms(padded, spot_geo, var_geo, rate_geo, mixing_only):
    spot_x, spot_first, spot_second = spot_geo
    var_x, var_first, var_second = var_geo
    rate_x, rate_first, rate_second = rate_geo
    spot_rows = padded.shape[0] - 2
    planes = padded.shape[1] - 2
    var_cols = padded.shape[2] - 2
    middle = padded[1:-1, 1:-1, 1:-1]
    cross_sv = 0.0
    cross_sr = 0.0
    cross_vr = 0.0
    for outer_step in range(3):
        for inner_step in range(3):
            cross_sv = (
                cross_sv
                + spot_first[outer_step]
                * var_first[inner_step]
                * padded[
                    outer_step : outer_step + spot_rows, 1:-1, inner_step : inner_step + var_cols
                ]
            )
            cross_sr = (
                cross_sr
                + spot_first[outer_step]
                * rate_first[inner_step]
                * padded[
                    outer_step : outer_step + spot_rows, inner_step : inner_step + planes, 1:-1
                ]
            )
            cross_vr = (
                cross_vr
                + var_first[outer_step]
                * rate_first[inner_step]
                * padded[1:-1, inner_step : inner_step + planes, outer_step : outer_step + var_cols]
            )
    root_var = jnp.sqrt(var_x)
    mixing = (
        coupling_sv * spot_x * var_x * cross_sv
        + coupling_sr * spot_x * root_var * cross_sr
        + coupling_vr * root_var * cross_vr
    )
    if mixing_only:
        return mixing
    reaction = rate_x / 3.0
    diffusion, advection = spot_terms(spot_x, var_x, rate_x)
    behind, centre, ahead = line_coefficients(
        diffusion, advection, reaction, spot_first, spot_second
    )
    along_spot = behind * padded[:-2, 1:-1, 1:-1] + centre * middle + ahead * padded[2:, 1:-1, 1:-1]
    diffusion, advection = var_terms(var_x)
    behind, centre, ahead = line_coefficients(diffusion, advection, reaction, var_first, var_second)
    along_var = behind * padded[1:-1, 1:-1, :-2] + centre * middle + ahead * padded[1:-1, 1:-1, 2:]
    diffusion, advection = rate_terms(rate_x)
    behind, centre, ahead = line_coefficients(
        diffusion, advection, reaction, rate_first, rate_second
    )
    along_rate = behind * padded[1:-1, :-2, 1:-1] + centre * middle + ahead * padded[1:-1, 2:, 1:-1]
    return mixing + along_spot + along_var + along_rate


def reduce_solve(lower_band, main_band, upper_band, right_side, dimension):
    length = right_side.shape[dimension]
    if length == 1:
        return right_side / main_band

    def even_rows(source):
        return lax.slice_in_dim(source, 0, length, 2, dimension)

    def odd_rows(source):
        return lax.slice_in_dim(source, 1, length, 2, dimension)

    def onward(source, filler):
        remainder = lax.slice_in_dim(source, 1, source.shape[dimension], axis=dimension)
        return jnp.concatenate(
            [remainder, jnp.zeros_like(lax.slice_in_dim(source, 0, 1, axis=dimension)) + filler],
            axis=dimension,
        )

    lower_even, main_even, upper_even, right_even = [
        even_rows(source) for source in (lower_band, main_band, upper_band, right_side)
    ]
    lower_odd, main_odd, upper_odd, right_odd = [
        odd_rows(source) for source in (lower_band, main_band, upper_band, right_side)
    ]
    lower_next = onward(lower_even, 0.0)
    main_next = onward(main_even, 1.0)
    upper_next = onward(upper_even, 0.0)
    right_next = onward(right_even, 0.0)
    ratio_back = -lower_odd / main_even
    ratio_ahead = -upper_odd / main_next
    solved_odd = reduce_solve(
        ratio_back * lower_even,
        main_odd + ratio_back * upper_even + ratio_ahead * lower_next,
        ratio_ahead * upper_next,
        right_odd + ratio_back * right_even + ratio_ahead * right_next,
        dimension,
    )
    remainder = lax.slice_in_dim(solved_odd, 0, solved_odd.shape[dimension] - 1, axis=dimension)
    solved_even = (
        right_even
        - lower_even
        * jnp.concatenate(
            [jnp.zeros_like(lax.slice_in_dim(solved_odd, 0, 1, axis=dimension)), remainder],
            axis=dimension,
        )
        - upper_even * solved_odd
    ) / main_even
    joined = jnp.stack([solved_even, solved_odd], axis=dimension + 1)
    return joined.reshape(right_side.shape)


def cyclic_kernel(lower_ref, main_ref, upper_ref, rhs_ref, out_ref, a_s, b_s, c_s, d_s):
    count, width = rhs_ref.shape
    pad = count // 2
    for ref, fill in ((a_s, 0.0), (b_s, 1.0), (c_s, 0.0), (d_s, 0.0)):
        ref[0:pad, :] = jnp.full((pad, width), fill, jnp.float32)
        ref[pad + count : 2 * pad + count, :] = jnp.full((pad, width), fill, jnp.float32)
    row = lax.broadcasted_iota(jnp.int32, (count, width), 0)
    a_s[pad : pad + count, :] = jnp.where(row == 0, 0.0, lower_ref[...])
    b_s[pad : pad + count, :] = main_ref[...]
    c_s[pad : pad + count, :] = jnp.where(row == count - 1, 0.0, upper_ref[...])
    d_s[pad : pad + count, :] = rhs_ref[...]
    stride = 1
    while stride < count:
        centre = slice(pad, pad + count)
        before = slice(pad - stride, pad - stride + count)
        after = slice(pad + stride, pad + stride + count)
        a, b, c, d = a_s[centre, :], b_s[centre, :], c_s[centre, :], d_s[centre, :]
        ratio_back = -a / b_s[before, :]
        ratio_ahead = -c / b_s[after, :]
        new_b = b + ratio_back * c_s[before, :] + ratio_ahead * a_s[after, :]
        new_d = d + ratio_back * d_s[before, :] + ratio_ahead * d_s[after, :]
        new_a = ratio_back * a_s[before, :]
        new_c = ratio_ahead * c_s[after, :]
        a_s[centre, :] = new_a
        b_s[centre, :] = new_b
        c_s[centre, :] = new_c
        d_s[centre, :] = new_d
        stride *= 2
    out_ref[...] = d_s[pad : pad + count, :] / b_s[pad : pad + count, :]


def line_solve(lower_band, main_band, upper_band, right_side):
    count, width = right_side.shape
    scratch = pltpu.VMEM((2 * (count // 2) + count, width), jnp.float32)
    return pl.pallas_call(
        cyclic_kernel,
        out_shape=jax.ShapeDtypeStruct((count, width), jnp.float32),
        scratch_shapes=[scratch] * 4,
    )(lower_band, main_band, upper_band, right_side)


def gather_kernel(blocks, ends_ref, out_ref, landed, send_sem, recv_sem):
    me = lax.axis_index("var")
    spot = lax.axis_index("spot")
    barrier = pltpu.get_barrier_semaphore()
    for shift in range(1, blocks):
        peer = lax.rem(me + shift, blocks)
        pl.semaphore_signal(barrier, inc=1, device_id=(spot, peer), device_id_type=pl.DeviceIdType.MESH)
    pl.semaphore_wait(barrier, blocks - 1)
    copies = []
    for shift in range(1, blocks):
        peer = lax.rem(me + shift, blocks)
        copy = pltpu.make_async_remote_copy(
            src_ref=ends_ref,
            dst_ref=landed.at[shift - 1],
            send_sem=send_sem.at[shift - 1],
            recv_sem=recv_sem.at[shift - 1],
            device_id=(spot, peer),
            device_id_type=pl.DeviceIdType.MESH,
        )
        copy.start()
        copies.append(copy)
    out_ref[0] = ends_ref[...]
    for copy in copies:
        copy.wait()
    for shift in range(1, blocks):
        out_ref[shift] = landed[shift - 1]


def gather_var(ends, blocks):
    return pl.pallas_call(
        functools.partial(gather_kernel, blocks),
        out_shape=jax.ShapeDtypeStruct((blocks,) + ends.shape, jnp.float32),
        scratch_shapes=[
            pltpu.VMEM((blocks - 1,) + ends.shape, jnp.float32),
            pltpu.SemaphoreType.DMA((blocks - 1,)),
            pltpu.SemaphoreType.DMA((blocks - 1,)),
        ],
        compiler_params=pltpu.CompilerParams(collective_id=0, has_side_effects=True),
    )(ends)


def implicit(system, right_side, dimension):
    behind, centre, ahead = system
    lower_band = jnp.broadcast_to(-solve_scale * behind, right_side.shape)
    main_band = jnp.broadcast_to(1.0 - solve_scale * centre, right_side.shape)
    upper_band = jnp.broadcast_to(-solve_scale * ahead, right_side.shape)
    return reduce_solve(lower_band, main_band, upper_band, right_side, dimension)


def shards(option_value, spot_nodes, var_nodes, rate_nodes):
    spot_rows, planes, var_cols = option_value.shape
    line_count = planes * var_cols
    spot_place = lax.axis_index("spot")
    var_place = lax.axis_index("var")
    spot_coords = coordinates(spot_nodes, spot_low, spot_high)
    var_coords = coordinates(var_nodes, var_low, var_high)
    rate_coords = coordinates(rate_nodes, rate_low, rate_high)
    spot_geo = geometry(spot_coords, 0, 3, spot_place * spot_rows, spot_rows)
    var_geo = geometry(var_coords, 2, 3, var_place * var_cols, var_cols)
    rate_geo = geometry(rate_coords, 1, 3, 0, planes)
    spot_whole = geometry(spot_coords, 0, 2, 0, spot_nodes.shape[0])
    var_whole = geometry(var_coords, 1, 2, 0, var_nodes.shape[0])
    rate_plain = rate_geo[0].reshape(planes)
    var_plain = var_geo[0].reshape(var_cols)

    def edge_terms(values, mixing_only):
        padded = padded_2(values, (("spot", 0), ("var", 2)), 1)
        padded = jnp.pad(padded, ((0, 0), (1, 1), (0, 0)))
        return explicit_terms(padded, spot_geo, var_geo, rate_geo, mixing_only)

    def spot_solve(values):
        gathered = lax.all_to_all(
            values.reshape(spot_rows, line_count), "spot", split_axis=1, concat_axis=0, tiled=True
        )
        per_device = gathered.shape[1]
        first_line = spot_place * per_device
        rate_flat = jnp.broadcast_to(rate_plain.reshape(planes, 1), (planes, var_cols)).reshape(
            line_count
        )
        var_flat = jnp.broadcast_to(var_plain.reshape(1, var_cols), (planes, var_cols)).reshape(
            line_count
        )
        rate_line = lax.dynamic_slice_in_dim(rate_flat, first_line, per_device).reshape(
            1, per_device
        )
        var_line = lax.dynamic_slice_in_dim(var_flat, first_line, per_device).reshape(1, per_device)
        diffusion, advection = spot_terms(spot_whole[0], var_line, rate_line)
        system = line_coefficients(
            diffusion, advection, rate_line / 3.0, spot_whole[1], spot_whole[2]
        )
        solved = implicit(system, gathered, 0)
        return lax.all_to_all(solved, "spot", split_axis=0, concat_axis=1, tiled=True).reshape(
            spot_rows, planes, var_cols
        )

    var_count = var_nodes.shape[0]
    blocks = var_count // var_cols
    var_vec = var_coords[1:-1]
    var_first, var_second = stencil_weights(var_coords)
    var_diffusion, var_advection = var_terms(var_vec)
    var_behind = var_diffusion * var_second[0] + var_advection * var_first[0]
    var_middle = var_diffusion * var_second[1] + var_advection * var_first[1]
    var_ahead = var_diffusion * var_second[2] + var_advection * var_first[2]
    reaction_plain = rate_plain / 3.0
    var_lower = (-solve_scale * var_behind).reshape(blocks, var_cols)
    var_upper = (-solve_scale * var_ahead).reshape(blocks, var_cols)
    var_main = (
        1.0 - solve_scale * (var_middle.reshape(var_count, 1) - reaction_plain.reshape(1, planes))
    ).reshape(blocks, var_cols, planes)

    lower_own = lax.dynamic_index_in_dim(var_lower, var_place, 0, keepdims=False)
    upper_own = lax.dynamic_index_in_dim(var_upper, var_place, 0, keepdims=False)
    main_own = lax.dynamic_index_in_dim(var_main, var_place, 0, keepdims=False)
    column_shape = (var_cols, 2, planes)
    position = lax.broadcasted_iota(jnp.int32, column_shape, 0)
    kind = lax.broadcasted_iota(jnp.int32, column_shape, 1)
    coupling = jnp.where(
        (kind == 0) & (position == 0),
        lower_own[0],
        jnp.where((kind == 1) & (position == var_cols - 1), upper_own[var_cols - 1], 0.0),
    )
    flat = (var_cols, 2 * planes)
    columns = line_solve(
        jnp.broadcast_to(lower_own.reshape(var_cols, 1), flat),
        jnp.broadcast_to(main_own.reshape(var_cols, 1, planes), column_shape).reshape(flat),
        jnp.broadcast_to(upper_own.reshape(var_cols, 1), flat),
        coupling.reshape(flat),
    ).reshape(column_shape)
    g_own, h_own = columns[:, 0, :], columns[:, 1, :]
    column_ends = jnp.stack([g_own[0], g_own[var_cols - 1], h_own[0], h_own[var_cols - 1]])
    def interface_solve(y_first, y_last, g_first, g_last, h_first, h_last):
        size = 2 * (blocks - 1)
        matrix = [[None] * size for _ in range(size)]
        rhs = [None] * size
        for b in range(blocks - 1):
            matrix[2 * b][2 * b] = 1.0
            if b >= 1:
                matrix[2 * b][2 * b - 2] = g_last[b]
            matrix[2 * b][2 * b + 1] = h_last[b]
            rhs[2 * b] = y_last[b]
            matrix[2 * b + 1][2 * b + 1] = 1.0
            matrix[2 * b + 1][2 * b] = g_first[b + 1]
            if b + 2 <= blocks - 1:
                matrix[2 * b + 1][2 * b + 3] = h_first[b + 1]
            rhs[2 * b + 1] = y_first[b + 1]
        for k in range(size):
            for i in range(k + 1, size):
                if matrix[i][k] is None:
                    continue
                factor = matrix[i][k] / matrix[k][k]
                for c in range(k + 1, size):
                    if matrix[k][c] is None:
                        continue
                    update = factor * matrix[k][c]
                    matrix[i][c] = -update if matrix[i][c] is None else matrix[i][c] - update
                rhs[i] = rhs[i] - factor * rhs[k]
                matrix[i][k] = None
        solved = [None] * size
        for k in reversed(range(size)):
            total = rhs[k]
            for c in range(k + 1, size):
                if matrix[k][c] is not None:
                    total = total - matrix[k][c] * solved[c]
            solved[k] = total / matrix[k][k]
        zero = jnp.zeros_like(y_first[0])
        left = jnp.stack([zero] + [solved[2 * b] for b in range(blocks - 1)])
        right = jnp.stack([solved[2 * b + 1] for b in range(blocks - 1)] + [zero])
        return (
            lax.dynamic_index_in_dim(left, var_place, 0, keepdims=False),
            lax.dynamic_index_in_dim(right, var_place, 0, keepdims=False),
        )

    def gather_ends(ends):
        stacked = gather_var(ends, blocks)
        order = (var_place - jnp.arange(blocks)) % blocks
        return jnp.take(stacked, order, axis=0)

    def var_solve(values):
        line_count = spot_rows * planes
        lines = values.transpose(2, 0, 1).reshape(var_cols, line_count)
        shape = lines.shape
        local = line_solve(
            jnp.broadcast_to(lower_own.reshape(var_cols, 1), shape),
            jnp.broadcast_to(main_own.reshape(var_cols, 1, planes), (var_cols, spot_rows, planes)).reshape(shape),
            jnp.broadcast_to(upper_own.reshape(var_cols, 1), shape),
            lines,
        ).reshape(var_cols, spot_rows, planes)
        message = jnp.concatenate(
            [local[0], local[var_cols - 1], column_ends], axis=0
        )
        ends = gather_ends(message)
        left, right = interface_solve(
            ends[:, :spot_rows],
            ends[:, spot_rows : 2 * spot_rows],
            ends[:, 2 * spot_rows],
            ends[:, 2 * spot_rows + 1],
            ends[:, 2 * spot_rows + 2],
            ends[:, 2 * spot_rows + 3],
        )
        solved = (
            local
            - left.reshape(1, spot_rows, planes) * g_own.reshape(var_cols, 1, planes)
            - right.reshape(1, spot_rows, planes) * h_own.reshape(var_cols, 1, planes)
        )
        return solved.transpose(1, 2, 0)

    def rate_solve(values):
        diffusion, advection = rate_terms(rate_geo[0])
        system = line_coefficients(
            diffusion, advection, rate_geo[0] / 3.0, rate_geo[1], rate_geo[2]
        )
        return implicit(system, values, 1)

    z_zero = time_step * edge_terms(option_value, False)
    z_one = spot_solve(z_zero)
    z_two = var_solve(z_one)
    z_three = rate_solve(z_two)
    w_zero = z_zero + half_step * edge_terms(z_three, True)
    w_one = spot_solve(w_zero)
    w_two = var_solve(w_one)
    w_three = rate_solve(w_two)
    return option_value + w_three


def solution(mesh):
    in_specs = (P("spot", None, "var"), P(), P(), P())
    out_specs = P("spot", None, "var")
    return jax.shard_map(shards, mesh=mesh, in_specs=in_specs, out_specs=out_specs, check_vma=False)
```

```python
import functools

import jax
import jax.numpy as jnp
from jax import lax
from jax.experimental import pallas as pl
from jax.experimental.pallas import tpu as pltpu
from jax.sharding import PartitionSpec as P

time_step = 0.01
solve_scale = 0.5 * time_step
half_step = 0.5 * time_step
spot_low = 0.5
spot_high = 2.5
var_low = 0.02
var_high = 1.0
rate_low = -0.1
rate_high = 0.2
dividend_yield = 0.02
reversion_var = 2.0
long_var = 0.04
vol_var = 0.6
reversion_rate = 0.1
long_rate = 0.05
vol_rate = 0.1
coupling_sv = -0.7 * vol_var
coupling_sr = 0.2 * vol_rate
coupling_vr = 0.1 * vol_var * vol_rate


def shift_both(piece, spot_step, var_step):
    spots, vars_ = lax.axis_size("spot"), lax.axis_size("var")
    pairs = []
    for s in range(spots):
        for v in range(vars_):
            ts, tv = s + spot_step, v + var_step
            if 0 <= ts < spots and 0 <= tv < vars_:
                pairs.append((s * vars_ + v, ts * vars_ + tv))
    return lax.ppermute(piece, ("spot", "var"), pairs)


def padded_2(array):
    rows, cols = array.shape[0], array.shape[2]
    first_row, last_row = array[0:1], array[rows - 1 : rows]
    first_col, last_col = array[:, :, 0:1], array[:, :, cols - 1 : cols]
    above = shift_both(last_row, 1, 0)
    below = shift_both(first_row, -1, 0)
    left = shift_both(last_col, 0, 1)
    right = shift_both(first_col, 0, -1)
    corner_above_left = shift_both(last_row[:, :, cols - 1 : cols], 1, 1)
    corner_above_right = shift_both(last_row[:, :, 0:1], 1, -1)
    corner_below_left = shift_both(first_row[:, :, cols - 1 : cols], -1, 1)
    corner_below_right = shift_both(first_row[:, :, 0:1], -1, -1)
    top = jnp.concatenate([corner_above_left, above, corner_above_right], axis=2)
    middle = jnp.concatenate([left, array, right], axis=2)
    bottom = jnp.concatenate([corner_below_left, below, corner_below_right], axis=2)
    return jnp.concatenate([top, middle, bottom], axis=0)


def coordinates(node_list, low_end, high_end):
    length = node_list.shape[0]
    extended = jnp.concatenate(
        [jnp.full((1,), -1, jnp.int32), node_list, jnp.full((1,), 4 * length, jnp.int32)]
    )
    return low_end + (high_end - low_end) * extended.astype(jnp.float32) / (4 * length - 1)


def stencil_weights(coords):
    behind = coords[1:-1] - coords[:-2]
    ahead = coords[2:] - coords[1:-1]
    spread = behind + ahead
    first_diff = (
        -ahead / (behind * spread),
        (ahead - behind) / (behind * ahead),
        behind / (ahead * spread),
    )
    second_diff = (2.0 / (behind * spread), -2.0 / (behind * ahead), 2.0 / (ahead * spread))
    return (first_diff, second_diff)


def geometry(coords, position, dim_count, offset, length):
    first_diff, second_diff = stencil_weights(coords)
    vectors = (coords[1:-1],) + first_diff + second_diff
    target = [1] * dim_count
    target[position] = length
    pieces = [
        lax.dynamic_slice_in_dim(vector, offset, length).reshape(target) for vector in vectors
    ]
    return (pieces[0], tuple(pieces[1:4]), tuple(pieces[4:7]))


def spot_terms(spot_x, var_x, rate_x):
    return (0.5 * spot_x * spot_x * var_x, (rate_x - dividend_yield) * spot_x)


def var_terms(var_x):
    return (0.5 * vol_var * vol_var * var_x, reversion_var * (long_var - var_x))


def rate_terms(rate_x):
    return (0.5 * vol_rate * vol_rate, reversion_rate * (long_rate - rate_x))


def line_coefficients(diffusion, advection, reaction, first_diff, second_diff):
    behind = diffusion * second_diff[0] + advection * first_diff[0]
    centre = diffusion * second_diff[1] + advection * first_diff[1] - reaction
    ahead = diffusion * second_diff[2] + advection * first_diff[2]
    return (behind, centre, ahead)


def explicit_terms(padded, spot_geo, var_geo, rate_geo, mixing_only):
    spot_x, spot_first, spot_second = spot_geo
    var_x, var_first, var_second = var_geo
    rate_x, rate_first, rate_second = rate_geo
    spot_rows = padded.shape[0] - 2
    planes = padded.shape[1] - 2
    var_cols = padded.shape[2] - 2
    middle = padded[1:-1, 1:-1, 1:-1]
    cross_sv = 0.0
    cross_sr = 0.0
    cross_vr = 0.0
    for outer_step in range(3):
        for inner_step in range(3):
            cross_sv = (
                cross_sv
                + spot_first[outer_step]
                * var_first[inner_step]
                * padded[
                    outer_step : outer_step + spot_rows, 1:-1, inner_step : inner_step + var_cols
                ]
            )
            cross_sr = (
                cross_sr
                + spot_first[outer_step]
                * rate_first[inner_step]
                * padded[
                    outer_step : outer_step + spot_rows, inner_step : inner_step + planes, 1:-1
                ]
            )
            cross_vr = (
                cross_vr
                + var_first[outer_step]
                * rate_first[inner_step]
                * padded[1:-1, inner_step : inner_step + planes, outer_step : outer_step + var_cols]
            )
    root_var = jnp.sqrt(var_x)
    mixing = (
        coupling_sv * spot_x * var_x * cross_sv
        + coupling_sr * spot_x * root_var * cross_sr
        + coupling_vr * root_var * cross_vr
    )
    if mixing_only:
        return mixing
    reaction = rate_x / 3.0
    diffusion, advection = spot_terms(spot_x, var_x, rate_x)
    behind, centre, ahead = line_coefficients(
        diffusion, advection, reaction, spot_first, spot_second
    )
    along_spot = behind * padded[:-2, 1:-1, 1:-1] + centre * middle + ahead * padded[2:, 1:-1, 1:-1]
    diffusion, advection = var_terms(var_x)
    behind, centre, ahead = line_coefficients(diffusion, advection, reaction, var_first, var_second)
    along_var = behind * padded[1:-1, 1:-1, :-2] + centre * middle + ahead * padded[1:-1, 1:-1, 2:]
    diffusion, advection = rate_terms(rate_x)
    behind, centre, ahead = line_coefficients(
        diffusion, advection, reaction, rate_first, rate_second
    )
    along_rate = behind * padded[1:-1, :-2, 1:-1] + centre * middle + ahead * padded[1:-1, 2:, 1:-1]
    return mixing + along_spot + along_var + along_rate


def reduce_solve(lower_band, main_band, upper_band, right_side, dimension):
    length = right_side.shape[dimension]
    if length == 1:
        return right_side / main_band

    def even_rows(source):
        return lax.slice_in_dim(source, 0, length, 2, dimension)

    def odd_rows(source):
        return lax.slice_in_dim(source, 1, length, 2, dimension)

    def onward(source, filler):
        remainder = lax.slice_in_dim(source, 1, source.shape[dimension], axis=dimension)
        return jnp.concatenate(
            [remainder, jnp.zeros_like(lax.slice_in_dim(source, 0, 1, axis=dimension)) + filler],
            axis=dimension,
        )

    lower_even, main_even, upper_even, right_even = [
        even_rows(source) for source in (lower_band, main_band, upper_band, right_side)
    ]
    lower_odd, main_odd, upper_odd, right_odd = [
        odd_rows(source) for source in (lower_band, main_band, upper_band, right_side)
    ]
    lower_next = onward(lower_even, 0.0)
    main_next = onward(main_even, 1.0)
    upper_next = onward(upper_even, 0.0)
    right_next = onward(right_even, 0.0)
    ratio_back = -lower_odd / main_even
    ratio_ahead = -upper_odd / main_next
    solved_odd = reduce_solve(
        ratio_back * lower_even,
        main_odd + ratio_back * upper_even + ratio_ahead * lower_next,
        ratio_ahead * upper_next,
        right_odd + ratio_back * right_even + ratio_ahead * right_next,
        dimension,
    )
    remainder = lax.slice_in_dim(solved_odd, 0, solved_odd.shape[dimension] - 1, axis=dimension)
    solved_even = (
        right_even
        - lower_even
        * jnp.concatenate(
            [jnp.zeros_like(lax.slice_in_dim(solved_odd, 0, 1, axis=dimension)), remainder],
            axis=dimension,
        )
        - upper_even * solved_odd
    ) / main_even
    joined = jnp.stack([solved_even, solved_odd], axis=dimension + 1)
    return joined.reshape(right_side.shape)


def cyclic_kernel(lower_ref, main_ref, upper_ref, rhs_ref, out_ref, a_s, b_s, c_s, d_s):
    count, width = rhs_ref.shape
    pad = count // 2
    for ref, fill in ((a_s, 0.0), (b_s, 1.0), (c_s, 0.0), (d_s, 0.0)):
        ref[0:pad, :] = jnp.full((pad, width), fill, jnp.float32)
        ref[pad + count : 2 * pad + count, :] = jnp.full((pad, width), fill, jnp.float32)
    row = lax.broadcasted_iota(jnp.int32, (count, width), 0)
    a_s[pad : pad + count, :] = jnp.where(row == 0, 0.0, lower_ref[...])
    b_s[pad : pad + count, :] = main_ref[...]
    c_s[pad : pad + count, :] = jnp.where(row == count - 1, 0.0, upper_ref[...])
    d_s[pad : pad + count, :] = rhs_ref[...]
    stride = 1
    while stride < count:
        centre = slice(pad, pad + count)
        before = slice(pad - stride, pad - stride + count)
        after = slice(pad + stride, pad + stride + count)
        a, b, c, d = a_s[centre, :], b_s[centre, :], c_s[centre, :], d_s[centre, :]
        ratio_back = -a / b_s[before, :]
        ratio_ahead = -c / b_s[after, :]
        new_b = b + ratio_back * c_s[before, :] + ratio_ahead * a_s[after, :]
        new_d = d + ratio_back * d_s[before, :] + ratio_ahead * d_s[after, :]
        new_a = ratio_back * a_s[before, :]
        new_c = ratio_ahead * c_s[after, :]
        a_s[centre, :] = new_a
        b_s[centre, :] = new_b
        c_s[centre, :] = new_c
        d_s[centre, :] = new_d
        stride *= 2
    out_ref[...] = d_s[pad : pad + count, :] / b_s[pad : pad + count, :]


def line_solve(lower_band, main_band, upper_band, right_side):
    count, width = right_side.shape
    scratch = pltpu.VMEM((2 * (count // 2) + count, width), jnp.float32)
    return pl.pallas_call(
        cyclic_kernel,
        out_shape=jax.ShapeDtypeStruct((count, width), jnp.float32),
        scratch_shapes=[scratch] * 4,
    )(lower_band, main_band, upper_band, right_side)


def gather_kernel(blocks, ends_ref, out_ref, landed, send_sem, recv_sem):
    me = lax.axis_index("var")
    spot = lax.axis_index("spot")
    barrier = pltpu.get_barrier_semaphore()
    for shift in range(1, blocks):
        peer = lax.rem(me + shift, blocks)
        pl.semaphore_signal(barrier, inc=1, device_id=(spot, peer), device_id_type=pl.DeviceIdType.MESH)
    pl.semaphore_wait(barrier, blocks - 1)
    copies = []
    for shift in range(1, blocks):
        peer = lax.rem(me + shift, blocks)
        copy = pltpu.make_async_remote_copy(
            src_ref=ends_ref,
            dst_ref=landed.at[shift - 1],
            send_sem=send_sem.at[shift - 1],
            recv_sem=recv_sem.at[shift - 1],
            device_id=(spot, peer),
            device_id_type=pl.DeviceIdType.MESH,
        )
        copy.start()
        copies.append(copy)
    out_ref[0] = ends_ref[...]
    for copy in copies:
        copy.wait()
    for shift in range(1, blocks):
        out_ref[shift] = landed[shift - 1]


def gather_var(ends, blocks):
    return pl.pallas_call(
        functools.partial(gather_kernel, blocks),
        out_shape=jax.ShapeDtypeStruct((blocks,) + ends.shape, jnp.float32),
        scratch_shapes=[
            pltpu.VMEM((blocks - 1,) + ends.shape, jnp.float32),
            pltpu.SemaphoreType.DMA((blocks - 1,)),
            pltpu.SemaphoreType.DMA((blocks - 1,)),
        ],
        compiler_params=pltpu.CompilerParams(collective_id=0, has_side_effects=True),
    )(ends)


def implicit(system, right_side, dimension):
    behind, centre, ahead = system
    lower_band = jnp.broadcast_to(-solve_scale * behind, right_side.shape)
    main_band = jnp.broadcast_to(1.0 - solve_scale * centre, right_side.shape)
    upper_band = jnp.broadcast_to(-solve_scale * ahead, right_side.shape)
    return reduce_solve(lower_band, main_band, upper_band, right_side, dimension)


def shards(option_value, spot_nodes, var_nodes, rate_nodes):
    spot_rows, planes, var_cols = option_value.shape
    line_count = planes * var_cols
    spot_place = lax.axis_index("spot")
    var_place = lax.axis_index("var")
    spot_coords = coordinates(spot_nodes, spot_low, spot_high)
    var_coords = coordinates(var_nodes, var_low, var_high)
    rate_coords = coordinates(rate_nodes, rate_low, rate_high)
    spot_geo = geometry(spot_coords, 0, 3, spot_place * spot_rows, spot_rows)
    var_geo = geometry(var_coords, 2, 3, var_place * var_cols, var_cols)
    rate_geo = geometry(rate_coords, 1, 3, 0, planes)
    spot_whole = geometry(spot_coords, 0, 2, 0, spot_nodes.shape[0])
    var_whole = geometry(var_coords, 1, 2, 0, var_nodes.shape[0])
    rate_plain = rate_geo[0].reshape(planes)
    var_plain = var_geo[0].reshape(var_cols)

    def edge_terms(values, mixing_only):
        padded = padded_2(values)
        padded = jnp.pad(padded, ((0, 0), (1, 1), (0, 0)))
        return explicit_terms(padded, spot_geo, var_geo, rate_geo, mixing_only)

    def spot_solve(values):
        gathered = lax.all_to_all(
            values.reshape(spot_rows, line_count), "spot", split_axis=1, concat_axis=0, tiled=True
        )
        per_device = gathered.shape[1]
        first_line = spot_place * per_device
        rate_flat = jnp.broadcast_to(rate_plain.reshape(planes, 1), (planes, var_cols)).reshape(
            line_count
        )
        var_flat = jnp.broadcast_to(var_plain.reshape(1, var_cols), (planes, var_cols)).reshape(
            line_count
        )
        rate_line = lax.dynamic_slice_in_dim(rate_flat, first_line, per_device).reshape(
            1, per_device
        )
        var_line = lax.dynamic_slice_in_dim(var_flat, first_line, per_device).reshape(1, per_device)
        diffusion, advection = spot_terms(spot_whole[0], var_line, rate_line)
        system = line_coefficients(
            diffusion, advection, rate_line / 3.0, spot_whole[1], spot_whole[2]
        )
        solved = implicit(system, gathered, 0)
        return lax.all_to_all(solved, "spot", split_axis=0, concat_axis=1, tiled=True).reshape(
            spot_rows, planes, var_cols
        )

    var_count = var_nodes.shape[0]
    blocks = var_count // var_cols
    var_vec = var_coords[1:-1]
    var_first, var_second = stencil_weights(var_coords)
    var_diffusion, var_advection = var_terms(var_vec)
    var_behind = var_diffusion * var_second[0] + var_advection * var_first[0]
    var_middle = var_diffusion * var_second[1] + var_advection * var_first[1]
    var_ahead = var_diffusion * var_second[2] + var_advection * var_first[2]
    reaction_plain = rate_plain / 3.0
    var_lower = (-solve_scale * var_behind).reshape(blocks, var_cols)
    var_upper = (-solve_scale * var_ahead).reshape(blocks, var_cols)
    var_main = (
        1.0 - solve_scale * (var_middle.reshape(var_count, 1) - reaction_plain.reshape(1, planes))
    ).reshape(blocks, var_cols, planes)

    lower_own = lax.dynamic_index_in_dim(var_lower, var_place, 0, keepdims=False)
    upper_own = lax.dynamic_index_in_dim(var_upper, var_place, 0, keepdims=False)
    main_own = lax.dynamic_index_in_dim(var_main, var_place, 0, keepdims=False)
    column_shape = (var_cols, 2, planes)
    position = lax.broadcasted_iota(jnp.int32, column_shape, 0)
    kind = lax.broadcasted_iota(jnp.int32, column_shape, 1)
    coupling = jnp.where(
        (kind == 0) & (position == 0),
        lower_own[0],
        jnp.where((kind == 1) & (position == var_cols - 1), upper_own[var_cols - 1], 0.0),
    )
    flat = (var_cols, 2 * planes)
    columns = line_solve(
        jnp.broadcast_to(lower_own.reshape(var_cols, 1), flat),
        jnp.broadcast_to(main_own.reshape(var_cols, 1, planes), column_shape).reshape(flat),
        jnp.broadcast_to(upper_own.reshape(var_cols, 1), flat),
        coupling.reshape(flat),
    ).reshape(column_shape)
    g_own, h_own = columns[:, 0, :], columns[:, 1, :]
    column_ends = jnp.stack([g_own[0], g_own[var_cols - 1], h_own[0], h_own[var_cols - 1]])
    def interface_solve(y_first, y_last, g_first, g_last, h_first, h_last):
        size = 2 * (blocks - 1)
        matrix = [[None] * size for _ in range(size)]
        rhs = [None] * size
        for b in range(blocks - 1):
            matrix[2 * b][2 * b] = 1.0
            if b >= 1:
                matrix[2 * b][2 * b - 2] = g_last[b]
            matrix[2 * b][2 * b + 1] = h_last[b]
            rhs[2 * b] = y_last[b]
            matrix[2 * b + 1][2 * b + 1] = 1.0
            matrix[2 * b + 1][2 * b] = g_first[b + 1]
            if b + 2 <= blocks - 1:
                matrix[2 * b + 1][2 * b + 3] = h_first[b + 1]
            rhs[2 * b + 1] = y_first[b + 1]
        for k in range(size):
            for i in range(k + 1, size):
                if matrix[i][k] is None:
                    continue
                factor = matrix[i][k] / matrix[k][k]
                for c in range(k + 1, size):
                    if matrix[k][c] is None:
                        continue
                    update = factor * matrix[k][c]
                    matrix[i][c] = -update if matrix[i][c] is None else matrix[i][c] - update
                rhs[i] = rhs[i] - factor * rhs[k]
                matrix[i][k] = None
        solved = [None] * size
        for k in reversed(range(size)):
            total = rhs[k]
            for c in range(k + 1, size):
                if matrix[k][c] is not None:
                    total = total - matrix[k][c] * solved[c]
            solved[k] = total / matrix[k][k]
        zero = jnp.zeros_like(y_first[0])
        left = jnp.stack([zero] + [solved[2 * b] for b in range(blocks - 1)])
        right = jnp.stack([solved[2 * b + 1] for b in range(blocks - 1)] + [zero])
        return (
            lax.dynamic_index_in_dim(left, var_place, 0, keepdims=False),
            lax.dynamic_index_in_dim(right, var_place, 0, keepdims=False),
        )

    def gather_ends(ends):
        stacked = gather_var(ends, blocks)
        order = (var_place - jnp.arange(blocks)) % blocks
        return jnp.take(stacked, order, axis=0)

    def var_solve(values):
        line_count = spot_rows * planes
        lines = values.transpose(2, 0, 1).reshape(var_cols, line_count)
        shape = lines.shape
        local = line_solve(
            jnp.broadcast_to(lower_own.reshape(var_cols, 1), shape),
            jnp.broadcast_to(main_own.reshape(var_cols, 1, planes), (var_cols, spot_rows, planes)).reshape(shape),
            jnp.broadcast_to(upper_own.reshape(var_cols, 1), shape),
            lines,
        ).reshape(var_cols, spot_rows, planes)
        message = jnp.concatenate(
            [local[0], local[var_cols - 1], column_ends], axis=0
        )
        ends = gather_ends(message)
        left, right = interface_solve(
            ends[:, :spot_rows],
            ends[:, spot_rows : 2 * spot_rows],
            ends[:, 2 * spot_rows],
            ends[:, 2 * spot_rows + 1],
            ends[:, 2 * spot_rows + 2],
            ends[:, 2 * spot_rows + 3],
        )
        solved = (
            local
            - left.reshape(1, spot_rows, planes) * g_own.reshape(var_cols, 1, planes)
            - right.reshape(1, spot_rows, planes) * h_own.reshape(var_cols, 1, planes)
        )
        return solved.transpose(1, 2, 0)

    def rate_solve(values):
        diffusion, advection = rate_terms(rate_geo[0])
        system = line_coefficients(
            diffusion, advection, rate_geo[0] / 3.0, rate_geo[1], rate_geo[2]
        )
        return implicit(system, values, 1)

    z_zero = time_step * edge_terms(option_value, False)
    z_one = spot_solve(z_zero)
    z_two = var_solve(z_one)
    z_three = rate_solve(z_two)
    w_zero = z_zero + half_step * edge_terms(z_three, True)
    w_one = spot_solve(w_zero)
    w_two = var_solve(w_one)
    w_three = rate_solve(w_two)
    return option_value + w_three


def solution(mesh):
    in_specs = (P("spot", None, "var"), P(), P(), P())
    out_specs = P("spot", None, "var")
    return jax.shard_map(shards, mesh=mesh, in_specs=in_specs, out_specs=out_specs, check_vma=False)
```

```python
import functools

import jax
import jax.numpy as jnp
from jax import lax
from jax.experimental import pallas as pl
from jax.experimental.pallas import tpu as pltpu
from jax.sharding import PartitionSpec as P

time_step = 0.01
solve_scale = 0.5 * time_step
half_step = 0.5 * time_step
spot_low = 0.5
spot_high = 2.5
var_low = 0.02
var_high = 1.0
rate_low = -0.1
rate_high = 0.2
dividend_yield = 0.02
reversion_var = 2.0
long_var = 0.04
vol_var = 0.6
reversion_rate = 0.1
long_rate = 0.05
vol_rate = 0.1
coupling_sv = -0.7 * vol_var
coupling_sr = 0.2 * vol_rate
coupling_vr = 0.1 * vol_var * vol_rate


def padded_2(array, sides, width):
    for axis, dim in sides:
        devices, length = (lax.axis_size(axis), array.shape[dim])
        up = [(i, (i + 1) % devices) for i in range(devices - 1)]
        down = [(j, i) for i, j in up]
        last = lax.slice_in_dim(array, length - width, length, axis=dim)
        initial = lax.slice_in_dim(array, 0, width, axis=dim)
        before = lax.ppermute(last, axis, up)
        after = lax.ppermute(initial, axis, down)
        array = jnp.concatenate([before, array, after], axis=dim)
    return array


def coordinates(node_list, low_end, high_end):
    length = node_list.shape[0]
    extended = jnp.concatenate(
        [jnp.full((1,), -1, jnp.int32), node_list, jnp.full((1,), 4 * length, jnp.int32)]
    )
    return low_end + (high_end - low_end) * extended.astype(jnp.float32) / (4 * length - 1)


def stencil_weights(coords):
    behind = coords[1:-1] - coords[:-2]
    ahead = coords[2:] - coords[1:-1]
    spread = behind + ahead
    first_diff = (
        -ahead / (behind * spread),
        (ahead - behind) / (behind * ahead),
        behind / (ahead * spread),
    )
    second_diff = (2.0 / (behind * spread), -2.0 / (behind * ahead), 2.0 / (ahead * spread))
    return (first_diff, second_diff)


def geometry(coords, position, dim_count, offset, length):
    first_diff, second_diff = stencil_weights(coords)
    vectors = (coords[1:-1],) + first_diff + second_diff
    target = [1] * dim_count
    target[position] = length
    pieces = [
        lax.dynamic_slice_in_dim(vector, offset, length).reshape(target) for vector in vectors
    ]
    return (pieces[0], tuple(pieces[1:4]), tuple(pieces[4:7]))


def spot_terms(spot_x, var_x, rate_x):
    return (0.5 * spot_x * spot_x * var_x, (rate_x - dividend_yield) * spot_x)


def var_terms(var_x):
    return (0.5 * vol_var * vol_var * var_x, reversion_var * (long_var - var_x))


def rate_terms(rate_x):
    return (0.5 * vol_rate * vol_rate, reversion_rate * (long_rate - rate_x))


def line_coefficients(diffusion, advection, reaction, first_diff, second_diff):
    behind = diffusion * second_diff[0] + advection * first_diff[0]
    centre = diffusion * second_diff[1] + advection * first_diff[1] - reaction
    ahead = diffusion * second_diff[2] + advection * first_diff[2]
    return (behind, centre, ahead)


def explicit_terms(padded, spot_geo, var_geo, rate_geo, mixing_only):
    spot_x, spot_first, spot_second = spot_geo
    var_x, var_first, var_second = var_geo
    rate_x, rate_first, rate_second = rate_geo
    spot_rows = padded.shape[0] - 2
    planes = padded.shape[1] - 2
    var_cols = padded.shape[2] - 2
    middle = padded[1:-1, 1:-1, 1:-1]
    cross_sv = 0.0
    cross_sr = 0.0
    cross_vr = 0.0
    for outer_step in range(3):
        for inner_step in range(3):
            cross_sv = (
                cross_sv
                + spot_first[outer_step]
                * var_first[inner_step]
                * padded[
                    outer_step : outer_step + spot_rows, 1:-1, inner_step : inner_step + var_cols
                ]
            )
            cross_sr = (
                cross_sr
                + spot_first[outer_step]
                * rate_first[inner_step]
                * padded[
                    outer_step : outer_step + spot_rows, inner_step : inner_step + planes, 1:-1
                ]
            )
            cross_vr = (
                cross_vr
                + var_first[outer_step]
                * rate_first[inner_step]
                * padded[1:-1, inner_step : inner_step + planes, outer_step : outer_step + var_cols]
            )
    root_var = jnp.sqrt(var_x)
    mixing = (
        coupling_sv * spot_x * var_x * cross_sv
        + coupling_sr * spot_x * root_var * cross_sr
        + coupling_vr * root_var * cross_vr
    )
    if mixing_only:
        return mixing
    reaction = rate_x / 3.0
    diffusion, advection = spot_terms(spot_x, var_x, rate_x)
    behind, centre, ahead = line_coefficients(
        diffusion, advection, reaction, spot_first, spot_second
    )
    along_spot = behind * padded[:-2, 1:-1, 1:-1] + centre * middle + ahead * padded[2:, 1:-1, 1:-1]
    diffusion, advection = var_terms(var_x)
    behind, centre, ahead = line_coefficients(diffusion, advection, reaction, var_first, var_second)
    along_var = behind * padded[1:-1, 1:-1, :-2] + centre * middle + ahead * padded[1:-1, 1:-1, 2:]
    diffusion, advection = rate_terms(rate_x)
    behind, centre, ahead = line_coefficients(
        diffusion, advection, reaction, rate_first, rate_second
    )
    along_rate = behind * padded[1:-1, :-2, 1:-1] + centre * middle + ahead * padded[1:-1, 2:, 1:-1]
    return mixing + along_spot + along_var + along_rate


def reduce_solve(lower_band, main_band, upper_band, right_side, dimension):
    length = right_side.shape[dimension]
    if length == 1:
        return right_side / main_band

    def even_rows(source):
        return lax.slice_in_dim(source, 0, length, 2, dimension)

    def odd_rows(source):
        return lax.slice_in_dim(source, 1, length, 2, dimension)

    def onward(source, filler):
        remainder = lax.slice_in_dim(source, 1, source.shape[dimension], axis=dimension)
        return jnp.concatenate(
            [remainder, jnp.zeros_like(lax.slice_in_dim(source, 0, 1, axis=dimension)) + filler],
            axis=dimension,
        )

    lower_even, main_even, upper_even, right_even = [
        even_rows(source) for source in (lower_band, main_band, upper_band, right_side)
    ]
    lower_odd, main_odd, upper_odd, right_odd = [
        odd_rows(source) for source in (lower_band, main_band, upper_band, right_side)
    ]
    lower_next = onward(lower_even, 0.0)
    main_next = onward(main_even, 1.0)
    upper_next = onward(upper_even, 0.0)
    right_next = onward(right_even, 0.0)
    ratio_back = -lower_odd / main_even
    ratio_ahead = -upper_odd / main_next
    solved_odd = reduce_solve(
        ratio_back * lower_even,
        main_odd + ratio_back * upper_even + ratio_ahead * lower_next,
        ratio_ahead * upper_next,
        right_odd + ratio_back * right_even + ratio_ahead * right_next,
        dimension,
    )
    remainder = lax.slice_in_dim(solved_odd, 0, solved_odd.shape[dimension] - 1, axis=dimension)
    solved_even = (
        right_even
        - lower_even
        * jnp.concatenate(
            [jnp.zeros_like(lax.slice_in_dim(solved_odd, 0, 1, axis=dimension)), remainder],
            axis=dimension,
        )
        - upper_even * solved_odd
    ) / main_even
    joined = jnp.stack([solved_even, solved_odd], axis=dimension + 1)
    return joined.reshape(right_side.shape)


def cyclic_kernel(lower_ref, main_ref, upper_ref, rhs_ref, out_ref, a_s, b_s, c_s, d_s):
    count, width = rhs_ref.shape
    pad = count // 2
    for ref, fill in ((a_s, 0.0), (b_s, 1.0), (c_s, 0.0), (d_s, 0.0)):
        ref[0:pad, :] = jnp.full((pad, width), fill, jnp.float32)
        ref[pad + count : 2 * pad + count, :] = jnp.full((pad, width), fill, jnp.float32)
    row = lax.broadcasted_iota(jnp.int32, (count, width), 0)
    a_s[pad : pad + count, :] = jnp.where(row == 0, 0.0, lower_ref[...])
    b_s[pad : pad + count, :] = main_ref[...]
    c_s[pad : pad + count, :] = jnp.where(row == count - 1, 0.0, upper_ref[...])
    d_s[pad : pad + count, :] = rhs_ref[...]
    stride = 1
    while stride < count:
        centre = slice(pad, pad + count)
        before = slice(pad - stride, pad - stride + count)
        after = slice(pad + stride, pad + stride + count)
        a, b, c, d = a_s[centre, :], b_s[centre, :], c_s[centre, :], d_s[centre, :]
        ratio_back = -a / b_s[before, :]
        ratio_ahead = -c / b_s[after, :]
        new_b = b + ratio_back * c_s[before, :] + ratio_ahead * a_s[after, :]
        new_d = d + ratio_back * d_s[before, :] + ratio_ahead * d_s[after, :]
        new_a = ratio_back * a_s[before, :]
        new_c = ratio_ahead * c_s[after, :]
        a_s[centre, :] = new_a
        b_s[centre, :] = new_b
        c_s[centre, :] = new_c
        d_s[centre, :] = new_d
        stride *= 2
    out_ref[...] = d_s[pad : pad + count, :] / b_s[pad : pad + count, :]


def line_solve(lower_band, main_band, upper_band, right_side):
    count, width = right_side.shape
    scratch = pltpu.VMEM((2 * (count // 2) + count, width), jnp.float32)
    return pl.pallas_call(
        cyclic_kernel,
        out_shape=jax.ShapeDtypeStruct((count, width), jnp.float32),
        scratch_shapes=[scratch] * 4,
    )(lower_band, main_band, upper_band, right_side)


def gather_kernel(blocks, ends_ref, out_ref, landed, send_sem, recv_sem):
    me = lax.axis_index("var")
    spot = lax.axis_index("spot")
    barrier = pltpu.get_barrier_semaphore()
    for shift in range(1, blocks):
        peer = lax.rem(me + shift, blocks)
        pl.semaphore_signal(barrier, inc=1, device_id=(spot, peer), device_id_type=pl.DeviceIdType.MESH)
    pl.semaphore_wait(barrier, blocks - 1)
    sends = []
    for shift in range(1, blocks):
        peer = lax.rem(me + shift, blocks)
        copy = pltpu.make_async_remote_copy(
            src_ref=ends_ref,
            dst_ref=landed.at[me],
            send_sem=send_sem.at[shift - 1],
            recv_sem=recv_sem.at[me],
            device_id=(spot, peer),
            device_id_type=pl.DeviceIdType.MESH,
        )
        copy.start()
        sends.append(copy)
    out_ref[me] = ends_ref[...]
    for copy in sends:
        copy.wait_send()
    for shift in range(1, blocks):
        source = lax.rem(me + blocks - shift, blocks)
        pltpu.make_async_remote_copy(
            src_ref=ends_ref,
            dst_ref=landed.at[source],
            send_sem=send_sem.at[shift - 1],
            recv_sem=recv_sem.at[source],
            device_id=(spot, source),
            device_id_type=pl.DeviceIdType.MESH,
        ).wait_recv()
        out_ref[source] = landed[source]


def gather_var(ends, blocks):
    return pl.pallas_call(
        functools.partial(gather_kernel, blocks),
        out_shape=jax.ShapeDtypeStruct((blocks,) + ends.shape, jnp.float32),
        scratch_shapes=[
            pltpu.VMEM((blocks,) + ends.shape, jnp.float32),
            pltpu.SemaphoreType.DMA((blocks - 1,)),
            pltpu.SemaphoreType.DMA((blocks,)),
        ],
        compiler_params=pltpu.CompilerParams(collective_id=0, has_side_effects=True),
    )(ends)


def implicit(system, right_side, dimension):
    behind, centre, ahead = system
    lower_band = jnp.broadcast_to(-solve_scale * behind, right_side.shape)
    main_band = jnp.broadcast_to(1.0 - solve_scale * centre, right_side.shape)
    upper_band = jnp.broadcast_to(-solve_scale * ahead, right_side.shape)
    return reduce_solve(lower_band, main_band, upper_band, right_side, dimension)


def shards(option_value, spot_nodes, var_nodes, rate_nodes):
    spot_rows, planes, var_cols = option_value.shape
    line_count = planes * var_cols
    spot_place = lax.axis_index("spot")
    var_place = lax.axis_index("var")
    spot_coords = coordinates(spot_nodes, spot_low, spot_high)
    var_coords = coordinates(var_nodes, var_low, var_high)
    rate_coords = coordinates(rate_nodes, rate_low, rate_high)
    spot_geo = geometry(spot_coords, 0, 3, spot_place * spot_rows, spot_rows)
    var_geo = geometry(var_coords, 2, 3, var_place * var_cols, var_cols)
    rate_geo = geometry(rate_coords, 1, 3, 0, planes)
    spot_whole = geometry(spot_coords, 0, 2, 0, spot_nodes.shape[0])
    var_whole = geometry(var_coords, 1, 2, 0, var_nodes.shape[0])
    rate_plain = rate_geo[0].reshape(planes)
    var_plain = var_geo[0].reshape(var_cols)

    def edge_terms(values, mixing_only):
        padded = padded_2(values, (("spot", 0), ("var", 2)), 1)
        padded = jnp.pad(padded, ((0, 0), (1, 1), (0, 0)))
        return explicit_terms(padded, spot_geo, var_geo, rate_geo, mixing_only)

    def spot_solve(values):
        gathered = lax.all_to_all(
            values.reshape(spot_rows, line_count), "spot", split_axis=1, concat_axis=0, tiled=True
        )
        per_device = gathered.shape[1]
        first_line = spot_place * per_device
        rate_flat = jnp.broadcast_to(rate_plain.reshape(planes, 1), (planes, var_cols)).reshape(
            line_count
        )
        var_flat = jnp.broadcast_to(var_plain.reshape(1, var_cols), (planes, var_cols)).reshape(
            line_count
        )
        rate_line = lax.dynamic_slice_in_dim(rate_flat, first_line, per_device).reshape(
            1, per_device
        )
        var_line = lax.dynamic_slice_in_dim(var_flat, first_line, per_device).reshape(1, per_device)
        diffusion, advection = spot_terms(spot_whole[0], var_line, rate_line)
        system = line_coefficients(
            diffusion, advection, rate_line / 3.0, spot_whole[1], spot_whole[2]
        )
        solved = implicit(system, gathered, 0)
        return lax.all_to_all(solved, "spot", split_axis=0, concat_axis=1, tiled=True).reshape(
            spot_rows, planes, var_cols
        )

    var_count = var_nodes.shape[0]
    blocks = var_count // var_cols
    var_vec = var_coords[1:-1]
    var_first, var_second = stencil_weights(var_coords)
    var_diffusion, var_advection = var_terms(var_vec)
    var_behind = var_diffusion * var_second[0] + var_advection * var_first[0]
    var_middle = var_diffusion * var_second[1] + var_advection * var_first[1]
    var_ahead = var_diffusion * var_second[2] + var_advection * var_first[2]
    reaction_plain = rate_plain / 3.0
    var_lower = (-solve_scale * var_behind).reshape(blocks, var_cols)
    var_upper = (-solve_scale * var_ahead).reshape(blocks, var_cols)
    var_main = (
        1.0 - solve_scale * (var_middle.reshape(var_count, 1) - reaction_plain.reshape(1, planes))
    ).reshape(blocks, var_cols, planes)

    lower_own = lax.dynamic_index_in_dim(var_lower, var_place, 0, keepdims=False)
    upper_own = lax.dynamic_index_in_dim(var_upper, var_place, 0, keepdims=False)
    main_own = lax.dynamic_index_in_dim(var_main, var_place, 0, keepdims=False)
    column_shape = (var_cols, 2, planes)
    position = lax.broadcasted_iota(jnp.int32, column_shape, 0)
    kind = lax.broadcasted_iota(jnp.int32, column_shape, 1)
    coupling = jnp.where(
        (kind == 0) & (position == 0),
        lower_own[0],
        jnp.where((kind == 1) & (position == var_cols - 1), upper_own[var_cols - 1], 0.0),
    )
    flat = (var_cols, 2 * planes)
    columns = line_solve(
        jnp.broadcast_to(lower_own.reshape(var_cols, 1), flat),
        jnp.broadcast_to(main_own.reshape(var_cols, 1, planes), column_shape).reshape(flat),
        jnp.broadcast_to(upper_own.reshape(var_cols, 1), flat),
        coupling.reshape(flat),
    ).reshape(column_shape)
    g_own, h_own = columns[:, 0, :], columns[:, 1, :]
    column_ends = jnp.stack([g_own[0], g_own[var_cols - 1], h_own[0], h_own[var_cols - 1]])
    def interface_solve(y_first, y_last, g_first, g_last, h_first, h_last):
        size = 2 * (blocks - 1)
        matrix = [[None] * size for _ in range(size)]
        rhs = [None] * size
        for b in range(blocks - 1):
            matrix[2 * b][2 * b] = 1.0
            if b >= 1:
                matrix[2 * b][2 * b - 2] = g_last[b]
            matrix[2 * b][2 * b + 1] = h_last[b]
            rhs[2 * b] = y_last[b]
            matrix[2 * b + 1][2 * b + 1] = 1.0
            matrix[2 * b + 1][2 * b] = g_first[b + 1]
            if b + 2 <= blocks - 1:
                matrix[2 * b + 1][2 * b + 3] = h_first[b + 1]
            rhs[2 * b + 1] = y_first[b + 1]
        for k in range(size):
            for i in range(k + 1, size):
                if matrix[i][k] is None:
                    continue
                factor = matrix[i][k] / matrix[k][k]
                for c in range(k + 1, size):
                    if matrix[k][c] is None:
                        continue
                    update = factor * matrix[k][c]
                    matrix[i][c] = -update if matrix[i][c] is None else matrix[i][c] - update
                rhs[i] = rhs[i] - factor * rhs[k]
                matrix[i][k] = None
        solved = [None] * size
        for k in reversed(range(size)):
            total = rhs[k]
            for c in range(k + 1, size):
                if matrix[k][c] is not None:
                    total = total - matrix[k][c] * solved[c]
            solved[k] = total / matrix[k][k]
        zero = jnp.zeros_like(y_first[0])
        left = jnp.stack([zero] + [solved[2 * b] for b in range(blocks - 1)])
        right = jnp.stack([solved[2 * b + 1] for b in range(blocks - 1)] + [zero])
        return (
            lax.dynamic_index_in_dim(left, var_place, 0, keepdims=False),
            lax.dynamic_index_in_dim(right, var_place, 0, keepdims=False),
        )

    def var_solve(values):
        line_count = spot_rows * planes
        lines = values.transpose(2, 0, 1).reshape(var_cols, line_count)
        shape = lines.shape
        local = line_solve(
            jnp.broadcast_to(lower_own.reshape(var_cols, 1), shape),
            jnp.broadcast_to(main_own.reshape(var_cols, 1, planes), (var_cols, spot_rows, planes)).reshape(shape),
            jnp.broadcast_to(upper_own.reshape(var_cols, 1), shape),
            lines,
        ).reshape(var_cols, spot_rows, planes)
        message = jnp.concatenate(
            [local[0], local[var_cols - 1], column_ends], axis=0
        )
        ends = gather_var(message, blocks)
        left, right = interface_solve(
            ends[:, :spot_rows],
            ends[:, spot_rows : 2 * spot_rows],
            ends[:, 2 * spot_rows],
            ends[:, 2 * spot_rows + 1],
            ends[:, 2 * spot_rows + 2],
            ends[:, 2 * spot_rows + 3],
        )
        solved = (
            local
            - left.reshape(1, spot_rows, planes) * g_own.reshape(var_cols, 1, planes)
            - right.reshape(1, spot_rows, planes) * h_own.reshape(var_cols, 1, planes)
        )
        return solved.transpose(1, 2, 0)

    def rate_solve(values):
        diffusion, advection = rate_terms(rate_geo[0])
        system = line_coefficients(
            diffusion, advection, rate_geo[0] / 3.0, rate_geo[1], rate_geo[2]
        )
        return implicit(system, values, 1)

    z_zero = time_step * edge_terms(option_value, False)
    z_one = spot_solve(z_zero)
    z_two = var_solve(z_one)
    z_three = rate_solve(z_two)
    w_zero = z_zero + half_step * edge_terms(z_three, True)
    w_one = spot_solve(w_zero)
    w_two = var_solve(w_one)
    w_three = rate_solve(w_two)
    return option_value + w_three


def solution(mesh):
    in_specs = (P("spot", None, "var"), P(), P(), P())
    out_specs = P("spot", None, "var")
    return jax.shard_map(shards, mesh=mesh, in_specs=in_specs, out_specs=out_specs, check_vma=False)
```

```python
import functools

import jax
import jax.numpy as jnp
from jax import lax
from jax.experimental import pallas as pl
from jax.experimental.pallas import tpu as pltpu
from jax.sharding import PartitionSpec as P

time_step = 0.01
solve_scale = 0.5 * time_step
half_step = 0.5 * time_step
spot_low = 0.5
spot_high = 2.5
var_low = 0.02
var_high = 1.0
rate_low = -0.1
rate_high = 0.2
dividend_yield = 0.02
reversion_var = 2.0
long_var = 0.04
vol_var = 0.6
reversion_rate = 0.1
long_rate = 0.05
vol_rate = 0.1
coupling_sv = -0.7 * vol_var
coupling_sr = 0.2 * vol_rate
coupling_vr = 0.1 * vol_var * vol_rate


def padded_2(array, sides, width):
    for axis, dim in sides:
        devices, length = (lax.axis_size(axis), array.shape[dim])
        up = [(i, (i + 1) % devices) for i in range(devices - 1)]
        down = [(j, i) for i, j in up]
        last = lax.slice_in_dim(array, length - width, length, axis=dim)
        initial = lax.slice_in_dim(array, 0, width, axis=dim)
        before = lax.ppermute(last, axis, up)
        after = lax.ppermute(initial, axis, down)
        array = jnp.concatenate([before, array, after], axis=dim)
    return array


def coordinates(node_list, low_end, high_end):
    length = node_list.shape[0]
    extended = jnp.concatenate(
        [jnp.full((1,), -1, jnp.int32), node_list, jnp.full((1,), 4 * length, jnp.int32)]
    )
    return low_end + (high_end - low_end) * extended.astype(jnp.float32) / (4 * length - 1)


def stencil_weights(coords):
    behind = coords[1:-1] - coords[:-2]
    ahead = coords[2:] - coords[1:-1]
    spread = behind + ahead
    first_diff = (
        -ahead / (behind * spread),
        (ahead - behind) / (behind * ahead),
        behind / (ahead * spread),
    )
    second_diff = (2.0 / (behind * spread), -2.0 / (behind * ahead), 2.0 / (ahead * spread))
    return (first_diff, second_diff)


def geometry(coords, position, dim_count, offset, length):
    first_diff, second_diff = stencil_weights(coords)
    vectors = (coords[1:-1],) + first_diff + second_diff
    target = [1] * dim_count
    target[position] = length
    pieces = [
        lax.dynamic_slice_in_dim(vector, offset, length).reshape(target) for vector in vectors
    ]
    return (pieces[0], tuple(pieces[1:4]), tuple(pieces[4:7]))


def spot_terms(spot_x, var_x, rate_x):
    return (0.5 * spot_x * spot_x * var_x, (rate_x - dividend_yield) * spot_x)


def var_terms(var_x):
    return (0.5 * vol_var * vol_var * var_x, reversion_var * (long_var - var_x))


def rate_terms(rate_x):
    return (0.5 * vol_rate * vol_rate, reversion_rate * (long_rate - rate_x))


def line_coefficients(diffusion, advection, reaction, first_diff, second_diff):
    behind = diffusion * second_diff[0] + advection * first_diff[0]
    centre = diffusion * second_diff[1] + advection * first_diff[1] - reaction
    ahead = diffusion * second_diff[2] + advection * first_diff[2]
    return (behind, centre, ahead)


def explicit_terms(padded, spot_geo, var_geo, rate_geo, mixing_only):
    spot_x, spot_first, spot_second = spot_geo
    var_x, var_first, var_second = var_geo
    rate_x, rate_first, rate_second = rate_geo
    spot_rows = padded.shape[0] - 2
    planes = padded.shape[1] - 2
    var_cols = padded.shape[2] - 2
    middle = padded[1:-1, 1:-1, 1:-1]
    cross_sv = 0.0
    cross_sr = 0.0
    cross_vr = 0.0
    for outer_step in range(3):
        for inner_step in range(3):
            cross_sv = (
                cross_sv
                + spot_first[outer_step]
                * var_first[inner_step]
                * padded[
                    outer_step : outer_step + spot_rows, 1:-1, inner_step : inner_step + var_cols
                ]
            )
            cross_sr = (
                cross_sr
                + spot_first[outer_step]
                * rate_first[inner_step]
                * padded[
                    outer_step : outer_step + spot_rows, inner_step : inner_step + planes, 1:-1
                ]
            )
            cross_vr = (
                cross_vr
                + var_first[outer_step]
                * rate_first[inner_step]
                * padded[1:-1, inner_step : inner_step + planes, outer_step : outer_step + var_cols]
            )
    root_var = jnp.sqrt(var_x)
    mixing = (
        coupling_sv * spot_x * var_x * cross_sv
        + coupling_sr * spot_x * root_var * cross_sr
        + coupling_vr * root_var * cross_vr
    )
    if mixing_only:
        return mixing
    reaction = rate_x / 3.0
    diffusion, advection = spot_terms(spot_x, var_x, rate_x)
    behind, centre, ahead = line_coefficients(
        diffusion, advection, reaction, spot_first, spot_second
    )
    along_spot = behind * padded[:-2, 1:-1, 1:-1] + centre * middle + ahead * padded[2:, 1:-1, 1:-1]
    diffusion, advection = var_terms(var_x)
    behind, centre, ahead = line_coefficients(diffusion, advection, reaction, var_first, var_second)
    along_var = behind * padded[1:-1, 1:-1, :-2] + centre * middle + ahead * padded[1:-1, 1:-1, 2:]
    diffusion, advection = rate_terms(rate_x)
    behind, centre, ahead = line_coefficients(
        diffusion, advection, reaction, rate_first, rate_second
    )
    along_rate = behind * padded[1:-1, :-2, 1:-1] + centre * middle + ahead * padded[1:-1, 2:, 1:-1]
    return mixing + along_spot + along_var + along_rate


def reduce_solve(lower_band, main_band, upper_band, right_side, dimension):
    length = right_side.shape[dimension]
    if length == 1:
        return right_side / main_band

    def even_rows(source):
        return lax.slice_in_dim(source, 0, length, 2, dimension)

    def odd_rows(source):
        return lax.slice_in_dim(source, 1, length, 2, dimension)

    def onward(source, filler):
        remainder = lax.slice_in_dim(source, 1, source.shape[dimension], axis=dimension)
        return jnp.concatenate(
            [remainder, jnp.zeros_like(lax.slice_in_dim(source, 0, 1, axis=dimension)) + filler],
            axis=dimension,
        )

    lower_even, main_even, upper_even, right_even = [
        even_rows(source) for source in (lower_band, main_band, upper_band, right_side)
    ]
    lower_odd, main_odd, upper_odd, right_odd = [
        odd_rows(source) for source in (lower_band, main_band, upper_band, right_side)
    ]
    lower_next = onward(lower_even, 0.0)
    main_next = onward(main_even, 1.0)
    upper_next = onward(upper_even, 0.0)
    right_next = onward(right_even, 0.0)
    ratio_back = -lower_odd / main_even
    ratio_ahead = -upper_odd / main_next
    solved_odd = reduce_solve(
        ratio_back * lower_even,
        main_odd + ratio_back * upper_even + ratio_ahead * lower_next,
        ratio_ahead * upper_next,
        right_odd + ratio_back * right_even + ratio_ahead * right_next,
        dimension,
    )
    remainder = lax.slice_in_dim(solved_odd, 0, solved_odd.shape[dimension] - 1, axis=dimension)
    solved_even = (
        right_even
        - lower_even
        * jnp.concatenate(
            [jnp.zeros_like(lax.slice_in_dim(solved_odd, 0, 1, axis=dimension)), remainder],
            axis=dimension,
        )
        - upper_even * solved_odd
    ) / main_even
    joined = jnp.stack([solved_even, solved_odd], axis=dimension + 1)
    return joined.reshape(right_side.shape)


def cyclic_kernel(lower_ref, main_ref, upper_ref, rhs_ref, out_ref, a_s, b_s, c_s, d_s):
    count, width = rhs_ref.shape
    pad = count // 2
    for ref, fill in ((a_s, 0.0), (b_s, 1.0), (c_s, 0.0), (d_s, 0.0)):
        ref[0:pad, :] = jnp.full((pad, width), fill, jnp.float32)
        ref[pad + count : 2 * pad + count, :] = jnp.full((pad, width), fill, jnp.float32)
    row = lax.broadcasted_iota(jnp.int32, (count, width), 0)
    a_s[pad : pad + count, :] = jnp.where(row == 0, 0.0, lower_ref[...])
    b_s[pad : pad + count, :] = main_ref[...]
    c_s[pad : pad + count, :] = jnp.where(row == count - 1, 0.0, upper_ref[...])
    d_s[pad : pad + count, :] = rhs_ref[...]
    stride = 1
    while stride < count:
        centre = slice(pad, pad + count)
        before = slice(pad - stride, pad - stride + count)
        after = slice(pad + stride, pad + stride + count)
        a, b, c, d = a_s[centre, :], b_s[centre, :], c_s[centre, :], d_s[centre, :]
        ratio_back = -a / b_s[before, :]
        ratio_ahead = -c / b_s[after, :]
        new_b = b + ratio_back * c_s[before, :] + ratio_ahead * a_s[after, :]
        new_d = d + ratio_back * d_s[before, :] + ratio_ahead * d_s[after, :]
        new_a = ratio_back * a_s[before, :]
        new_c = ratio_ahead * c_s[after, :]
        a_s[centre, :] = new_a
        b_s[centre, :] = new_b
        c_s[centre, :] = new_c
        d_s[centre, :] = new_d
        stride *= 2
    out_ref[...] = d_s[pad : pad + count, :] / b_s[pad : pad + count, :]


def line_solve(lower_band, main_band, upper_band, right_side):
    count, width = right_side.shape
    scratch = pltpu.VMEM((2 * (count // 2) + count, width), jnp.float32)
    return pl.pallas_call(
        cyclic_kernel,
        out_shape=jax.ShapeDtypeStruct((count, width), jnp.float32),
        scratch_shapes=[scratch] * 4,
    )(lower_band, main_band, upper_band, right_side)


def gather_kernel(blocks, ends_ref, out_ref, landed, send_sem, recv_sem):
    me = lax.axis_index("var")
    spot = lax.axis_index("spot")
    barrier = pltpu.get_barrier_semaphore()
    for shift in range(1, blocks):
        peer = lax.rem(me + shift, blocks)
        pl.semaphore_signal(barrier, inc=1, device_id=(spot, peer), device_id_type=pl.DeviceIdType.MESH)
    pl.semaphore_wait(barrier, blocks - 1)
    copies = []
    for shift in range(1, blocks):
        peer = lax.rem(me + shift, blocks)
        copy = pltpu.make_async_remote_copy(
            src_ref=ends_ref,
            dst_ref=landed.at[shift - 1],
            send_sem=send_sem.at[shift - 1],
            recv_sem=recv_sem.at[shift - 1],
            device_id=(spot, peer),
            device_id_type=pl.DeviceIdType.MESH,
        )
        copy.start()
        copies.append(copy)
    out_ref[0] = ends_ref[...]
    for copy in copies:
        copy.wait()
    for shift in range(1, blocks):
        out_ref[shift] = landed[shift - 1]


def gather_var(ends, blocks):
    return pl.pallas_call(
        functools.partial(gather_kernel, blocks),
        out_shape=jax.ShapeDtypeStruct((blocks,) + ends.shape, jnp.float32),
        scratch_shapes=[
            pltpu.VMEM((blocks - 1,) + ends.shape, jnp.float32),
            pltpu.SemaphoreType.DMA((blocks - 1,)),
            pltpu.SemaphoreType.DMA((blocks - 1,)),
        ],
        compiler_params=pltpu.CompilerParams(collective_id=0, has_side_effects=True),
    )(ends)


def implicit(system, right_side, dimension):
    behind, centre, ahead = system
    lower_band = jnp.broadcast_to(-solve_scale * behind, right_side.shape)
    main_band = jnp.broadcast_to(1.0 - solve_scale * centre, right_side.shape)
    upper_band = jnp.broadcast_to(-solve_scale * ahead, right_side.shape)
    return reduce_solve(lower_band, main_band, upper_band, right_side, dimension)


def shards(option_value, spot_nodes, var_nodes, rate_nodes):
    spot_rows, planes, var_cols = option_value.shape
    line_count = planes * var_cols
    spot_place = lax.axis_index("spot")
    var_place = lax.axis_index("var")
    spot_coords = coordinates(spot_nodes, spot_low, spot_high)
    var_coords = coordinates(var_nodes, var_low, var_high)
    rate_coords = coordinates(rate_nodes, rate_low, rate_high)
    spot_geo = geometry(spot_coords, 0, 3, spot_place * spot_rows, spot_rows)
    var_geo = geometry(var_coords, 2, 3, var_place * var_cols, var_cols)
    rate_geo = geometry(rate_coords, 1, 3, 0, planes)
    spot_whole = geometry(spot_coords, 0, 2, 0, spot_nodes.shape[0])
    var_whole = geometry(var_coords, 1, 2, 0, var_nodes.shape[0])
    rate_plain = rate_geo[0].reshape(planes)
    var_plain = var_geo[0].reshape(var_cols)

    def edge_terms(values, mixing_only):
        padded = padded_2(values, (("spot", 0), ("var", 2)), 1)
        padded = jnp.pad(padded, ((0, 0), (1, 1), (0, 0)))
        return explicit_terms(padded, spot_geo, var_geo, rate_geo, mixing_only)

    def spot_solve(values):
        gathered = lax.all_to_all(
            values.reshape(spot_rows, line_count), "spot", split_axis=1, concat_axis=0, tiled=True
        )
        per_device = gathered.shape[1]
        first_line = spot_place * per_device
        rate_flat = jnp.broadcast_to(rate_plain.reshape(planes, 1), (planes, var_cols)).reshape(
            line_count
        )
        var_flat = jnp.broadcast_to(var_plain.reshape(1, var_cols), (planes, var_cols)).reshape(
            line_count
        )
        rate_line = lax.dynamic_slice_in_dim(rate_flat, first_line, per_device).reshape(
            1, per_device
        )
        var_line = lax.dynamic_slice_in_dim(var_flat, first_line, per_device).reshape(1, per_device)
        diffusion, advection = spot_terms(spot_whole[0], var_line, rate_line)
        system = line_coefficients(
            diffusion, advection, rate_line / 3.0, spot_whole[1], spot_whole[2]
        )
        solved = implicit(system, gathered, 0)
        return lax.all_to_all(solved, "spot", split_axis=0, concat_axis=1, tiled=True).reshape(
            spot_rows, planes, var_cols
        )

    var_count = var_nodes.shape[0]
    blocks = var_count // var_cols
    var_vec = var_coords[1:-1]
    var_first, var_second = stencil_weights(var_coords)
    var_diffusion, var_advection = var_terms(var_vec)
    var_behind = var_diffusion * var_second[0] + var_advection * var_first[0]
    var_middle = var_diffusion * var_second[1] + var_advection * var_first[1]
    var_ahead = var_diffusion * var_second[2] + var_advection * var_first[2]
    reaction_plain = rate_plain / 3.0
    var_lower = (-solve_scale * var_behind).reshape(blocks, var_cols)
    var_upper = (-solve_scale * var_ahead).reshape(blocks, var_cols)
    var_main = (
        1.0 - solve_scale * (var_middle.reshape(var_count, 1) - reaction_plain.reshape(1, planes))
    ).reshape(blocks, var_cols, planes)

    lower_own = lax.dynamic_index_in_dim(var_lower, var_place, 0, keepdims=False)
    upper_own = lax.dynamic_index_in_dim(var_upper, var_place, 0, keepdims=False)
    main_own = lax.dynamic_index_in_dim(var_main, var_place, 0, keepdims=False)
    column_shape = (var_cols, 2, planes)
    position = lax.broadcasted_iota(jnp.int32, column_shape, 0)
    kind = lax.broadcasted_iota(jnp.int32, column_shape, 1)
    coupling = jnp.where(
        (kind == 0) & (position == 0),
        lower_own[0],
        jnp.where((kind == 1) & (position == var_cols - 1), upper_own[var_cols - 1], 0.0),
    )
    flat = (var_cols, 2 * planes)
    columns = line_solve(
        jnp.broadcast_to(lower_own.reshape(var_cols, 1), flat),
        jnp.broadcast_to(main_own.reshape(var_cols, 1, planes), column_shape).reshape(flat),
        jnp.broadcast_to(upper_own.reshape(var_cols, 1), flat),
        coupling.reshape(flat),
    ).reshape(column_shape)
    g_own, h_own = columns[:, 0, :], columns[:, 1, :]
    column_ends = jnp.stack([g_own[0], g_own[var_cols - 1], h_own[0], h_own[var_cols - 1]])
    def interface_solve(y_first, y_last, g_first, g_last, h_first, h_last):
        size = 2 * (blocks - 1)
        matrix = [[None] * size for _ in range(size)]
        rhs = [None] * size
        for b in range(blocks - 1):
            matrix[2 * b][2 * b] = 1.0
            if b >= 1:
                matrix[2 * b][2 * b - 2] = g_last[b]
            matrix[2 * b][2 * b + 1] = h_last[b]
            rhs[2 * b] = y_last[b]
            matrix[2 * b + 1][2 * b + 1] = 1.0
            matrix[2 * b + 1][2 * b] = g_first[b + 1]
            if b + 2 <= blocks - 1:
                matrix[2 * b + 1][2 * b + 3] = h_first[b + 1]
            rhs[2 * b + 1] = y_first[b + 1]
        for k in range(size):
            for i in range(k + 1, size):
                if matrix[i][k] is None:
                    continue
                factor = matrix[i][k] / matrix[k][k]
                for c in range(k + 1, size):
                    if matrix[k][c] is None:
                        continue
                    update = factor * matrix[k][c]
                    matrix[i][c] = -update if matrix[i][c] is None else matrix[i][c] - update
                rhs[i] = rhs[i] - factor * rhs[k]
                matrix[i][k] = None
        solved = [None] * size
        for k in reversed(range(size)):
            total = rhs[k]
            for c in range(k + 1, size):
                if matrix[k][c] is not None:
                    total = total - matrix[k][c] * solved[c]
            solved[k] = total / matrix[k][k]
        zero = jnp.zeros_like(y_first[0])
        left = jnp.stack([zero] + [solved[2 * b] for b in range(blocks - 1)])
        right = jnp.stack([solved[2 * b + 1] for b in range(blocks - 1)] + [zero])
        return (
            lax.dynamic_index_in_dim(left, var_place, 0, keepdims=False),
            lax.dynamic_index_in_dim(right, var_place, 0, keepdims=False),
        )

    def gather_ends(ends):
        stacked = gather_var(ends, blocks)
        order = (var_place - jnp.arange(blocks)) % blocks
        return jnp.take(stacked, order, axis=0)

    def var_solve(values):
        line_count = spot_rows * planes
        lines = values.transpose(2, 0, 1).reshape(var_cols, line_count)
        shape = lines.shape
        local = line_solve(
            jnp.broadcast_to(lower_own.reshape(var_cols, 1), shape),
            jnp.broadcast_to(main_own.reshape(var_cols, 1, planes), (var_cols, spot_rows, planes)).reshape(shape),
            jnp.broadcast_to(upper_own.reshape(var_cols, 1), shape),
            lines,
        ).reshape(var_cols, spot_rows, planes)
        message = jnp.concatenate(
            [local[0], local[var_cols - 1], column_ends], axis=0
        )
        ends = gather_ends(message)
        left, right = interface_solve(
            ends[:, :spot_rows],
            ends[:, spot_rows : 2 * spot_rows],
            ends[:, 2 * spot_rows],
            ends[:, 2 * spot_rows + 1],
            ends[:, 2 * spot_rows + 2],
            ends[:, 2 * spot_rows + 3],
        )
        solved = (
            local
            - left.reshape(1, spot_rows, planes) * g_own.reshape(var_cols, 1, planes)
            - right.reshape(1, spot_rows, planes) * h_own.reshape(var_cols, 1, planes)
        )
        return solved.transpose(1, 2, 0), left, right

    def rate_solve(values):
        diffusion, advection = rate_terms(rate_geo[0])
        system = line_coefficients(
            diffusion, advection, rate_geo[0] / 3.0, rate_geo[1], rate_geo[2]
        )
        return implicit(system, values, 1)

    def spot_pad(array):
        devices, rows = lax.axis_size("spot"), array.shape[0]
        up = [(i, i + 1) for i in range(devices - 1)]
        down = [(j, i) for i, j in up]
        before = lax.ppermute(array[rows - 1 : rows], "spot", up)
        after = lax.ppermute(array[0:1], "spot", down)
        return jnp.concatenate([before, array, after], axis=0)

    z_zero = time_step * edge_terms(option_value, False)
    z_one = spot_solve(z_zero)
    z_two, edge_left, edge_right = var_solve(z_one)
    z_two_wide = jnp.concatenate(
        [edge_left.reshape(spot_rows, planes, 1), z_two, edge_right.reshape(spot_rows, planes, 1)],
        axis=2,
    )
    z_three_wide = rate_solve(z_two_wide)
    padded = jnp.pad(spot_pad(z_three_wide), ((0, 0), (1, 1), (0, 0)))
    w_zero = z_zero + half_step * explicit_terms(padded, spot_geo, var_geo, rate_geo, True)
    w_one = spot_solve(w_zero)
    w_two, _, _ = var_solve(w_one)
    w_three = rate_solve(w_two)
    return option_value + w_three


def solution(mesh):
    in_specs = (P("spot", None, "var"), P(), P(), P())
    out_specs = P("spot", None, "var")
    return jax.shard_map(shards, mesh=mesh, in_specs=in_specs, out_specs=out_specs, check_vma=False)
```

```python
import functools

import jax
import jax.numpy as jnp
from jax import lax
from jax.experimental import pallas as pl
from jax.experimental.pallas import tpu as pltpu
from jax.sharding import PartitionSpec as P

time_step = 0.01
solve_scale = 0.5 * time_step
half_step = 0.5 * time_step
spot_low = 0.5
spot_high = 2.5
var_low = 0.02
var_high = 1.0
rate_low = -0.1
rate_high = 0.2
dividend_yield = 0.02
reversion_var = 2.0
long_var = 0.04
vol_var = 0.6
reversion_rate = 0.1
long_rate = 0.05
vol_rate = 0.1
coupling_sv = -0.7 * vol_var
coupling_sr = 0.2 * vol_rate
coupling_vr = 0.1 * vol_var * vol_rate


def padded_2(array, sides, width):
    for axis, dim in sides:
        devices, length = (lax.axis_size(axis), array.shape[dim])
        up = [(i, (i + 1) % devices) for i in range(devices - 1)]
        down = [(j, i) for i, j in up]
        last = lax.slice_in_dim(array, length - width, length, axis=dim)
        initial = lax.slice_in_dim(array, 0, width, axis=dim)
        before = lax.ppermute(last, axis, up)
        after = lax.ppermute(initial, axis, down)
        array = jnp.concatenate([before, array, after], axis=dim)
    return array


def coordinates(node_list, low_end, high_end):
    length = node_list.shape[0]
    extended = jnp.concatenate(
        [jnp.full((1,), -1, jnp.int32), node_list, jnp.full((1,), 4 * length, jnp.int32)]
    )
    return low_end + (high_end - low_end) * extended.astype(jnp.float32) / (4 * length - 1)


def stencil_weights(coords):
    behind = coords[1:-1] - coords[:-2]
    ahead = coords[2:] - coords[1:-1]
    spread = behind + ahead
    first_diff = (
        -ahead / (behind * spread),
        (ahead - behind) / (behind * ahead),
        behind / (ahead * spread),
    )
    second_diff = (2.0 / (behind * spread), -2.0 / (behind * ahead), 2.0 / (ahead * spread))
    return (first_diff, second_diff)


def geometry(coords, position, dim_count, offset, length):
    first_diff, second_diff = stencil_weights(coords)
    vectors = (coords[1:-1],) + first_diff + second_diff
    target = [1] * dim_count
    target[position] = length
    pieces = [
        lax.dynamic_slice_in_dim(vector, offset, length).reshape(target) for vector in vectors
    ]
    return (pieces[0], tuple(pieces[1:4]), tuple(pieces[4:7]))


def spot_terms(spot_x, var_x, rate_x):
    return (0.5 * spot_x * spot_x * var_x, (rate_x - dividend_yield) * spot_x)


def var_terms(var_x):
    return (0.5 * vol_var * vol_var * var_x, reversion_var * (long_var - var_x))


def rate_terms(rate_x):
    return (0.5 * vol_rate * vol_rate, reversion_rate * (long_rate - rate_x))


def line_coefficients(diffusion, advection, reaction, first_diff, second_diff):
    behind = diffusion * second_diff[0] + advection * first_diff[0]
    centre = diffusion * second_diff[1] + advection * first_diff[1] - reaction
    ahead = diffusion * second_diff[2] + advection * first_diff[2]
    return (behind, centre, ahead)


def explicit_terms(padded, spot_geo, var_geo, rate_geo, mixing_only):
    spot_x, spot_first, spot_second = spot_geo
    var_x, var_first, var_second = var_geo
    rate_x, rate_first, rate_second = rate_geo
    spot_rows = padded.shape[0] - 2
    planes = padded.shape[1] - 2
    var_cols = padded.shape[2] - 2
    middle = padded[1:-1, 1:-1, 1:-1]
    cross_sv = 0.0
    cross_sr = 0.0
    cross_vr = 0.0
    for outer_step in range(3):
        for inner_step in range(3):
            cross_sv = (
                cross_sv
                + spot_first[outer_step]
                * var_first[inner_step]
                * padded[
                    outer_step : outer_step + spot_rows, 1:-1, inner_step : inner_step + var_cols
                ]
            )
            cross_sr = (
                cross_sr
                + spot_first[outer_step]
                * rate_first[inner_step]
                * padded[
                    outer_step : outer_step + spot_rows, inner_step : inner_step + planes, 1:-1
                ]
            )
            cross_vr = (
                cross_vr
                + var_first[outer_step]
                * rate_first[inner_step]
                * padded[1:-1, inner_step : inner_step + planes, outer_step : outer_step + var_cols]
            )
    root_var = jnp.sqrt(var_x)
    mixing = (
        coupling_sv * spot_x * var_x * cross_sv
        + coupling_sr * spot_x * root_var * cross_sr
        + coupling_vr * root_var * cross_vr
    )
    if mixing_only:
        return mixing
    reaction = rate_x / 3.0
    diffusion, advection = spot_terms(spot_x, var_x, rate_x)
    behind, centre, ahead = line_coefficients(
        diffusion, advection, reaction, spot_first, spot_second
    )
    along_spot = behind * padded[:-2, 1:-1, 1:-1] + centre * middle + ahead * padded[2:, 1:-1, 1:-1]
    diffusion, advection = var_terms(var_x)
    behind, centre, ahead = line_coefficients(diffusion, advection, reaction, var_first, var_second)
    along_var = behind * padded[1:-1, 1:-1, :-2] + centre * middle + ahead * padded[1:-1, 1:-1, 2:]
    diffusion, advection = rate_terms(rate_x)
    behind, centre, ahead = line_coefficients(
        diffusion, advection, reaction, rate_first, rate_second
    )
    along_rate = behind * padded[1:-1, :-2, 1:-1] + centre * middle + ahead * padded[1:-1, 2:, 1:-1]
    return mixing + along_spot + along_var + along_rate


def reduce_solve(lower_band, main_band, upper_band, right_side, dimension):
    length = right_side.shape[dimension]
    if length == 1:
        return right_side / main_band

    def even_rows(source):
        return lax.slice_in_dim(source, 0, length, 2, dimension)

    def odd_rows(source):
        return lax.slice_in_dim(source, 1, length, 2, dimension)

    def onward(source, filler):
        remainder = lax.slice_in_dim(source, 1, source.shape[dimension], axis=dimension)
        return jnp.concatenate(
            [remainder, jnp.zeros_like(lax.slice_in_dim(source, 0, 1, axis=dimension)) + filler],
            axis=dimension,
        )

    lower_even, main_even, upper_even, right_even = [
        even_rows(source) for source in (lower_band, main_band, upper_band, right_side)
    ]
    lower_odd, main_odd, upper_odd, right_odd = [
        odd_rows(source) for source in (lower_band, main_band, upper_band, right_side)
    ]
    lower_next = onward(lower_even, 0.0)
    main_next = onward(main_even, 1.0)
    upper_next = onward(upper_even, 0.0)
    right_next = onward(right_even, 0.0)
    ratio_back = -lower_odd / main_even
    ratio_ahead = -upper_odd / main_next
    solved_odd = reduce_solve(
        ratio_back * lower_even,
        main_odd + ratio_back * upper_even + ratio_ahead * lower_next,
        ratio_ahead * upper_next,
        right_odd + ratio_back * right_even + ratio_ahead * right_next,
        dimension,
    )
    remainder = lax.slice_in_dim(solved_odd, 0, solved_odd.shape[dimension] - 1, axis=dimension)
    solved_even = (
        right_even
        - lower_even
        * jnp.concatenate(
            [jnp.zeros_like(lax.slice_in_dim(solved_odd, 0, 1, axis=dimension)), remainder],
            axis=dimension,
        )
        - upper_even * solved_odd
    ) / main_even
    joined = jnp.stack([solved_even, solved_odd], axis=dimension + 1)
    return joined.reshape(right_side.shape)


def cyclic_kernel(lower_ref, main_ref, upper_ref, rhs_ref, out_ref, a_s, b_s, c_s, d_s):
    count, width = rhs_ref.shape
    pad = count // 2
    for ref, fill in ((a_s, 0.0), (b_s, 1.0), (c_s, 0.0), (d_s, 0.0)):
        ref[0:pad, :] = jnp.full((pad, width), fill, jnp.float32)
        ref[pad + count : 2 * pad + count, :] = jnp.full((pad, width), fill, jnp.float32)
    row = lax.broadcasted_iota(jnp.int32, (count, width), 0)
    a_s[pad : pad + count, :] = jnp.where(row == 0, 0.0, lower_ref[...])
    b_s[pad : pad + count, :] = main_ref[...]
    c_s[pad : pad + count, :] = jnp.where(row == count - 1, 0.0, upper_ref[...])
    d_s[pad : pad + count, :] = rhs_ref[...]
    stride = 1
    while stride < count:
        centre = slice(pad, pad + count)
        before = slice(pad - stride, pad - stride + count)
        after = slice(pad + stride, pad + stride + count)
        a, b, c, d = a_s[centre, :], b_s[centre, :], c_s[centre, :], d_s[centre, :]
        ratio_back = -a / b_s[before, :]
        ratio_ahead = -c / b_s[after, :]
        new_b = b + ratio_back * c_s[before, :] + ratio_ahead * a_s[after, :]
        new_d = d + ratio_back * d_s[before, :] + ratio_ahead * d_s[after, :]
        new_a = ratio_back * a_s[before, :]
        new_c = ratio_ahead * c_s[after, :]
        a_s[centre, :] = new_a
        b_s[centre, :] = new_b
        c_s[centre, :] = new_c
        d_s[centre, :] = new_d
        stride *= 2
    out_ref[...] = d_s[pad : pad + count, :] / b_s[pad : pad + count, :]


def line_solve(lower_band, main_band, upper_band, right_side):
    count, width = right_side.shape
    scratch = pltpu.VMEM((2 * (count // 2) + count, width), jnp.float32)
    return pl.pallas_call(
        cyclic_kernel,
        out_shape=jax.ShapeDtypeStruct((count, width), jnp.float32),
        scratch_shapes=[scratch] * 4,
    )(lower_band, main_band, upper_band, right_side)


def gather_kernel(blocks, ends_ref, out_ref, landed, send_sem, recv_sem):
    me = lax.axis_index("var")
    spot = lax.axis_index("spot")
    barrier = pltpu.get_barrier_semaphore()
    for shift in range(1, blocks):
        peer = lax.rem(me + shift, blocks)
        pl.semaphore_signal(barrier, inc=1, device_id=(spot, peer), device_id_type=pl.DeviceIdType.MESH)
    pl.semaphore_wait(barrier, blocks - 1)
    copies = []
    for shift in range(1, blocks):
        peer = lax.rem(me + shift, blocks)
        copy = pltpu.make_async_remote_copy(
            src_ref=ends_ref,
            dst_ref=landed.at[shift - 1],
            send_sem=send_sem.at[shift - 1],
            recv_sem=recv_sem.at[shift - 1],
            device_id=(spot, peer),
            device_id_type=pl.DeviceIdType.MESH,
        )
        copy.start()
        copies.append(copy)
    out_ref[0] = ends_ref[...]
    for copy in copies:
        copy.wait()
    for shift in range(1, blocks):
        out_ref[shift] = landed[shift - 1]


def gather_var(ends, blocks):
    return pl.pallas_call(
        functools.partial(gather_kernel, blocks),
        out_shape=jax.ShapeDtypeStruct((blocks,) + ends.shape, jnp.float32),
        scratch_shapes=[
            pltpu.VMEM((blocks - 1,) + ends.shape, jnp.float32),
            pltpu.SemaphoreType.DMA((blocks - 1,)),
            pltpu.SemaphoreType.DMA((blocks - 1,)),
        ],
        compiler_params=pltpu.CompilerParams(collective_id=0, has_side_effects=True),
    )(ends)


def implicit(system, right_side, dimension):
    behind, centre, ahead = system
    lower_band = jnp.broadcast_to(-solve_scale * behind, right_side.shape)
    main_band = jnp.broadcast_to(1.0 - solve_scale * centre, right_side.shape)
    upper_band = jnp.broadcast_to(-solve_scale * ahead, right_side.shape)
    return reduce_solve(lower_band, main_band, upper_band, right_side, dimension)


def shards(option_value, spot_nodes, var_nodes, rate_nodes):
    spot_rows, planes, var_cols = option_value.shape
    line_count = planes * var_cols
    spot_place = lax.axis_index("spot")
    var_place = lax.axis_index("var")
    spot_coords = coordinates(spot_nodes, spot_low, spot_high)
    var_coords = coordinates(var_nodes, var_low, var_high)
    rate_coords = coordinates(rate_nodes, rate_low, rate_high)
    spot_geo = geometry(spot_coords, 0, 3, spot_place * spot_rows, spot_rows)
    var_geo = geometry(var_coords, 2, 3, var_place * var_cols, var_cols)
    rate_geo = geometry(rate_coords, 1, 3, 0, planes)
    spot_whole = geometry(spot_coords, 0, 2, 0, spot_nodes.shape[0])
    var_whole = geometry(var_coords, 1, 2, 0, var_nodes.shape[0])
    rate_plain = rate_geo[0].reshape(planes)
    var_plain = var_geo[0].reshape(var_cols)

    def spot_pad(array):
        devices, rows = lax.axis_size("spot"), array.shape[0]
        up = [(i, i + 1) for i in range(devices - 1)]
        down = [(j, i) for i, j in up]
        before = lax.ppermute(array[rows - 1 : rows], "spot", up)
        after = lax.ppermute(array[0:1], "spot", down)
        return jnp.concatenate([before, array, after], axis=0)

    def edge_terms(values, mixing_only):
        devices, cols = lax.axis_size("var"), values.shape[2]
        up = [(i, i + 1) for i in range(devices - 1)]
        down = [(j, i) for i, j in up]
        left = lax.ppermute(values[:, :, cols - 1 : cols], "var", up)
        right = lax.ppermute(values[:, :, 0:1], "var", down)
        rows = spot_pad(values)
        sides = spot_pad(jnp.concatenate([left, right], axis=2))
        padded = jnp.concatenate([sides[:, :, 0:1], rows, sides[:, :, 1:2]], axis=2)
        padded = jnp.pad(padded, ((0, 0), (1, 1), (0, 0)))
        return explicit_terms(padded, spot_geo, var_geo, rate_geo, mixing_only)

    def spot_solve(values):
        gathered = lax.all_to_all(
            values.reshape(spot_rows, line_count), "spot", split_axis=1, concat_axis=0, tiled=True
        )
        per_device = gathered.shape[1]
        first_line = spot_place * per_device
        rate_flat = jnp.broadcast_to(rate_plain.reshape(planes, 1), (planes, var_cols)).reshape(
            line_count
        )
        var_flat = jnp.broadcast_to(var_plain.reshape(1, var_cols), (planes, var_cols)).reshape(
            line_count
        )
        rate_line = lax.dynamic_slice_in_dim(rate_flat, first_line, per_device).reshape(
            1, per_device
        )
        var_line = lax.dynamic_slice_in_dim(var_flat, first_line, per_device).reshape(1, per_device)
        diffusion, advection = spot_terms(spot_whole[0], var_line, rate_line)
        system = line_coefficients(
            diffusion, advection, rate_line / 3.0, spot_whole[1], spot_whole[2]
        )
        solved = implicit(system, gathered, 0)
        return lax.all_to_all(solved, "spot", split_axis=0, concat_axis=1, tiled=True).reshape(
            spot_rows, planes, var_cols
        )

    var_count = var_nodes.shape[0]
    blocks = var_count // var_cols
    var_vec = var_coords[1:-1]
    var_first, var_second = stencil_weights(var_coords)
    var_diffusion, var_advection = var_terms(var_vec)
    var_behind = var_diffusion * var_second[0] + var_advection * var_first[0]
    var_middle = var_diffusion * var_second[1] + var_advection * var_first[1]
    var_ahead = var_diffusion * var_second[2] + var_advection * var_first[2]
    reaction_plain = rate_plain / 3.0
    var_lower = (-solve_scale * var_behind).reshape(blocks, var_cols)
    var_upper = (-solve_scale * var_ahead).reshape(blocks, var_cols)
    var_main = (
        1.0 - solve_scale * (var_middle.reshape(var_count, 1) - reaction_plain.reshape(1, planes))
    ).reshape(blocks, var_cols, planes)

    lower_own = lax.dynamic_index_in_dim(var_lower, var_place, 0, keepdims=False)
    upper_own = lax.dynamic_index_in_dim(var_upper, var_place, 0, keepdims=False)
    main_own = lax.dynamic_index_in_dim(var_main, var_place, 0, keepdims=False)
    column_shape = (var_cols, 2, planes)
    position = lax.broadcasted_iota(jnp.int32, column_shape, 0)
    kind = lax.broadcasted_iota(jnp.int32, column_shape, 1)
    coupling = jnp.where(
        (kind == 0) & (position == 0),
        lower_own[0],
        jnp.where((kind == 1) & (position == var_cols - 1), upper_own[var_cols - 1], 0.0),
    )
    flat = (var_cols, 2 * planes)
    columns = line_solve(
        jnp.broadcast_to(lower_own.reshape(var_cols, 1), flat),
        jnp.broadcast_to(main_own.reshape(var_cols, 1, planes), column_shape).reshape(flat),
        jnp.broadcast_to(upper_own.reshape(var_cols, 1), flat),
        coupling.reshape(flat),
    ).reshape(column_shape)
    g_own, h_own = columns[:, 0, :], columns[:, 1, :]
    column_ends = jnp.stack([g_own[0], g_own[var_cols - 1], h_own[0], h_own[var_cols - 1]])
    def interface_solve(y_first, y_last, g_first, g_last, h_first, h_last):
        size = 2 * (blocks - 1)
        matrix = [[None] * size for _ in range(size)]
        rhs = [None] * size
        for b in range(blocks - 1):
            matrix[2 * b][2 * b] = 1.0
            if b >= 1:
                matrix[2 * b][2 * b - 2] = g_last[b]
            matrix[2 * b][2 * b + 1] = h_last[b]
            rhs[2 * b] = y_last[b]
            matrix[2 * b + 1][2 * b + 1] = 1.0
            matrix[2 * b + 1][2 * b] = g_first[b + 1]
            if b + 2 <= blocks - 1:
                matrix[2 * b + 1][2 * b + 3] = h_first[b + 1]
            rhs[2 * b + 1] = y_first[b + 1]
        for k in range(size):
            for i in range(k + 1, size):
                if matrix[i][k] is None:
                    continue
                factor = matrix[i][k] / matrix[k][k]
                for c in range(k + 1, size):
                    if matrix[k][c] is None:
                        continue
                    update = factor * matrix[k][c]
                    matrix[i][c] = -update if matrix[i][c] is None else matrix[i][c] - update
                rhs[i] = rhs[i] - factor * rhs[k]
                matrix[i][k] = None
        solved = [None] * size
        for k in reversed(range(size)):
            total = rhs[k]
            for c in range(k + 1, size):
                if matrix[k][c] is not None:
                    total = total - matrix[k][c] * solved[c]
            solved[k] = total / matrix[k][k]
        zero = jnp.zeros_like(y_first[0])
        left = jnp.stack([zero] + [solved[2 * b] for b in range(blocks - 1)])
        right = jnp.stack([solved[2 * b + 1] for b in range(blocks - 1)] + [zero])
        return (
            lax.dynamic_index_in_dim(left, var_place, 0, keepdims=False),
            lax.dynamic_index_in_dim(right, var_place, 0, keepdims=False),
        )

    def gather_ends(ends):
        stacked = gather_var(ends, blocks)
        order = (var_place - jnp.arange(blocks)) % blocks
        return jnp.take(stacked, order, axis=0)

    def var_solve(values):
        line_count = spot_rows * planes
        lines = values.transpose(2, 0, 1).reshape(var_cols, line_count)
        shape = lines.shape
        local = line_solve(
            jnp.broadcast_to(lower_own.reshape(var_cols, 1), shape),
            jnp.broadcast_to(main_own.reshape(var_cols, 1, planes), (var_cols, spot_rows, planes)).reshape(shape),
            jnp.broadcast_to(upper_own.reshape(var_cols, 1), shape),
            lines,
        ).reshape(var_cols, spot_rows, planes)
        message = jnp.concatenate(
            [local[0], local[var_cols - 1], column_ends], axis=0
        )
        ends = gather_ends(message)
        left, right = interface_solve(
            ends[:, :spot_rows],
            ends[:, spot_rows : 2 * spot_rows],
            ends[:, 2 * spot_rows],
            ends[:, 2 * spot_rows + 1],
            ends[:, 2 * spot_rows + 2],
            ends[:, 2 * spot_rows + 3],
        )
        solved = (
            local
            - left.reshape(1, spot_rows, planes) * g_own.reshape(var_cols, 1, planes)
            - right.reshape(1, spot_rows, planes) * h_own.reshape(var_cols, 1, planes)
        )
        return solved.transpose(1, 2, 0), left, right

    def rate_solve(values):
        diffusion, advection = rate_terms(rate_geo[0])
        system = line_coefficients(
            diffusion, advection, rate_geo[0] / 3.0, rate_geo[1], rate_geo[2]
        )
        return implicit(system, values, 1)

    z_zero = time_step * edge_terms(option_value, False)
    z_one = spot_solve(z_zero)
    z_two, edge_left, edge_right = var_solve(z_one)
    z_two_wide = jnp.concatenate(
        [edge_left.reshape(spot_rows, planes, 1), z_two, edge_right.reshape(spot_rows, planes, 1)],
        axis=2,
    )
    z_three_wide = rate_solve(z_two_wide)
    padded = jnp.pad(spot_pad(z_three_wide), ((0, 0), (1, 1), (0, 0)))
    w_zero = z_zero + half_step * explicit_terms(padded, spot_geo, var_geo, rate_geo, True)
    w_one = spot_solve(w_zero)
    w_two, _, _ = var_solve(w_one)
    w_three = rate_solve(w_two)
    return option_value + w_three


def solution(mesh):
    in_specs = (P("spot", None, "var"), P(), P(), P())
    out_specs = P("spot", None, "var")
    return jax.shard_map(shards, mesh=mesh, in_specs=in_specs, out_specs=out_specs, check_vma=False)
```

```python
import functools

import jax
import jax.numpy as jnp
from jax import lax
from jax.experimental import pallas as pl
from jax.experimental.pallas import tpu as pltpu
from jax.sharding import PartitionSpec as P

time_step = 0.01
solve_scale = 0.5 * time_step
half_step = 0.5 * time_step
spot_low = 0.5
spot_high = 2.5
var_low = 0.02
var_high = 1.0
rate_low = -0.1
rate_high = 0.2
dividend_yield = 0.02
reversion_var = 2.0
long_var = 0.04
vol_var = 0.6
reversion_rate = 0.1
long_rate = 0.05
vol_rate = 0.1
coupling_sv = -0.7 * vol_var
coupling_sr = 0.2 * vol_rate
coupling_vr = 0.1 * vol_var * vol_rate


def padded_2(array, sides, width):
    for axis, dim in sides:
        devices, length = (lax.axis_size(axis), array.shape[dim])
        up = [(i, (i + 1) % devices) for i in range(devices - 1)]
        down = [(j, i) for i, j in up]
        last = lax.slice_in_dim(array, length - width, length, axis=dim)
        initial = lax.slice_in_dim(array, 0, width, axis=dim)
        before = lax.ppermute(last, axis, up)
        after = lax.ppermute(initial, axis, down)
        array = jnp.concatenate([before, array, after], axis=dim)
    return array


def coordinates(node_list, low_end, high_end):
    length = node_list.shape[0]
    extended = jnp.concatenate(
        [jnp.full((1,), -1, jnp.int32), node_list, jnp.full((1,), 4 * length, jnp.int32)]
    )
    return low_end + (high_end - low_end) * extended.astype(jnp.float32) / (4 * length - 1)


def stencil_weights(coords):
    behind = coords[1:-1] - coords[:-2]
    ahead = coords[2:] - coords[1:-1]
    spread = behind + ahead
    first_diff = (
        -ahead / (behind * spread),
        (ahead - behind) / (behind * ahead),
        behind / (ahead * spread),
    )
    second_diff = (2.0 / (behind * spread), -2.0 / (behind * ahead), 2.0 / (ahead * spread))
    return (first_diff, second_diff)


def geometry(coords, position, dim_count, offset, length):
    first_diff, second_diff = stencil_weights(coords)
    vectors = (coords[1:-1],) + first_diff + second_diff
    target = [1] * dim_count
    target[position] = length
    pieces = [
        lax.dynamic_slice_in_dim(vector, offset, length).reshape(target) for vector in vectors
    ]
    return (pieces[0], tuple(pieces[1:4]), tuple(pieces[4:7]))


def spot_terms(spot_x, var_x, rate_x):
    return (0.5 * spot_x * spot_x * var_x, (rate_x - dividend_yield) * spot_x)


def var_terms(var_x):
    return (0.5 * vol_var * vol_var * var_x, reversion_var * (long_var - var_x))


def rate_terms(rate_x):
    return (0.5 * vol_rate * vol_rate, reversion_rate * (long_rate - rate_x))


def line_coefficients(diffusion, advection, reaction, first_diff, second_diff):
    behind = diffusion * second_diff[0] + advection * first_diff[0]
    centre = diffusion * second_diff[1] + advection * first_diff[1] - reaction
    ahead = diffusion * second_diff[2] + advection * first_diff[2]
    return (behind, centre, ahead)


def explicit_terms(padded, spot_geo, var_geo, rate_geo, mixing_only):
    spot_x, spot_first, spot_second = spot_geo
    var_x, var_first, var_second = var_geo
    rate_x, rate_first, rate_second = rate_geo
    spot_rows = padded.shape[0] - 2
    planes = padded.shape[1] - 2
    var_cols = padded.shape[2] - 2
    middle = padded[1:-1, 1:-1, 1:-1]
    cross_sv = 0.0
    cross_sr = 0.0
    cross_vr = 0.0
    for outer_step in range(3):
        for inner_step in range(3):
            cross_sv = (
                cross_sv
                + spot_first[outer_step]
                * var_first[inner_step]
                * padded[
                    outer_step : outer_step + spot_rows, 1:-1, inner_step : inner_step + var_cols
                ]
            )
            cross_sr = (
                cross_sr
                + spot_first[outer_step]
                * rate_first[inner_step]
                * padded[
                    outer_step : outer_step + spot_rows, inner_step : inner_step + planes, 1:-1
                ]
            )
            cross_vr = (
                cross_vr
                + var_first[outer_step]
                * rate_first[inner_step]
                * padded[1:-1, inner_step : inner_step + planes, outer_step : outer_step + var_cols]
            )
    root_var = jnp.sqrt(var_x)
    mixing = (
        coupling_sv * spot_x * var_x * cross_sv
        + coupling_sr * spot_x * root_var * cross_sr
        + coupling_vr * root_var * cross_vr
    )
    if mixing_only:
        return mixing
    reaction = rate_x / 3.0
    diffusion, advection = spot_terms(spot_x, var_x, rate_x)
    behind, centre, ahead = line_coefficients(
        diffusion, advection, reaction, spot_first, spot_second
    )
    along_spot = behind * padded[:-2, 1:-1, 1:-1] + centre * middle + ahead * padded[2:, 1:-1, 1:-1]
    diffusion, advection = var_terms(var_x)
    behind, centre, ahead = line_coefficients(diffusion, advection, reaction, var_first, var_second)
    along_var = behind * padded[1:-1, 1:-1, :-2] + centre * middle + ahead * padded[1:-1, 1:-1, 2:]
    diffusion, advection = rate_terms(rate_x)
    behind, centre, ahead = line_coefficients(
        diffusion, advection, reaction, rate_first, rate_second
    )
    along_rate = behind * padded[1:-1, :-2, 1:-1] + centre * middle + ahead * padded[1:-1, 2:, 1:-1]
    return mixing + along_spot + along_var + along_rate


def reduce_solve(lower_band, main_band, upper_band, right_side, dimension):
    length = right_side.shape[dimension]
    if length == 1:
        return right_side / main_band

    def even_rows(source):
        return lax.slice_in_dim(source, 0, length, 2, dimension)

    def odd_rows(source):
        return lax.slice_in_dim(source, 1, length, 2, dimension)

    def onward(source, filler):
        remainder = lax.slice_in_dim(source, 1, source.shape[dimension], axis=dimension)
        return jnp.concatenate(
            [remainder, jnp.zeros_like(lax.slice_in_dim(source, 0, 1, axis=dimension)) + filler],
            axis=dimension,
        )

    lower_even, main_even, upper_even, right_even = [
        even_rows(source) for source in (lower_band, main_band, upper_band, right_side)
    ]
    lower_odd, main_odd, upper_odd, right_odd = [
        odd_rows(source) for source in (lower_band, main_band, upper_band, right_side)
    ]
    lower_next = onward(lower_even, 0.0)
    main_next = onward(main_even, 1.0)
    upper_next = onward(upper_even, 0.0)
    right_next = onward(right_even, 0.0)
    ratio_back = -lower_odd / main_even
    ratio_ahead = -upper_odd / main_next
    solved_odd = reduce_solve(
        ratio_back * lower_even,
        main_odd + ratio_back * upper_even + ratio_ahead * lower_next,
        ratio_ahead * upper_next,
        right_odd + ratio_back * right_even + ratio_ahead * right_next,
        dimension,
    )
    remainder = lax.slice_in_dim(solved_odd, 0, solved_odd.shape[dimension] - 1, axis=dimension)
    solved_even = (
        right_even
        - lower_even
        * jnp.concatenate(
            [jnp.zeros_like(lax.slice_in_dim(solved_odd, 0, 1, axis=dimension)), remainder],
            axis=dimension,
        )
        - upper_even * solved_odd
    ) / main_even
    joined = jnp.stack([solved_even, solved_odd], axis=dimension + 1)
    return joined.reshape(right_side.shape)


def cyclic_kernel(lower_ref, main_ref, upper_ref, rhs_ref, out_ref, a_s, b_s, c_s, d_s):
    count, width = rhs_ref.shape
    pad = count // 2
    for ref, fill in ((a_s, 0.0), (b_s, 1.0), (c_s, 0.0), (d_s, 0.0)):
        ref[0:pad, :] = jnp.full((pad, width), fill, jnp.float32)
        ref[pad + count : 2 * pad + count, :] = jnp.full((pad, width), fill, jnp.float32)
    row = lax.broadcasted_iota(jnp.int32, (count, width), 0)
    a_s[pad : pad + count, :] = jnp.where(row == 0, 0.0, lower_ref[...])
    b_s[pad : pad + count, :] = main_ref[...]
    c_s[pad : pad + count, :] = jnp.where(row == count - 1, 0.0, upper_ref[...])
    d_s[pad : pad + count, :] = rhs_ref[...]
    stride = 1
    while stride < count:
        centre = slice(pad, pad + count)
        before = slice(pad - stride, pad - stride + count)
        after = slice(pad + stride, pad + stride + count)
        a, b, c, d = a_s[centre, :], b_s[centre, :], c_s[centre, :], d_s[centre, :]
        ratio_back = -a / b_s[before, :]
        ratio_ahead = -c / b_s[after, :]
        new_b = b + ratio_back * c_s[before, :] + ratio_ahead * a_s[after, :]
        new_d = d + ratio_back * d_s[before, :] + ratio_ahead * d_s[after, :]
        new_a = ratio_back * a_s[before, :]
        new_c = ratio_ahead * c_s[after, :]
        a_s[centre, :] = new_a
        b_s[centre, :] = new_b
        c_s[centre, :] = new_c
        d_s[centre, :] = new_d
        stride *= 2
    out_ref[...] = d_s[pad : pad + count, :] / b_s[pad : pad + count, :]


def line_solve(lower_band, main_band, upper_band, right_side):
    count, width = right_side.shape
    scratch = pltpu.VMEM((2 * (count // 2) + count, width), jnp.float32)
    return pl.pallas_call(
        cyclic_kernel,
        out_shape=jax.ShapeDtypeStruct((count, width), jnp.float32),
        scratch_shapes=[scratch] * 4,
    )(lower_band, main_band, upper_band, right_side)


def gather_kernel(blocks, ends_ref, out_ref, landed, send_sem, recv_sem):
    me = lax.axis_index("var")
    spot = lax.axis_index("spot")
    barrier = pltpu.get_barrier_semaphore()
    for shift in range(1, blocks):
        peer = lax.rem(me + shift, blocks)
        pl.semaphore_signal(barrier, inc=1, device_id=(spot, peer), device_id_type=pl.DeviceIdType.MESH)
    pl.semaphore_wait(barrier, blocks - 1)
    copies = []
    for shift in range(1, blocks):
        peer = lax.rem(me + shift, blocks)
        copy = pltpu.make_async_remote_copy(
            src_ref=ends_ref,
            dst_ref=landed.at[shift - 1],
            send_sem=send_sem.at[shift - 1],
            recv_sem=recv_sem.at[shift - 1],
            device_id=(spot, peer),
            device_id_type=pl.DeviceIdType.MESH,
        )
        copy.start()
        copies.append(copy)
    out_ref[0] = ends_ref[...]
    for copy in copies:
        copy.wait()
    for shift in range(1, blocks):
        out_ref[shift] = landed[shift - 1]


def gather_var(ends, blocks):
    return pl.pallas_call(
        functools.partial(gather_kernel, blocks),
        out_shape=jax.ShapeDtypeStruct((blocks,) + ends.shape, jnp.float32),
        scratch_shapes=[
            pltpu.VMEM((blocks - 1,) + ends.shape, jnp.float32),
            pltpu.SemaphoreType.DMA((blocks - 1,)),
            pltpu.SemaphoreType.DMA((blocks - 1,)),
        ],
        compiler_params=pltpu.CompilerParams(collective_id=0, has_side_effects=True),
    )(ends)


def implicit(system, right_side, dimension):
    behind, centre, ahead = system
    lower_band = jnp.broadcast_to(-solve_scale * behind, right_side.shape)
    main_band = jnp.broadcast_to(1.0 - solve_scale * centre, right_side.shape)
    upper_band = jnp.broadcast_to(-solve_scale * ahead, right_side.shape)
    return reduce_solve(lower_band, main_band, upper_band, right_side, dimension)


def shards(option_value, spot_nodes, var_nodes, rate_nodes):
    spot_rows, planes, var_cols = option_value.shape
    line_count = planes * var_cols
    spot_place = lax.axis_index("spot")
    var_place = lax.axis_index("var")
    spot_coords = coordinates(spot_nodes, spot_low, spot_high)
    var_coords = coordinates(var_nodes, var_low, var_high)
    rate_coords = coordinates(rate_nodes, rate_low, rate_high)
    spot_geo = geometry(spot_coords, 0, 3, spot_place * spot_rows, spot_rows)
    var_geo = geometry(var_coords, 2, 3, var_place * var_cols, var_cols)
    rate_geo = geometry(rate_coords, 1, 3, 0, planes)
    spot_whole = geometry(spot_coords, 0, 2, 0, spot_nodes.shape[0])
    var_whole = geometry(var_coords, 1, 2, 0, var_nodes.shape[0])
    rate_plain = rate_geo[0].reshape(planes)
    var_plain = var_geo[0].reshape(var_cols)

    def edge_terms(values, mixing_only):
        padded = padded_2(values, (("var", 2), ("spot", 0)), 1)
        padded = jnp.pad(padded, ((0, 0), (1, 1), (0, 0)))
        return explicit_terms(padded, spot_geo, var_geo, rate_geo, mixing_only)

    def spot_solve(values):
        gathered = lax.all_to_all(
            values.reshape(spot_rows, line_count), "spot", split_axis=1, concat_axis=0, tiled=True
        )
        per_device = gathered.shape[1]
        first_line = spot_place * per_device
        rate_flat = jnp.broadcast_to(rate_plain.reshape(planes, 1), (planes, var_cols)).reshape(
            line_count
        )
        var_flat = jnp.broadcast_to(var_plain.reshape(1, var_cols), (planes, var_cols)).reshape(
            line_count
        )
        rate_line = lax.dynamic_slice_in_dim(rate_flat, first_line, per_device).reshape(
            1, per_device
        )
        var_line = lax.dynamic_slice_in_dim(var_flat, first_line, per_device).reshape(1, per_device)
        diffusion, advection = spot_terms(spot_whole[0], var_line, rate_line)
        system = line_coefficients(
            diffusion, advection, rate_line / 3.0, spot_whole[1], spot_whole[2]
        )
        solved = implicit(system, gathered, 0)
        return lax.all_to_all(solved, "spot", split_axis=0, concat_axis=1, tiled=True).reshape(
            spot_rows, planes, var_cols
        )

    var_count = var_nodes.shape[0]
    blocks = var_count // var_cols
    var_vec = var_coords[1:-1]
    var_first, var_second = stencil_weights(var_coords)
    var_diffusion, var_advection = var_terms(var_vec)
    var_behind = var_diffusion * var_second[0] + var_advection * var_first[0]
    var_middle = var_diffusion * var_second[1] + var_advection * var_first[1]
    var_ahead = var_diffusion * var_second[2] + var_advection * var_first[2]
    reaction_plain = rate_plain / 3.0
    var_lower = (-solve_scale * var_behind).reshape(blocks, var_cols)
    var_upper = (-solve_scale * var_ahead).reshape(blocks, var_cols)
    var_main = (
        1.0 - solve_scale * (var_middle.reshape(var_count, 1) - reaction_plain.reshape(1, planes))
    ).reshape(blocks, var_cols, planes)

    lower_own = lax.dynamic_index_in_dim(var_lower, var_place, 0, keepdims=False)
    upper_own = lax.dynamic_index_in_dim(var_upper, var_place, 0, keepdims=False)
    main_own = lax.dynamic_index_in_dim(var_main, var_place, 0, keepdims=False)
    column_shape = (var_cols, 2, planes)
    position = lax.broadcasted_iota(jnp.int32, column_shape, 0)
    kind = lax.broadcasted_iota(jnp.int32, column_shape, 1)
    coupling = jnp.where(
        (kind == 0) & (position == 0),
        lower_own[0],
        jnp.where((kind == 1) & (position == var_cols - 1), upper_own[var_cols - 1], 0.0),
    )
    flat = (var_cols, 2 * planes)
    columns = line_solve(
        jnp.broadcast_to(lower_own.reshape(var_cols, 1), flat),
        jnp.broadcast_to(main_own.reshape(var_cols, 1, planes), column_shape).reshape(flat),
        jnp.broadcast_to(upper_own.reshape(var_cols, 1), flat),
        coupling.reshape(flat),
    ).reshape(column_shape)
    g_own, h_own = columns[:, 0, :], columns[:, 1, :]
    column_ends = jnp.stack([g_own[0], g_own[var_cols - 1], h_own[0], h_own[var_cols - 1]])
    def interface_solve(y_first, y_last, g_first, g_last, h_first, h_last):
        size = 2 * (blocks - 1)
        matrix = [[None] * size for _ in range(size)]
        rhs = [None] * size
        for b in range(blocks - 1):
            matrix[2 * b][2 * b] = 1.0
            if b >= 1:
                matrix[2 * b][2 * b - 2] = g_last[b]
            matrix[2 * b][2 * b + 1] = h_last[b]
            rhs[2 * b] = y_last[b]
            matrix[2 * b + 1][2 * b + 1] = 1.0
            matrix[2 * b + 1][2 * b] = g_first[b + 1]
            if b + 2 <= blocks - 1:
                matrix[2 * b + 1][2 * b + 3] = h_first[b + 1]
            rhs[2 * b + 1] = y_first[b + 1]
        for k in range(size):
            for i in range(k + 1, size):
                if matrix[i][k] is None:
                    continue
                factor = matrix[i][k] / matrix[k][k]
                for c in range(k + 1, size):
                    if matrix[k][c] is None:
                        continue
                    update = factor * matrix[k][c]
                    matrix[i][c] = -update if matrix[i][c] is None else matrix[i][c] - update
                rhs[i] = rhs[i] - factor * rhs[k]
                matrix[i][k] = None
        solved = [None] * size
        for k in reversed(range(size)):
            total = rhs[k]
            for c in range(k + 1, size):
                if matrix[k][c] is not None:
                    total = total - matrix[k][c] * solved[c]
            solved[k] = total / matrix[k][k]
        zero = jnp.zeros_like(y_first[0])
        left = jnp.stack([zero] + [solved[2 * b] for b in range(blocks - 1)])
        right = jnp.stack([solved[2 * b + 1] for b in range(blocks - 1)] + [zero])
        return (
            lax.dynamic_index_in_dim(left, var_place, 0, keepdims=False),
            lax.dynamic_index_in_dim(right, var_place, 0, keepdims=False),
        )

    def gather_ends(ends):
        stacked = gather_var(ends, blocks)
        order = (var_place - jnp.arange(blocks)) % blocks
        return jnp.take(stacked, order, axis=0)

    def var_solve(values):
        line_count = spot_rows * planes
        lines = values.transpose(2, 0, 1).reshape(var_cols, line_count)
        shape = lines.shape
        local = line_solve(
            jnp.broadcast_to(lower_own.reshape(var_cols, 1), shape),
            jnp.broadcast_to(main_own.reshape(var_cols, 1, planes), (var_cols, spot_rows, planes)).reshape(shape),
            jnp.broadcast_to(upper_own.reshape(var_cols, 1), shape),
            lines,
        ).reshape(var_cols, spot_rows, planes)
        message = jnp.concatenate(
            [local[0], local[var_cols - 1], column_ends], axis=0
        )
        ends = gather_ends(message)
        left, right = interface_solve(
            ends[:, :spot_rows],
            ends[:, spot_rows : 2 * spot_rows],
            ends[:, 2 * spot_rows],
            ends[:, 2 * spot_rows + 1],
            ends[:, 2 * spot_rows + 2],
            ends[:, 2 * spot_rows + 3],
        )
        solved = (
            local
            - left.reshape(1, spot_rows, planes) * g_own.reshape(var_cols, 1, planes)
            - right.reshape(1, spot_rows, planes) * h_own.reshape(var_cols, 1, planes)
        )
        return solved.transpose(1, 2, 0), left, right

    def rate_solve(values):
        diffusion, advection = rate_terms(rate_geo[0])
        system = line_coefficients(
            diffusion, advection, rate_geo[0] / 3.0, rate_geo[1], rate_geo[2]
        )
        return implicit(system, values, 1)

    def spot_pad(array):
        devices, rows = lax.axis_size("spot"), array.shape[0]
        up = [(i, i + 1) for i in range(devices - 1)]
        down = [(j, i) for i, j in up]
        before = lax.ppermute(array[rows - 1 : rows], "spot", up)
        after = lax.ppermute(array[0:1], "spot", down)
        return jnp.concatenate([before, array, after], axis=0)

    z_zero = time_step * edge_terms(option_value, False)
    z_one = spot_solve(z_zero)
    z_two, edge_left, edge_right = var_solve(z_one)
    z_two_wide = jnp.concatenate(
        [edge_left.reshape(spot_rows, planes, 1), z_two, edge_right.reshape(spot_rows, planes, 1)],
        axis=2,
    )
    z_three_wide = rate_solve(z_two_wide)
    padded = jnp.pad(spot_pad(z_three_wide), ((0, 0), (1, 1), (0, 0)))
    w_zero = z_zero + half_step * explicit_terms(padded, spot_geo, var_geo, rate_geo, True)
    w_one = spot_solve(w_zero)
    w_two, _, _ = var_solve(w_one)
    w_three = rate_solve(w_two)
    return option_value + w_three


def solution(mesh):
    in_specs = (P("spot", None, "var"), P(), P(), P())
    out_specs = P("spot", None, "var")
    return jax.shard_map(shards, mesh=mesh, in_specs=in_specs, out_specs=out_specs, check_vma=False)
```

```python
import functools

import jax
import jax.numpy as jnp
from jax import lax
from jax.experimental import pallas as pl
from jax.experimental.pallas import tpu as pltpu
from jax.sharding import PartitionSpec as P

time_step = 0.01
solve_scale = 0.5 * time_step
half_step = 0.5 * time_step
spot_low = 0.5
spot_high = 2.5
var_low = 0.02
var_high = 1.0
rate_low = -0.1
rate_high = 0.2
dividend_yield = 0.02
reversion_var = 2.0
long_var = 0.04
vol_var = 0.6
reversion_rate = 0.1
long_rate = 0.05
vol_rate = 0.1
coupling_sv = -0.7 * vol_var
coupling_sr = 0.2 * vol_rate
coupling_vr = 0.1 * vol_var * vol_rate


def padded_2(array, sides, width):
    for axis, dim in sides:
        devices, length = (lax.axis_size(axis), array.shape[dim])
        up = [(i, (i + 1) % devices) for i in range(devices - 1)]
        down = [(j, i) for i, j in up]
        last = lax.slice_in_dim(array, length - width, length, axis=dim)
        initial = lax.slice_in_dim(array, 0, width, axis=dim)
        before = lax.ppermute(last, axis, up)
        after = lax.ppermute(initial, axis, down)
        array = jnp.concatenate([before, array, after], axis=dim)
    return array


def coordinates(node_list, low_end, high_end):
    length = node_list.shape[0]
    extended = jnp.concatenate(
        [jnp.full((1,), -1, jnp.int32), node_list, jnp.full((1,), 4 * length, jnp.int32)]
    )
    return low_end + (high_end - low_end) * extended.astype(jnp.float32) / (4 * length - 1)


def stencil_weights(coords):
    behind = coords[1:-1] - coords[:-2]
    ahead = coords[2:] - coords[1:-1]
    spread = behind + ahead
    first_diff = (
        -ahead / (behind * spread),
        (ahead - behind) / (behind * ahead),
        behind / (ahead * spread),
    )
    second_diff = (2.0 / (behind * spread), -2.0 / (behind * ahead), 2.0 / (ahead * spread))
    return (first_diff, second_diff)


def geometry(coords, position, dim_count, offset, length):
    first_diff, second_diff = stencil_weights(coords)
    vectors = (coords[1:-1],) + first_diff + second_diff
    target = [1] * dim_count
    target[position] = length
    pieces = [
        lax.dynamic_slice_in_dim(vector, offset, length).reshape(target) for vector in vectors
    ]
    return (pieces[0], tuple(pieces[1:4]), tuple(pieces[4:7]))


def spot_terms(spot_x, var_x, rate_x):
    return (0.5 * spot_x * spot_x * var_x, (rate_x - dividend_yield) * spot_x)


def var_terms(var_x):
    return (0.5 * vol_var * vol_var * var_x, reversion_var * (long_var - var_x))


def rate_terms(rate_x):
    return (0.5 * vol_rate * vol_rate, reversion_rate * (long_rate - rate_x))


def line_coefficients(diffusion, advection, reaction, first_diff, second_diff):
    behind = diffusion * second_diff[0] + advection * first_diff[0]
    centre = diffusion * second_diff[1] + advection * first_diff[1] - reaction
    ahead = diffusion * second_diff[2] + advection * first_diff[2]
    return (behind, centre, ahead)


def explicit_terms(padded, spot_geo, var_geo, rate_geo, mixing_only):
    spot_x, spot_first, spot_second = spot_geo
    var_x, var_first, var_second = var_geo
    rate_x, rate_first, rate_second = rate_geo
    spot_rows = padded.shape[0] - 2
    planes = padded.shape[1] - 2
    var_cols = padded.shape[2] - 2
    middle = padded[1:-1, 1:-1, 1:-1]
    cross_sv = 0.0
    cross_sr = 0.0
    cross_vr = 0.0
    for outer_step in range(3):
        for inner_step in range(3):
            cross_sv = (
                cross_sv
                + spot_first[outer_step]
                * var_first[inner_step]
                * padded[
                    outer_step : outer_step + spot_rows, 1:-1, inner_step : inner_step + var_cols
                ]
            )
            cross_sr = (
                cross_sr
                + spot_first[outer_step]
                * rate_first[inner_step]
                * padded[
                    outer_step : outer_step + spot_rows, inner_step : inner_step + planes, 1:-1
                ]
            )
            cross_vr = (
                cross_vr
                + var_first[outer_step]
                * rate_first[inner_step]
                * padded[1:-1, inner_step : inner_step + planes, outer_step : outer_step + var_cols]
            )
    root_var = jnp.sqrt(var_x)
    mixing = (
        coupling_sv * spot_x * var_x * cross_sv
        + coupling_sr * spot_x * root_var * cross_sr
        + coupling_vr * root_var * cross_vr
    )
    if mixing_only:
        return mixing
    reaction = rate_x / 3.0
    diffusion, advection = spot_terms(spot_x, var_x, rate_x)
    behind, centre, ahead = line_coefficients(
        diffusion, advection, reaction, spot_first, spot_second
    )
    along_spot = behind * padded[:-2, 1:-1, 1:-1] + centre * middle + ahead * padded[2:, 1:-1, 1:-1]
    diffusion, advection = var_terms(var_x)
    behind, centre, ahead = line_coefficients(diffusion, advection, reaction, var_first, var_second)
    along_var = behind * padded[1:-1, 1:-1, :-2] + centre * middle + ahead * padded[1:-1, 1:-1, 2:]
    diffusion, advection = rate_terms(rate_x)
    behind, centre, ahead = line_coefficients(
        diffusion, advection, reaction, rate_first, rate_second
    )
    along_rate = behind * padded[1:-1, :-2, 1:-1] + centre * middle + ahead * padded[1:-1, 2:, 1:-1]
    return mixing + along_spot + along_var + along_rate


def reduce_solve(lower_band, main_band, upper_band, right_side, dimension):
    length = right_side.shape[dimension]
    if length == 1:
        return right_side / main_band

    def even_rows(source):
        return lax.slice_in_dim(source, 0, length, 2, dimension)

    def odd_rows(source):
        return lax.slice_in_dim(source, 1, length, 2, dimension)

    def onward(source, filler):
        remainder = lax.slice_in_dim(source, 1, source.shape[dimension], axis=dimension)
        return jnp.concatenate(
            [remainder, jnp.zeros_like(lax.slice_in_dim(source, 0, 1, axis=dimension)) + filler],
            axis=dimension,
        )

    lower_even, main_even, upper_even, right_even = [
        even_rows(source) for source in (lower_band, main_band, upper_band, right_side)
    ]
    lower_odd, main_odd, upper_odd, right_odd = [
        odd_rows(source) for source in (lower_band, main_band, upper_band, right_side)
    ]
    lower_next = onward(lower_even, 0.0)
    main_next = onward(main_even, 1.0)
    upper_next = onward(upper_even, 0.0)
    right_next = onward(right_even, 0.0)
    ratio_back = -lower_odd / main_even
    ratio_ahead = -upper_odd / main_next
    solved_odd = reduce_solve(
        ratio_back * lower_even,
        main_odd + ratio_back * upper_even + ratio_ahead * lower_next,
        ratio_ahead * upper_next,
        right_odd + ratio_back * right_even + ratio_ahead * right_next,
        dimension,
    )
    remainder = lax.slice_in_dim(solved_odd, 0, solved_odd.shape[dimension] - 1, axis=dimension)
    solved_even = (
        right_even
        - lower_even
        * jnp.concatenate(
            [jnp.zeros_like(lax.slice_in_dim(solved_odd, 0, 1, axis=dimension)), remainder],
            axis=dimension,
        )
        - upper_even * solved_odd
    ) / main_even
    joined = jnp.stack([solved_even, solved_odd], axis=dimension + 1)
    return joined.reshape(right_side.shape)


def cyclic_kernel(lower_ref, main_ref, upper_ref, rhs_ref, out_ref, a_s, b_s, c_s, d_s):
    count, width = rhs_ref.shape
    pad = count // 2
    for ref, fill in ((a_s, 0.0), (b_s, 1.0), (c_s, 0.0), (d_s, 0.0)):
        ref[0:pad, :] = jnp.full((pad, width), fill, jnp.float32)
        ref[pad + count : 2 * pad + count, :] = jnp.full((pad, width), fill, jnp.float32)
    row = lax.broadcasted_iota(jnp.int32, (count, width), 0)
    a_s[pad : pad + count, :] = jnp.where(row == 0, 0.0, lower_ref[...])
    b_s[pad : pad + count, :] = main_ref[...]
    c_s[pad : pad + count, :] = jnp.where(row == count - 1, 0.0, upper_ref[...])
    d_s[pad : pad + count, :] = rhs_ref[...]
    stride = 1
    while stride < count:
        centre = slice(pad, pad + count)
        before = slice(pad - stride, pad - stride + count)
        after = slice(pad + stride, pad + stride + count)
        a, b, c, d = a_s[centre, :], b_s[centre, :], c_s[centre, :], d_s[centre, :]
        ratio_back = -a / b_s[before, :]
        ratio_ahead = -c / b_s[after, :]
        new_b = b + ratio_back * c_s[before, :] + ratio_ahead * a_s[after, :]
        new_d = d + ratio_back * d_s[before, :] + ratio_ahead * d_s[after, :]
        new_a = ratio_back * a_s[before, :]
        new_c = ratio_ahead * c_s[after, :]
        a_s[centre, :] = new_a
        b_s[centre, :] = new_b
        c_s[centre, :] = new_c
        d_s[centre, :] = new_d
        stride *= 2
    out_ref[...] = d_s[pad : pad + count, :] / b_s[pad : pad + count, :]


def line_solve(lower_band, main_band, upper_band, right_side):
    count, width = right_side.shape
    scratch = pltpu.VMEM((2 * (count // 2) + count, width), jnp.float32)
    return pl.pallas_call(
        cyclic_kernel,
        out_shape=jax.ShapeDtypeStruct((count, width), jnp.float32),
        scratch_shapes=[scratch] * 4,
    )(lower_band, main_band, upper_band, right_side)


def gather_kernel(blocks, ends_ref, out_ref, landed, send_sem, recv_sem):
    me = lax.axis_index("var")
    spot = lax.axis_index("spot")
    barrier = pltpu.get_barrier_semaphore()
    for shift in range(1, blocks):
        peer = lax.rem(me + shift, blocks)
        pl.semaphore_signal(barrier, inc=1, device_id=(spot, peer), device_id_type=pl.DeviceIdType.MESH)
    pl.semaphore_wait(barrier, blocks - 1)
    copies = []
    for shift in range(1, blocks):
        peer = lax.rem(me + shift, blocks)
        copy = pltpu.make_async_remote_copy(
            src_ref=ends_ref,
            dst_ref=landed.at[shift - 1],
            send_sem=send_sem.at[shift - 1],
            recv_sem=recv_sem.at[shift - 1],
            device_id=(spot, peer),
            device_id_type=pl.DeviceIdType.MESH,
        )
        copy.start()
        copies.append(copy)
    out_ref[0] = ends_ref[...]
    for copy in copies:
        copy.wait()
    for shift in range(1, blocks):
        out_ref[shift] = landed[shift - 1]


def gather_var(ends, blocks):
    return pl.pallas_call(
        functools.partial(gather_kernel, blocks),
        out_shape=jax.ShapeDtypeStruct((blocks,) + ends.shape, jnp.float32),
        scratch_shapes=[
            pltpu.VMEM((blocks - 1,) + ends.shape, jnp.float32),
            pltpu.SemaphoreType.DMA((blocks - 1,)),
            pltpu.SemaphoreType.DMA((blocks - 1,)),
        ],
        compiler_params=pltpu.CompilerParams(collective_id=0, has_side_effects=True),
    )(ends)


def implicit(system, right_side, dimension):
    behind, centre, ahead = system
    lower_band = jnp.broadcast_to(-solve_scale * behind, right_side.shape)
    main_band = jnp.broadcast_to(1.0 - solve_scale * centre, right_side.shape)
    upper_band = jnp.broadcast_to(-solve_scale * ahead, right_side.shape)
    return reduce_solve(lower_band, main_band, upper_band, right_side, dimension)


def shards(option_value, spot_nodes, var_nodes, rate_nodes):
    spot_rows, planes, var_cols = option_value.shape
    line_count = planes * var_cols
    spot_place = lax.axis_index("spot")
    var_place = lax.axis_index("var")
    spot_coords = coordinates(spot_nodes, spot_low, spot_high)
    var_coords = coordinates(var_nodes, var_low, var_high)
    rate_coords = coordinates(rate_nodes, rate_low, rate_high)
    spot_geo = geometry(spot_coords, 0, 3, spot_place * spot_rows, spot_rows)
    var_geo = geometry(var_coords, 2, 3, var_place * var_cols, var_cols)
    rate_geo = geometry(rate_coords, 1, 3, 0, planes)
    spot_whole = geometry(spot_coords, 0, 2, 0, spot_nodes.shape[0])
    var_whole = geometry(var_coords, 1, 2, 0, var_nodes.shape[0])
    rate_plain = rate_geo[0].reshape(planes)
    var_plain = var_geo[0].reshape(var_cols)

    def edge_terms(values, mixing_only):
        padded = padded_2(values, (("var", 2), ("spot", 0)), 1)
        padded = jnp.pad(padded, ((0, 0), (1, 1), (0, 0)))
        return explicit_terms(padded, spot_geo, var_geo, rate_geo, mixing_only)

    def spot_solve(values):
        gathered = lax.all_to_all(
            values.reshape(spot_rows, line_count), "spot", split_axis=1, concat_axis=0, tiled=True
        )
        per_device = gathered.shape[1]
        first_line = spot_place * per_device
        rate_flat = jnp.broadcast_to(rate_plain.reshape(planes, 1), (planes, var_cols)).reshape(
            line_count
        )
        var_flat = jnp.broadcast_to(var_plain.reshape(1, var_cols), (planes, var_cols)).reshape(
            line_count
        )
        rate_line = lax.dynamic_slice_in_dim(rate_flat, first_line, per_device).reshape(
            1, per_device
        )
        var_line = lax.dynamic_slice_in_dim(var_flat, first_line, per_device).reshape(1, per_device)
        diffusion, advection = spot_terms(spot_whole[0], var_line, rate_line)
        system = line_coefficients(
            diffusion, advection, rate_line / 3.0, spot_whole[1], spot_whole[2]
        )
        behind, centre, ahead = system
        shape = gathered.shape
        solved = line_solve(
            jnp.broadcast_to(-solve_scale * behind, shape),
            jnp.broadcast_to(1.0 - solve_scale * centre, shape),
            jnp.broadcast_to(-solve_scale * ahead, shape),
            gathered,
        )
        return lax.all_to_all(solved, "spot", split_axis=0, concat_axis=1, tiled=True).reshape(
            spot_rows, planes, var_cols
        )

    var_count = var_nodes.shape[0]
    blocks = var_count // var_cols
    var_vec = var_coords[1:-1]
    var_first, var_second = stencil_weights(var_coords)
    var_diffusion, var_advection = var_terms(var_vec)
    var_behind = var_diffusion * var_second[0] + var_advection * var_first[0]
    var_middle = var_diffusion * var_second[1] + var_advection * var_first[1]
    var_ahead = var_diffusion * var_second[2] + var_advection * var_first[2]
    reaction_plain = rate_plain / 3.0
    var_lower = (-solve_scale * var_behind).reshape(blocks, var_cols)
    var_upper = (-solve_scale * var_ahead).reshape(blocks, var_cols)
    var_main = (
        1.0 - solve_scale * (var_middle.reshape(var_count, 1) - reaction_plain.reshape(1, planes))
    ).reshape(blocks, var_cols, planes)

    lower_own = lax.dynamic_index_in_dim(var_lower, var_place, 0, keepdims=False)
    upper_own = lax.dynamic_index_in_dim(var_upper, var_place, 0, keepdims=False)
    main_own = lax.dynamic_index_in_dim(var_main, var_place, 0, keepdims=False)
    column_shape = (var_cols, 2, planes)
    position = lax.broadcasted_iota(jnp.int32, column_shape, 0)
    kind = lax.broadcasted_iota(jnp.int32, column_shape, 1)
    coupling = jnp.where(
        (kind == 0) & (position == 0),
        lower_own[0],
        jnp.where((kind == 1) & (position == var_cols - 1), upper_own[var_cols - 1], 0.0),
    )
    flat = (var_cols, 2 * planes)
    columns = line_solve(
        jnp.broadcast_to(lower_own.reshape(var_cols, 1), flat),
        jnp.broadcast_to(main_own.reshape(var_cols, 1, planes), column_shape).reshape(flat),
        jnp.broadcast_to(upper_own.reshape(var_cols, 1), flat),
        coupling.reshape(flat),
    ).reshape(column_shape)
    g_own, h_own = columns[:, 0, :], columns[:, 1, :]
    column_ends = jnp.stack([g_own[0], g_own[var_cols - 1], h_own[0], h_own[var_cols - 1]])
    def interface_solve(y_first, y_last, g_first, g_last, h_first, h_last):
        size = 2 * (blocks - 1)
        matrix = [[None] * size for _ in range(size)]
        rhs = [None] * size
        for b in range(blocks - 1):
            matrix[2 * b][2 * b] = 1.0
            if b >= 1:
                matrix[2 * b][2 * b - 2] = g_last[b]
            matrix[2 * b][2 * b + 1] = h_last[b]
            rhs[2 * b] = y_last[b]
            matrix[2 * b + 1][2 * b + 1] = 1.0
            matrix[2 * b + 1][2 * b] = g_first[b + 1]
            if b + 2 <= blocks - 1:
                matrix[2 * b + 1][2 * b + 3] = h_first[b + 1]
            rhs[2 * b + 1] = y_first[b + 1]
        for k in range(size):
            for i in range(k + 1, size):
                if matrix[i][k] is None:
                    continue
                factor = matrix[i][k] / matrix[k][k]
                for c in range(k + 1, size):
                    if matrix[k][c] is None:
                        continue
                    update = factor * matrix[k][c]
                    matrix[i][c] = -update if matrix[i][c] is None else matrix[i][c] - update
                rhs[i] = rhs[i] - factor * rhs[k]
                matrix[i][k] = None
        solved = [None] * size
        for k in reversed(range(size)):
            total = rhs[k]
            for c in range(k + 1, size):
                if matrix[k][c] is not None:
                    total = total - matrix[k][c] * solved[c]
            solved[k] = total / matrix[k][k]
        zero = jnp.zeros_like(y_first[0])
        left = jnp.stack([zero] + [solved[2 * b] for b in range(blocks - 1)])
        right = jnp.stack([solved[2 * b + 1] for b in range(blocks - 1)] + [zero])
        return (
            lax.dynamic_index_in_dim(left, var_place, 0, keepdims=False),
            lax.dynamic_index_in_dim(right, var_place, 0, keepdims=False),
        )

    def gather_ends(ends):
        stacked = gather_var(ends, blocks)
        order = (var_place - jnp.arange(blocks)) % blocks
        return jnp.take(stacked, order, axis=0)

    def var_solve(values):
        line_count = spot_rows * planes
        lines = values.transpose(2, 0, 1).reshape(var_cols, line_count)
        shape = lines.shape
        local = line_solve(
            jnp.broadcast_to(lower_own.reshape(var_cols, 1), shape),
            jnp.broadcast_to(main_own.reshape(var_cols, 1, planes), (var_cols, spot_rows, planes)).reshape(shape),
            jnp.broadcast_to(upper_own.reshape(var_cols, 1), shape),
            lines,
        ).reshape(var_cols, spot_rows, planes)
        message = jnp.concatenate(
            [local[0], local[var_cols - 1], column_ends], axis=0
        )
        ends = gather_ends(message)
        left, right = interface_solve(
            ends[:, :spot_rows],
            ends[:, spot_rows : 2 * spot_rows],
            ends[:, 2 * spot_rows],
            ends[:, 2 * spot_rows + 1],
            ends[:, 2 * spot_rows + 2],
            ends[:, 2 * spot_rows + 3],
        )
        solved = (
            local
            - left.reshape(1, spot_rows, planes) * g_own.reshape(var_cols, 1, planes)
            - right.reshape(1, spot_rows, planes) * h_own.reshape(var_cols, 1, planes)
        )
        return solved.transpose(1, 2, 0), left, right

    def rate_solve(values):
        diffusion, advection = rate_terms(rate_geo[0])
        system = line_coefficients(
            diffusion, advection, rate_geo[0] / 3.0, rate_geo[1], rate_geo[2]
        )
        return implicit(system, values, 1)

    def spot_pad(array):
        devices, rows = lax.axis_size("spot"), array.shape[0]
        up = [(i, i + 1) for i in range(devices - 1)]
        down = [(j, i) for i, j in up]
        before = lax.ppermute(array[rows - 1 : rows], "spot", up)
        after = lax.ppermute(array[0:1], "spot", down)
        return jnp.concatenate([before, array, after], axis=0)

    z_zero = time_step * edge_terms(option_value, False)
    z_one = spot_solve(z_zero)
    z_two, edge_left, edge_right = var_solve(z_one)
    z_two_wide = jnp.concatenate(
        [edge_left.reshape(spot_rows, planes, 1), z_two, edge_right.reshape(spot_rows, planes, 1)],
        axis=2,
    )
    z_three_wide = rate_solve(z_two_wide)
    padded = jnp.pad(spot_pad(z_three_wide), ((0, 0), (1, 1), (0, 0)))
    w_zero = z_zero + half_step * explicit_terms(padded, spot_geo, var_geo, rate_geo, True)
    w_one = spot_solve(w_zero)
    w_two, _, _ = var_solve(w_one)
    w_three = rate_solve(w_two)
    return option_value + w_three


def solution(mesh):
    in_specs = (P("spot", None, "var"), P(), P(), P())
    out_specs = P("spot", None, "var")
    return jax.shard_map(shards, mesh=mesh, in_specs=in_specs, out_specs=out_specs, check_vma=False)
```
